32 devices in a mesh: dp: 4 (over y, core), mp: 8 (over z, x).
Axes of the slice: x: 2, y: 2, z: 4, core: 2. Of those that a mesh axis runs over, the one named last changes fastest.
Arguments:
- frames: bfloat16 [16384, 768], P(('dp', 'mp')), may hold values from -6 to 6
- seg_ids: int32 [32, 512], P('dp'), may hold values from 0 to 3, never falling along the last dimension, each value on 1 to 384 neighbouring positions
- text: bfloat16 [128, 77, 768], P(('dp', 'mp')), may hold values from -6 to 6
- text_lens: int32 [128], P('dp'), may hold values from 1 to 77, as said below
- step_ids: int32 [128], P('dp'), may hold values from 0 to 999
- step_table: bfloat16 [1000, 768], P(None, 'mp'), may hold values from -6 to 6
- ada_weight: bfloat16 [768, 4608], P('mp'), may hold values from -0.21875 to 0.21875
- ada_bias: bfloat16 [4608], replicated, may hold values from -3 to 3
- query_w: bfloat16 [768, 768], P(None, 'mp'), may hold values from -0.21875 to 0.21875
- key_w: bfloat16 [768, 768], P(None, 'mp'), may hold values from -0.21875 to 0.21875
- value_w: bfloat16 [768, 768], P(None, 'mp'), may hold values from -0.21875 to 0.21875
- out_w: bfloat16 [768, 768], P('mp'), may hold values from -1.25 to 1.25
- cross_query_w: bfloat16 [768, 768], P(None, 'mp'), may hold values from -0.21875 to 0.21875
- cross_key_w: bfloat16 [768, 768], P(None, 'mp'), may hold values from -0.21875 to 0.21875
- cross_value_w: bfloat16 [768, 768], P(None, 'mp'), may hold values from -0.21875 to 0.21875
- cross_out_w: bfloat16 [768, 768], P('mp'), may hold values from -1.25 to 1.25
- up_weight: bfloat16 [768, 3072], P(None, 'mp'), may hold values from -0.21875 to 0.21875
- down_weight: bfloat16 [3072, 768], P('mp'), may hold values from -0.21875 to 0.21875
- out_grad: bfloat16 [16384, 768], P(('dp', 'mp')), may hold values from -6 to 6
Outputs:
- layer_out: bfloat16 [16384, 768], P(('dp', 'mp'))
- grad_frames: float32 [16384, 768], P(('dp', 'mp'))
- grad_text: float32 [128, 77, 768], P(('dp', 'mp'))
- grad_step_table: float32 [1000, 768], P(None, 'mp')
- grad_ada_weight: float32 [768, 4608], P('mp')
- grad_ada_bias: float32 [4608], replicated
- grad_query_w: float32 [768, 768], P(None, 'mp')
- grad_key_w: float32 [768, 768], P(None, 'mp')
- grad_value_w: float32 [768, 768], P(None, 'mp')
- grad_out_w: float32 [768, 768], P('mp')
- grad_cross_query_w: float32 [768, 768], P(None, 'mp')
- grad_cross_key_w: float32 [768, 768], P(None, 'mp')
- grad_cross_value_w: float32 [768, 768], P(None, 'mp')
- grad_cross_out_w: float32 [768, 768], P('mp')
- grad_up_weight: float32 [768, 3072], P(None, 'mp')
- grad_down_weight: float32 [3072, 768], P('mp')
The draws below stay inside these ranges and needn't reach their ends.
Inputs may be any that keep to these rules, and one draw needn't show every extreme that they name: `seg_ids`: within a row the clip number never falls, each of the 4 numbers appears, no clip has more than 384 frames and some clip in each row has exactly 384. A caption's first text_lens tokens are real; its other rows are padding that no frame attends to.
All inputs are finite; a program needn't handle non-finite values.
Results may differ from the reference program's by a relative error of at most 0.022.
Values may be sent and summed in bfloat16 or wider, within the bound.
No kernel may reach another device: no remote copies, remote signals or barrier semaphores. Data moves between devices by JAX's collectives and lax.ppermute only.
A program may use at most 320 MiB of HBM per device.

```python
import math
import jax
import jax.numpy as jnp
import numpy as np
from jax import lax

D = 768
HEADS = 12
HD = 64
FF = 3072
CAPTION = 77
TSTEPS = 1000
FRAMES = 512
SEGS = 4
MOST = 384
ROWS = 32
TOKENS = 16384
NSEG = 128


def draw_text_lens(key, part):
    drawn = jax.random.randint(key, (NSEG,), 1, CAPTION + 1).astype(jnp.int32)
    drawn = drawn.at[0].set(CAPTION)
    return drawn.at[1].set(1)


def with_ends(array, stream_key, smallest, high):
    spot = [jax.random.randint(jax.random.fold_in(stream_key, axis), (), 0, length) for axis, length in enumerate(array.shape)]
    longest = array.shape.index(max(array.shape))
    neighbour = spot[:longest] + [(spot[longest] + 1) % array.shape[longest]] + spot[longest + 1:]
    return array.at[tuple(spot)].set(smallest).at[tuple(neighbour)].set(high)


def shard_levels(own_key, shape, cuts, low, largest):
    factor_of, own = 1.0, jax.random.fold_in(own_key, 6)
    for axis_at, shards_of in cuts:
        steps = jnp.exp(jax.random.uniform(jax.random.fold_in(own, axis_at), (shards_of,), jnp.float32, low / len(cuts), largest / len(cuts)))
        factor_of = factor_of * jnp.repeat(steps, shape[axis_at] // shards_of).reshape([-1 if axis == axis_at else 1 for axis in range(len(shape))])
    return factor_of


def length_profile(amount, total, most, skew):
    loads = [(1 << 20) // math.isqrt(rank ** skew) + 1 for rank in range(2, amount + 1)]
    spare, holding = total - most - (amount - 1), [1] * (amount - 1)
    while spare > 0:
        movable = [i for i in range(amount - 1) if holding[i] < most]
        pool, remaining = sum([loads[i] for i in movable]), spare
        for i in movable:
            more = min(most - holding[i], max(1, remaining * loads[i] // pool), spare)
            holding[i] = holding[i] + more
            spare = spare - more
    return np.array([most] + holding)


def uneven(key, number_of, total, reach, lean):
    if number_of == 2:
        one = jax.random.randint(key, (), max(1, total - reach), min(reach, total - 1) + 1)
        return jnp.stack([one, total - one])
    tallies = jnp.asarray(length_profile(number_of, total, reach, lean), jnp.int32)
    twos = (number_of - 1) // 2
    giver, taker = tallies[1:1 + 2 * twos:2], tallies[2:2 + 2 * twos:2]
    slack = jnp.minimum(giver - 1, reach - taker)
    moved = jax.random.randint(jax.random.fold_in(key, 1), (twos,), 0, 1 << 20) % (slack + 1)
    tallies = tallies.at[1:1 + 2 * twos:2].set(giver - moved).at[2:2 + 2 * twos:2].set(taker + moved)
    return tallies[jax.random.permutation(jax.random.fold_in(key, 2), number_of)]


def bell_draw(key, shape, deviation, bound, shards=(), dtype=jnp.bfloat16):
    values = deviation * jax.random.normal(key, shape, jnp.float32)
    if shards:
        values = values * shard_levels(key, shape, shards, -0.22, 0.18)
    return jnp.clip(values, -bound, bound).astype(dtype)


def setup_inputs(seed: int = 0) -> dict:
    splits = jax.random.split(jax.random.key(seed), 20)
    frames = bell_draw(splits[0], (TOKENS, D), 1.0, 6.0, ((0, 32),))
    seg_ids = jax.vmap(lambda own: jnp.searchsorted(jnp.cumsum(uneven(own, SEGS, FRAMES, MOST, 1)), jnp.arange(FRAMES), side="right"))(jax.random.split(splits[1], ROWS)).reshape((ROWS, FRAMES)).astype(jnp.int32)
    text = bell_draw(splits[2], (NSEG, CAPTION, D), 1.0, 6.0, ((0, 32),))
    text_lens = draw_text_lens(jax.random.fold_in(splits[19], 71), 0)
    step_ids = with_ends(jax.random.randint(splits[4], (NSEG,), 0, TSTEPS), jax.random.fold_in(splits[4], 1), 0, TSTEPS - 1).astype(jnp.int32)
    step_table = bell_draw(splits[5], (TSTEPS, D), 1.0, 6.0, ((1, 8),))
    ada_weight = bell_draw(splits[6], (D, 6 * D), D ** -0.5, 0.21875, ((0, 8),))
    ada_bias = bell_draw(splits[7], (6 * D,), 0.5, 3.0)
    query_w = bell_draw(splits[8], (D, D), D ** -0.5, 0.21875, ((1, 8),))
    key_w = bell_draw(splits[9], (D, D), D ** -0.5, 0.21875, ((1, 8),))
    value_w = bell_draw(splits[10], (D, D), D ** -0.5, 0.21875, ((1, 8),))
    out_w = bell_draw(splits[11], (D, D), (max(D // 32, 4)) ** -0.5, 1.25, ((0, 8),))
    cross_query_w = bell_draw(splits[12], (D, D), D ** -0.5, 0.21875, ((1, 8),))
    cross_key_w = bell_draw(splits[13], (D, D), D ** -0.5, 0.21875, ((1, 8),))
    cross_value_w = bell_draw(splits[14], (D, D), D ** -0.5, 0.21875, ((1, 8),))
    cross_out_w = bell_draw(splits[15], (D, D), (max(D // 32, 4)) ** -0.5, 1.25, ((0, 8),))
    up_weight = bell_draw(splits[16], (D, FF), D ** -0.5, 0.21875, ((1, 8),))
    down_weight = bell_draw(splits[17], (FF, D), (FF // 4) ** -0.5, 0.21875, ((0, 8),))
    out_grad = bell_draw(splits[18], (TOKENS, D), 1.0, 6.0, ((0, 32),))
    return dict(frames=frames, seg_ids=seg_ids, text=text, text_lens=text_lens, step_ids=step_ids, step_table=step_table, ada_weight=ada_weight, ada_bias=ada_bias, query_w=query_w, key_w=key_w, value_w=value_w, out_w=out_w, cross_query_w=cross_query_w, cross_key_w=cross_key_w, cross_value_w=cross_value_w, cross_out_w=cross_out_w, up_weight=up_weight, down_weight=down_weight, out_grad=out_grad)


@jax.custom_vjp
def low(v):
    return lax.optimization_barrier(v.astype(jnp.bfloat16)).astype(jnp.float32)

@jax.custom_vjp
def low_back(v):
    return v

def low_keep(v):
    return (low(v), None)

def low_pass(kept, grad):
    return (grad,)

def back_keep(v):
    return (v, None)

def back_low(kept, grad):
    return (low(grad),)
low.defvjp(low_keep, low_pass)
low_back.defvjp(back_keep, back_low)
highest = lax.Precision.HIGHEST
epsilon = 1e-06
masked_score = -1e+30

def normalize(values):
    centre = values - lax.optimization_barrier(jnp.mean(values, axis=-1, keepdims=True))
    return centre * lax.rsqrt(lax.optimization_barrier(jnp.mean(centre * centre, axis=-1, keepdims=True)) + epsilon)

def project(left, right):
    return jnp.einsum('...d,de->...e', left, right, precision=highest)

def row_attention(block_item):
    query, keys, values, allowed = block_item
    scores = low_back(jnp.einsum('qhe,khe->hqk', query, keys, precision=highest) * HD ** (-0.5))
    scores = jnp.where(allowed[None], scores, masked_score)
    shifted = jnp.exp(scores - lax.optimization_barrier(jnp.max(scores, axis=-1, keepdims=True)))
    weights = shifted / lax.optimization_barrier(jnp.sum(shifted, axis=-1, keepdims=True))
    return jnp.einsum('hqk,khe->qhe', low(weights), values, precision=highest)

def block_forward(frames_in, text_in, seg_rows, lens_in, steps_in, table, ada_weight, ada_bias, query_w, key_w, value_w, out_w, cross_query_w, cross_key_w, cross_value_w, cross_out_w, up_weight, down_weight):
    row_count = frames_in.shape[0]
    cond = jnp.take(table, steps_in, axis=0)
    silu_cond = low(jax.nn.silu(cond))
    modulation = (project(silu_cond, ada_weight) + ada_bias).reshape(row_count, SEGS, 6 * D)
    chooser = (seg_rows[:, :, None] == jnp.arange(SEGS)[None, None, :]).astype(jnp.float32)
    frame_mod = jnp.einsum('rsk,rkc->rsc', chooser, modulation, precision=highest)
    shift_one, scale_one, gate_one, shift_two, scale_two, gate_two = jnp.split(frame_mod, 6, axis=-1)
    head_shape = (row_count, FRAMES, HEADS, HD)
    first_in = low(normalize(frames_in) * (1.0 + scale_one) + shift_one)
    query = low_back(low(project(first_in, query_w))).reshape(head_shape)
    keys = low_back(low(project(first_in, key_w))).reshape(head_shape)
    values = low_back(low(project(first_in, value_w))).reshape(head_shape)
    same_seg = seg_rows[:, :, None] == seg_rows[:, None, :]
    self_mix = lax.map(jax.checkpoint(row_attention), (query, keys, values, same_seg))
    self_mix = low_back(low(self_mix.reshape(row_count, FRAMES, D)))
    self_out = low_back(project(self_mix, out_w))
    resid_one = frames_in + gate_one * self_out
    second_in = low(normalize(resid_one))
    text_shape = (row_count, SEGS * CAPTION, HEADS, HD)
    cross_query = low_back(low(project(second_in, cross_query_w))).reshape(head_shape)
    cross_keys = low_back(low(project(text_in, cross_key_w))).reshape(text_shape)
    cross_values = low_back(low(project(text_in, cross_value_w))).reshape(text_shape)
    key_segment = jnp.arange(SEGS * CAPTION) // CAPTION
    valid_key = (jnp.arange(CAPTION)[None, None, :] < lens_in.reshape(row_count, SEGS)[:, :, None]).reshape(row_count, SEGS * CAPTION)
    allowed = (seg_rows[:, :, None] == key_segment[None, None, :]) & valid_key[:, None, :]
    cross_mix = lax.map(jax.checkpoint(row_attention), (cross_query, cross_keys, cross_values, allowed))
    cross_mix = low_back(low(cross_mix.reshape(row_count, FRAMES, D)))
    cross_out = low_back(project(cross_mix, cross_out_w))
    resid_two = resid_one + cross_out
    third_in = low(normalize(resid_two) * (1.0 + scale_two) + shift_two)
    pre_act = low_back(project(third_in, up_weight))
    activated = low(jax.nn.gelu(pre_act, approximate=True))
    mlp_out = low_back(project(activated, down_weight))
    return resid_two + gate_two * mlp_out

def reference(frames, seg_ids, text, text_lens, step_ids, step_table, ada_weight, ada_bias, query_w, key_w, value_w, out_w, cross_query_w, cross_key_w, cross_value_w, cross_out_w, up_weight, down_weight, out_grad):
    per_block = 8 if ROWS % 8 == 0 else 1
    blocks = ROWS // per_block
    params = tuple((weight.astype(jnp.float32) for weight in (step_table, ada_weight, ada_bias, query_w, key_w, value_w, out_w, cross_query_w, cross_key_w, cross_value_w, cross_out_w, up_weight, down_weight)))
    items = (frames.reshape(blocks, per_block, FRAMES, D), text.reshape(blocks, per_block * SEGS, CAPTION, D), seg_ids.reshape(blocks, per_block, FRAMES), text_lens.reshape(blocks, per_block * SEGS), step_ids.reshape(blocks, per_block * SEGS), out_grad.reshape(blocks, per_block, FRAMES, D))

    def one_block(totals, block_item):
        block_frames, block_text, block_ids, block_lens, block_steps, block_grad = block_item

        def forward(frames_in, text_in, *weights):
            return block_forward(frames_in, text_in, block_ids, block_lens, block_steps, *weights)
        output, pullback = jax.vjp(forward, block_frames.astype(jnp.float32), block_text.astype(jnp.float32), *params)
        gradients = pullback(block_grad.astype(jnp.float32))
        totals = tuple((total + piece for total, piece in zip(totals, gradients[2:])))
        return (totals, (output.astype(jnp.bfloat16), gradients[0], gradients[1]))
    initial = tuple((jnp.zeros_like(weight) for weight in params))
    totals, (outputs, grad_frames, grad_text) = lax.scan(one_block, initial, items)
    return (outputs.reshape(TOKENS, D), grad_frames.reshape(TOKENS, D), grad_text.reshape(NSEG, CAPTION, D), totals[0], totals[1], totals[2], totals[3], totals[4], totals[5], totals[6], totals[7], totals[8], totals[9], totals[10], totals[11], totals[12])
```

```python
from functools import partial

import jax
import jax.numpy as jnp
from jax import lax
from jax.experimental import pallas as pl
from jax.experimental.pallas import tpu as pltpu
from jax.sharding import Mesh, PartitionSpec as P

HEADS = 12
HD = 64
CAPTION = 77
SEGS = 4

PAIR = 2 * HD
highest = lax.Precision.HIGHEST
epsilon = 1e-06
masked_score = -1e30
bf16 = jnp.bfloat16
f32 = jnp.float32
FINE = ("y", "core", "z", "x")
WEIGHT_ORDER = ("z", "x", "y", "core")
VMEM = 48 << 20


def shifted(value, axis, steps):
    count = lax.axis_size(axis)
    return lax.ppermute(value, axis, [(k, (k + steps) % count) for k in range(count)])


def gather_axis(value, axis):
    count = lax.axis_size(axis)
    if count == 1:
        return value[None]
    me = lax.axis_index(axis)
    pieces = [value] + [shifted(value, axis, s) for s in range(1, count)]
    if count == 2:
        first = me == 0
        return jnp.stack(
            [jnp.where(first, pieces[0], pieces[1]), jnp.where(first, pieces[1], pieces[0])]
        )
    turned = jnp.stack(pieces[::-1] + pieces[::-1])
    return lax.dynamic_slice_in_dim(turned, count - 1 - me, count, 0)


def scatter_axis(value, axis, dim):
    count = lax.axis_size(axis)
    me = lax.axis_index(axis)

    def piece(which):
        return lax.dynamic_index_in_dim(value, which % count, dim, keepdims=False)

    arrived = [shifted(piece(me + s), axis, s) for s in range(1, count)]
    total = piece(me).astype(f32)
    for part in arrived:
        total = total + part.astype(f32)
    return total


def gather_weights(shards):
    count, rows, width = len(shards), shards[0].shape[0], shards[0].shape[1]
    copies = lax.axis_size("y") * lax.axis_size("core")
    part = rows // copies
    mine = lax.axis_index("y") * lax.axis_size("core") + lax.axis_index("core")
    stacked = jnp.stack([lax.dynamic_slice_in_dim(s, mine * part, part, 0) for s in shards])
    column = gather_axis(stacked, "z")
    half = width // 2
    left = gather_axis(gather_axis(column[..., :half], "x"), "y")
    right = gather_axis(gather_axis(column[..., half:], "y"), "x")
    left = gather_axis(left, "core").transpose(4, 3, 2, 1, 0, 5, 6)
    right = gather_axis(right, "core").transpose(4, 3, 1, 2, 0, 5, 6)
    whole = jnp.concatenate([left, right], axis=-1)
    return whole.reshape(count, -1, width)


def pair_product(left, right):
    half = right.shape[1] // 2
    me = lax.axis_index("core")
    mine = lax.dynamic_slice_in_dim(right, me * half, half, 1)
    other = lax.dynamic_slice_in_dim(right, (1 - me) * half, half, 1)
    sent = shifted(inner_rows(left, other).astype(bf16), "core", 1)
    return (inner_rows(left, mine) + sent.astype(f32)).astype(bf16)


def reduce_grads(grads):
    nz, nx, ny = (lax.axis_size(a) for a in ("z", "x", "y"))
    width = grads[0].shape[1]
    stacked = [g.reshape(nz, nx, ny, -1, width) for g in grads]
    half = stacked[0].shape[3] // 2
    first = jnp.stack([g[:, :, :, :half] for g in stacked])
    second = jnp.stack([g[:, :, :, half:] for g in stacked])
    first = scatter_axis(first, "x", 2).astype(bf16)
    second = scatter_axis(second, "y", 3).astype(bf16)
    first = scatter_axis(first, "y", 2).astype(bf16)
    second = scatter_axis(second, "x", 2).astype(bf16)
    both = jnp.concatenate([first, second], axis=2)
    done = scatter_axis(both, "z", 1).astype(bf16)
    done = gather_axis(gather_axis(done, "y"), "core")
    done = done.transpose(2, 1, 3, 0, 4)
    return done.reshape(len(grads), -1, width * lax.axis_size("core"))


def gather_all(rows):
    value = gather_axis(gather_axis(rows, "z"), "x")
    value = gather_axis(gather_axis(value, "y"), "core")
    value = value.transpose(1, 0, 3, 2, 4, 5)
    return value.reshape(-1, rows.shape[-1])


def normalize(values):
    centre = values - jnp.mean(values, axis=-1, keepdims=True)
    inverse = lax.rsqrt(jnp.mean(centre * centre, axis=-1, keepdims=True) + epsilon)
    return (centre * inverse, inverse)


def norm_back(normed, inverse, upstream):
    mean_grad = jnp.mean(upstream, axis=-1, keepdims=True)
    mean_both = jnp.mean(upstream * normed, axis=-1, keepdims=True)
    return inverse * (upstream - mean_grad - normed * mean_both)


def matmul(left, right):
    return jnp.dot(left, right, preferred_element_type=f32)


def inner_rows(left, right):
    return lax.dot_general(left, right, (((0,), (0,)), ((), ())), preferred_element_type=f32)


def outer_cols(left, right):
    return lax.dot_general(left, right, (((1,), (1,)), ((), ())), preferred_element_type=f32)


def gelu_back(pre_act, upstream):
    return jax.vjp(partial(jax.nn.gelu, approximate=True), pre_act)[1](upstream)[0]


def silu_back(inputs, upstream):
    return jax.vjp(jax.nn.silu, inputs)[1](upstream)[0]


def half_lanes(head):
    lane = lax.broadcasted_iota(jnp.int32, (1, PAIR), 1)
    return lane < HD if head == 0 else lane >= HD


def forward_kernel(q_ref, k_ref, v_ref, bias_ref, mix_ref):
    query = q_ref[...] * bf16(HD**-0.5)
    keys, values, bias = k_ref[...], v_ref[...], bias_ref[0]
    parts = []
    for head in range(2):
        own = jnp.where(half_lanes(head), query, bf16(0))
        scores = outer_cols(own, keys) + bias
        shifted_scores = jnp.exp(scores - jnp.max(scores, axis=1, keepdims=True))
        total = jnp.sum(shifted_scores, axis=1, keepdims=True)
        parts.append(matmul(shifted_scores.astype(bf16), values) / total)
    mix_ref[...] = jnp.where(half_lanes(0), parts[0], parts[1]).astype(bf16)


def backward_kernel(q_ref, k_ref, v_ref, bias_ref, g_ref, gq_ref, gk_ref, gv_ref):
    query = q_ref[...] * bf16(HD**-0.5)
    keys, values, bias, grad = k_ref[...], v_ref[...], bias_ref[0], g_ref[...]
    gq, gk, gv = [], [], []
    for head in range(2):
        own = half_lanes(head)
        scores = outer_cols(keys, jnp.where(own, query, bf16(0))) + bias
        raised = jnp.exp(scores - jnp.max(scores, axis=0, keepdims=True))
        weights = raised * (1.0 / jnp.sum(raised, axis=0, keepdims=True))
        grad_weights = outer_cols(jnp.where(own, values, bf16(0)), grad)
        mean = jnp.sum(weights * grad_weights, axis=0, keepdims=True)
        grad_scores = (weights * (grad_weights - mean)).astype(bf16)
        gv.append(matmul(weights.astype(bf16), grad))
        gk.append(matmul(grad_scores, query))
        gq.append(inner_rows(grad_scores, keys))
    gq_ref[...] = (jnp.where(half_lanes(0), gq[0], gq[1]) * HD**-0.5).astype(bf16)
    gk_ref[...] = jnp.where(half_lanes(0), gk[0], gk[1]).astype(bf16)
    gv_ref[...] = jnp.where(half_lanes(0), gv[0], gv[1]).astype(bf16)


def attend(query, keys, values, bias):
    rows, frames, tokens = bias.shape
    pairs = query.shape[1] // PAIR
    blocks = [pl.BlockSpec((n, PAIR), lambda r, h: (r, h)) for n in (frames, tokens, tokens)]
    return pl.pallas_call(
        forward_kernel,
        grid=(rows, pairs),
        in_specs=blocks + [pl.BlockSpec((1, frames, tokens), lambda r, h: (r, 0, 0))],
        out_specs=blocks[0],
        out_shape=jax.ShapeDtypeStruct(query.shape, bf16),
        compiler_params=pltpu.CompilerParams(vmem_limit_bytes=VMEM),
        cost_estimate=pl.CostEstimate(
            flops=4 * rows * frames * tokens * query.shape[1] * 2,
            transcendentals=rows * frames * tokens * pairs * 2,
            bytes_accessed=8 * query.size,
        ),
    )(query, keys, values, bias)


def attend_back(query, keys, values, bias, grad):
    rows, tokens, frames = bias.shape
    pairs = query.shape[1] // PAIR
    wide = pl.BlockSpec((frames, PAIR), lambda r, h: (r, h))
    held = pl.BlockSpec((tokens, PAIR), lambda r, h: (r, h))
    return pl.pallas_call(
        backward_kernel,
        grid=(rows, pairs),
        in_specs=[wide, held, held, pl.BlockSpec((1, tokens, frames), lambda r, h: (r, 0, 0)), wide],
        out_specs=[wide, held, held],
        out_shape=[jax.ShapeDtypeStruct(a.shape, bf16) for a in (query, keys, values)],
        compiler_params=pltpu.CompilerParams(vmem_limit_bytes=VMEM),
        cost_estimate=pl.CostEstimate(
            flops=10 * rows * frames * tokens * query.shape[1] * 2,
            transcendentals=rows * frames * tokens * pairs * 2,
            bytes_accessed=16 * query.size,
        ),
    )(query, keys, values, bias, grad)


def shards(
    frames,
    seg_ids,
    text,
    text_lens,
    step_ids,
    step_table,
    ada_weight,
    ada_bias,
    query_w,
    key_w,
    value_w,
    out_w,
    cross_query_w,
    cross_key_w,
    cross_value_w,
    cross_out_w,
    up_weight,
    down_weight,
    out_grad,
):
    width = frames.shape[1]
    mp = lax.axis_size("z") * lax.axis_size("x")
    position = lax.axis_index("z") * lax.axis_size("x") + lax.axis_index("x")
    rows_dev = seg_ids.shape[0] // mp
    frames_row = seg_ids.shape[1]
    segs_dev = rows_dev * SEGS
    my_ids = lax.dynamic_slice_in_dim(seg_ids, position * rows_dev, rows_dev, 0)
    my_lens = lax.dynamic_slice_in_dim(text_lens, position * segs_dev, segs_dev, 0)

    qkv = gather_weights([query_w.T, key_w.T, value_w.T]).reshape(-1, width)
    others = gather_weights([out_w, cross_query_w.T, cross_key_w.T, cross_value_w.T, cross_out_w])
    out_full, cquery_t, cout_full = others[0], others[1], others[4]
    ckv_t = others[2:4].reshape(-1, width)
    copies = lax.axis_size("y") * lax.axis_size("core")
    mine = lax.axis_index("y") * lax.axis_size("core") + lax.axis_index("core")
    hidden_part = down_weight.shape[0] // copies
    ff_mine = lax.dynamic_slice_in_dim(
        jnp.concatenate([up_weight.T, down_weight], axis=1), mine * hidden_part, hidden_part, 0
    )
    ff_full = lax.all_gather(ff_mine, WEIGHT_ORDER, axis=0, tiled=True)
    up_t, down_full = ff_full[:, :width], ff_full[:, width:]

    table_low = step_table
    choose_step = (step_ids[:, None] == jnp.arange(step_table.shape[0])[None, :]).astype(bf16)
    silu_mine = jax.nn.silu(matmul(choose_step, table_low)).astype(bf16)
    partial_mod = matmul(silu_mine, ada_weight).astype(bf16)
    partial_mod = partial_mod.reshape(
        lax.axis_size("z"), lax.axis_size("x"), segs_dev, partial_mod.shape[1]
    )
    modulation = scatter_axis(scatter_axis(partial_mod, "x", 1).astype(bf16), "z", 0)
    modulation = modulation + ada_bias.astype(f32)
    flat_ids = my_ids.reshape(-1)
    row_of = jnp.arange(flat_ids.shape[0]) // frames_row
    clip = flat_ids + row_of * SEGS
    chosen = clip[:, None] == jnp.arange(segs_dev)[None, :]

    def per_frame(index):
        table = modulation[:, index * width : (index + 1) * width]
        value = jnp.broadcast_to(table[0:1], (clip.shape[0], width))
        for segment in range(1, segs_dev):
            value = jnp.where(chosen[:, segment : segment + 1], table[segment : segment + 1], value)
        return value

    shift_one, scale_one, gate_one, shift_two, scale_two, gate_two = map(per_frame, range(6))

    same_seg = my_ids[:, :, None] == my_ids[:, None, :]
    self_bias = jnp.where(same_seg, 0.0, masked_score).astype(f32)
    key_segment = jnp.arange(SEGS * CAPTION) // CAPTION
    valid_key = (
        jnp.arange(CAPTION)[None, None, :] < my_lens.reshape(rows_dev, SEGS)[:, :, None]
    ).reshape(rows_dev, SEGS * CAPTION)
    allowed = (my_ids[:, :, None] == key_segment[None, None, :]) & valid_key[:, None, :]
    cross_bias = jnp.where(allowed, 0.0, masked_score).astype(f32)
    allowed_t = (my_ids[:, None, :] == key_segment[None, :, None]) & valid_key[:, :, None]
    cross_bias_t = jnp.where(allowed_t, 0.0, masked_score).astype(f32)

    base = frames.astype(f32)
    text_flat = text.reshape(-1, width)
    normed_one, inverse_one = normalize(base)
    first_in = (normed_one * (1.0 + scale_one) + shift_one).astype(bf16)
    query, keys, values = (
        outer_cols(first_in, qkv[i * width : (i + 1) * width]).astype(bf16) for i in range(3)
    )
    self_mix = attend(query, keys, values, self_bias)
    self_out = matmul(self_mix, out_full)
    resid_one = base + gate_one * self_out
    normed_two, inverse_two = normalize(resid_one)
    second_in = normed_two.astype(bf16)
    cross_query = outer_cols(second_in, cquery_t).astype(bf16)
    cross_keys = outer_cols(text_flat, ckv_t[:width]).astype(bf16)
    cross_values = outer_cols(text_flat, ckv_t[width:]).astype(bf16)
    cross_mix = attend(cross_query, cross_keys, cross_values, cross_bias)
    resid_two = resid_one + matmul(cross_mix, cout_full)
    normed_three, inverse_three = normalize(resid_two)
    third_in = (normed_three * (1.0 + scale_two) + shift_two).astype(bf16)
    pre_act = outer_cols(third_in, up_t)
    activated = jax.nn.gelu(pre_act, approximate=True).astype(bf16)
    mlp_out = matmul(activated, down_full)
    layer_out = (resid_two + gate_two * mlp_out).astype(bf16)

    upstream = out_grad.astype(f32)
    grad_gate_two = upstream * mlp_out
    grad_mlp = (gate_two * upstream).astype(bf16)
    grad_pre = gelu_back(pre_act, outer_cols(grad_mlp, down_full)).astype(bf16)
    grad_down = pair_product(activated, grad_mlp)
    grad_up_t = pair_product(grad_pre, third_in)
    grad_third = matmul(grad_pre, up_t)
    shard_up, shard_down = reduce_grads([grad_up_t, grad_down])
    grad_resid_two = upstream + norm_back(
        normed_three, inverse_three, grad_third * (1.0 + scale_two)
    )
    grad_cross = grad_resid_two.astype(bf16)
    grad_cout = pair_product(cross_mix, grad_cross)
    grad_cross_mix = outer_cols(grad_cross, cout_full).astype(bf16)
    grad_cq, grad_ck, grad_cv = attend_back(
        cross_query, cross_keys, cross_values, cross_bias_t, grad_cross_mix
    )
    grad_cquery_t = pair_product(grad_cq, second_in)
    grad_ckey_t = pair_product(grad_ck, text_flat)
    grad_cvalue_t = pair_product(grad_cv, text_flat)
    grad_second = matmul(grad_cq, cquery_t)
    grad_text = matmul(grad_ck, ckv_t[:width]) + matmul(grad_cv, ckv_t[width:])
    grad_resid_one = grad_resid_two + norm_back(normed_two, inverse_two, grad_second)
    grad_gate_one = grad_resid_one * self_out
    grad_self = (gate_one * grad_resid_one).astype(bf16)
    grad_out = pair_product(self_mix, grad_self)
    shard_out, shard_cout, shard_cquery, shard_ckey, shard_cvalue = reduce_grads(
        [grad_out, grad_cout, grad_cquery_t, grad_ckey_t, grad_cvalue_t]
    )
    grad_self_mix = outer_cols(grad_self, out_full).astype(bf16)
    grad_sq, grad_sk, grad_sv = attend_back(query, keys, values, self_bias, grad_self_mix)
    grad_query_t = pair_product(grad_sq, first_in)
    grad_key_t = pair_product(grad_sk, first_in)
    grad_value_t = pair_product(grad_sv, first_in)
    shard_query, shard_key, shard_value = reduce_grads([grad_query_t, grad_key_t, grad_value_t])
    grad_first = (
        matmul(grad_sq, qkv[:width])
        + matmul(grad_sk, qkv[width : 2 * width])
        + matmul(grad_sv, qkv[2 * width :])
    )
    grad_frames = grad_resid_one + norm_back(
        normed_one, inverse_one, grad_first * (1.0 + scale_one)
    )

    chooser = chosen.astype(f32)

    def clip_sums(value):
        return lax.dot_general(chooser, value, (((0,), (0,)), ((), ())), precision=highest)

    late = jnp.concatenate([clip_sums(grad_first), clip_sums(grad_first * normed_one)], axis=1)
    early = jnp.concatenate(
        [
            clip_sums(grad_gate_one),
            clip_sums(grad_third),
            clip_sums(grad_third * normed_three),
            clip_sums(grad_gate_two),
        ],
        axis=1,
    )
    early_all = gather_all(early.astype(bf16))
    late_all = gather_all(late.astype(bf16))
    grad_mod_all = jnp.concatenate([late_all, early_all], axis=1)
    steps_all = gather_axis(gather_axis(step_ids.astype(f32), "y"), "core")
    steps_all = steps_all.transpose(1, 0, 2).reshape(-1)
    choose_all = (
        steps_all[:, None] == jnp.arange(step_table.shape[0]).astype(f32)[None, :]
    ).astype(bf16)
    cond_all = matmul(choose_all, table_low)
    silu_all = jax.nn.silu(cond_all).astype(bf16)
    grad_ada_w = inner_rows(silu_all, grad_mod_all)
    grad_ada_b = jnp.sum(grad_mod_all.astype(f32), axis=0)
    grad_cond = silu_back(cond_all, outer_cols(grad_mod_all, ada_weight))
    grad_table = lax.dot_general(
        choose_all.astype(f32), grad_cond, (((0,), (0,)), ((), ())), precision=highest
    )

    def columns(value):
        return value.T.astype(f32)

    return (
        layer_out,
        grad_frames,
        grad_text.reshape(text.shape),
        grad_table,
        grad_ada_w,
        grad_ada_b,
        columns(shard_query),
        columns(shard_key),
        columns(shard_value),
        shard_out.astype(f32),
        columns(shard_cquery),
        columns(shard_ckey),
        columns(shard_cvalue),
        shard_cout.astype(f32),
        columns(shard_up),
        shard_down.astype(f32),
    )


def solution(mesh):
    dp, mp = mesh.shape["dp"], mesh.shape["mp"]
    fine = Mesh(mesh.devices.reshape(dp // 2, 2, mp // 2, 2), FINE)
    dp_axes, mp_axes = ("y", "core"), ("z", "x")
    return jax.shard_map(
        shards,
        mesh=fine,
        in_specs=(
            P(FINE, None),
            P(dp_axes, None),
            P(FINE, None, None),
            P(dp_axes),
            P(dp_axes),
            P(None, mp_axes),
            P(mp_axes, None),
            P(),
            P(None, mp_axes),
            P(None, mp_axes),
            P(None, mp_axes),
            P(mp_axes, None),
            P(None, mp_axes),
            P(None, mp_axes),
            P(None, mp_axes),
            P(mp_axes, None),
            P(None, mp_axes),
            P(mp_axes, None),
            P(FINE, None),
        ),
        out_specs=(
            P(FINE, None),
            P(FINE, None),
            P(FINE, None, None),
            P(None, mp_axes),
            P(mp_axes, None),
            P(),
            P(None, mp_axes),
            P(None, mp_axes),
            P(None, mp_axes),
            P(mp_axes, None),
            P(None, mp_axes),
            P(None, mp_axes),
            P(None, mp_axes),
            P(mp_axes, None),
            P(None, mp_axes),
            P(mp_axes, None),
        ),
        check_vma=False,
    )
```

```python
from functools import partial

import jax
import jax.numpy as jnp
from jax import lax
from jax.experimental import pallas as pl
from jax.experimental.pallas import tpu as pltpu
from jax.sharding import Mesh, PartitionSpec as P

HEADS = 12
HD = 64
CAPTION = 77
SEGS = 4

QUAD = 4 * HD
highest = lax.Precision.HIGHEST
epsilon = 1e-06
masked_score = -1e30
bf16 = jnp.bfloat16
f32 = jnp.float32
FINE = ("y", "core", "za", "zb", "x")
MP_AXES = ("za", "zb", "x")
VMEM = 48 << 20


def shifted(value, axis, steps):
    count = lax.axis_size(axis)
    with jax.named_scope(f"to_{axis}_{steps}"):
        return lax.ppermute(value, axis, [(k, (k + steps) % count) for k in range(count)])


def gather_axis(value, axis, *hold):
    count = lax.axis_size(axis)
    me = lax.axis_index(axis)
    pieces = [shifted(value, axis, s) for s in range(1, count)]
    if hold:
        pieces = [after(piece, *hold) for piece in pieces]
    pieces = [value] + pieces

    def at(place):
        turn = (me - place) % count
        chosen = pieces[0]
        for s in range(1, count):
            chosen = jnp.where(turn == s, pieces[s], chosen)
        return chosen

    return jnp.stack([at(place) for place in range(count)])


def after(value, *done):
    return lax.optimization_barrier((value, *done))[0]


def picked(terms, dim, which):
    return [lax.dynamic_index_in_dim(t, which, dim, keepdims=False) for t in terms]


def summed(terms):
    total = terms[0].astype(f32)
    for term in terms[1:]:
        total = total + term.astype(f32)
    return total


def launch(terms, axis, dim):
    count = lax.axis_size(axis)
    me = lax.axis_index(axis)
    sent = [
        summed(picked(terms, dim, (me + s) % count)).astype(bf16) for s in range(1, count)
    ]
    arrived = [shifted(part, axis, s) for s, part in enumerate(sent, 1)]
    return picked(terms, dim, me), sent, arrived


def launch_wide(value, axis, dim):
    count = lax.axis_size(axis)
    me = lax.axis_index(axis)
    sent = [picked([value], dim, (me + s) % count)[0] for s in range(1, count)]
    arrived = [shifted(part, axis, s) for s, part in enumerate(sent, 1)]
    return picked([value], dim, me), sent, arrived


def landed(started, *done):
    kept, _, arrived = started
    if done:
        arrived = [after(part, *done) for part in arrived]
    return kept + arrived


def split_rows(part):
    grid = [lax.axis_size(a) for a in (*MP_AXES, "y")]
    return part.reshape(part.shape[0], *grid, -1, part.shape[-1])


def first_stage(mine_a, mine_b, other_a, other_b, *done):
    other_a, other_b = shifted(other_a, "core", 1), shifted(other_b, "core", 1)
    if done:
        other_a, other_b = after(other_a, *done), after(other_b, *done)
    left = [split_rows(mine_a), split_rows(other_a)]
    right = [split_rows(mine_b), split_rows(other_b)]
    return launch(left, "x", 3), launch(right, "y", 4)


def second_stage(stage, *done):
    left = launch(landed(stage[0], *done), "y", 3)
    right = launch(landed(stage[1], *done), "x", 3)
    return left, right


def third_stage(stage, *done):
    left, right = (summed(landed(part, *done)).astype(bf16) for part in stage)
    return launch([jnp.stack([left, right])], "zb", 3)


def fourth_stage(stage, *done):
    return launch(landed(stage, *done), "za", 2)


def sends(stage):
    return stage[0][1] + stage[1][1]


def assemble(left, right):
    left = left.transpose(5, 4, 3, 2, 1, 0, 6, 7)
    right = right.transpose(5, 4, 3, 1, 2, 0, 6, 7)
    whole = jnp.concatenate([left, right], axis=-1)
    return whole.reshape(whole.shape[0], -1, whole.shape[-1])


def parts_kernel(mine_ref, *refs):
    *sources, up_ref, down_ref, first_ref, more_ref, feed_ref, turned_ref, tall_ref = refs
    rows, hidden = first_ref.shape[1], feed_ref.shape[1]
    width = down_ref.shape[1]

    def own(ref, count):
        return ref[pl.ds(pl.multiple_of(mine_ref[0] * count, 8), count), :]

    for which, source in enumerate(sources):
        shard = source[...].astype(f32)
        turned_ref[...] = shard.T if shard.shape[1] < width else shard
        target, place = (first_ref, which) if which < 3 else (more_ref, which - 3)
        target[place] = own(turned_ref, rows).astype(bf16)
    tall_ref[...] = up_ref[...].astype(f32).T
    feed_ref[0] = own(tall_ref, hidden).astype(bf16)
    tall_ref[...] = down_ref[...].astype(f32)
    feed_ref[1] = own(tall_ref, hidden).astype(bf16)


def weight_parts(weights, up_weight, down_weight):
    copies = lax.axis_size("y") * lax.axis_size("core")
    mine = lax.axis_index("y") * lax.axis_size("core") + lax.axis_index("core")
    hidden, width = down_weight.shape
    shard = min(weights[0].shape)
    rows = shard // copies
    if rows % 8 or hidden // copies % 8:

        def own(value):
            part = value.shape[0] // copies
            return lax.dynamic_slice_in_dim(value, mine * part, part, 0)

        turned = [own(w.T if w.shape[1] < width else w) for w in weights]
        feed_part = jnp.stack([own(up_weight.T), own(down_weight)])
        return jnp.stack(turned[:3]), jnp.stack(turned[3:]), feed_part
    shapes = [
        (3, rows, width),
        (len(weights) - 3, rows, width),
        (2, hidden // copies, width),
    ]

    def whole(shape):
        return pl.BlockSpec(shape, lambda i: (0,) * len(shape))

    sources = [*weights, up_weight, down_weight]
    return pl.pallas_call(
        parts_kernel,
        grid=(1,),
        in_specs=[pl.BlockSpec(memory_space=pltpu.SMEM)] + [whole(w.shape) for w in sources],
        out_specs=[whole(shape) for shape in shapes],
        out_shape=[jax.ShapeDtypeStruct(shape, bf16) for shape in shapes],
        scratch_shapes=[pltpu.VMEM((shard, width), f32), pltpu.VMEM((hidden, width), f32)],
        compiler_params=pltpu.CompilerParams(vmem_limit_bytes=VMEM),
    )(mine.reshape(1), *sources)


def columns_whole(done):
    done = gather_axis(gather_axis(done, "y"), "core")
    done = done.transpose(2, 3, 1, 4, 0, 5)
    return done.reshape(-1, done.shape[2] * done.shape[3], done.shape[4] * done.shape[5])


def rows_whole(done):
    done = gather_axis(gather_axis(done, "y"), "core")
    done = done.transpose(2, 3, 0, 1, 4, 5)
    return done.reshape(done.shape[0], -1, done.shape[5])


def normalize(values):
    centre = values - jnp.mean(values, axis=-1, keepdims=True)
    inverse = lax.rsqrt(jnp.mean(centre * centre, axis=-1, keepdims=True) + epsilon)
    return (centre * inverse, inverse)


def norm_back(normed, inverse, upstream):
    mean_grad = jnp.mean(upstream, axis=-1, keepdims=True)
    mean_both = jnp.mean(upstream * normed, axis=-1, keepdims=True)
    return inverse * (upstream - mean_grad - normed * mean_both)


def matmul(left, right):
    return jnp.dot(left, right, preferred_element_type=f32)


def inner_rows(left, right):
    return lax.dot_general(left, right, (((0,), (0,)), ((), ())), preferred_element_type=f32)


def outer_cols(left, right):
    return lax.dot_general(left, right, (((1,), (1,)), ((), ())), preferred_element_type=f32)


def gelu_back(pre_act, upstream):
    return jax.vjp(partial(jax.nn.gelu, approximate=True), pre_act)[1](upstream)[0]


def silu_back(inputs, upstream):
    return jax.vjp(jax.nn.silu, inputs)[1](upstream)[0]


def own_lanes(head):
    lane = lax.broadcasted_iota(jnp.int32, (1, QUAD), 1)
    return (lane >= head * HD) & (lane < (head + 1) * HD)


def merged(parts):
    whole = parts[0]
    for head in range(1, len(parts)):
        whole = jnp.where(own_lanes(head), parts[head], whole)
    return whole


def forward_kernel(q_ref, k_ref, v_ref, bias_ref, mix_ref):
    query = q_ref[...] * bf16(HD**-0.5)
    keys, values, bias = k_ref[...], v_ref[...], bias_ref[0]
    parts = []
    for head in range(QUAD // HD):
        own = jnp.where(own_lanes(head), query, bf16(0))
        scores = outer_cols(own, keys) + bias
        raised = jnp.exp(scores - jnp.max(scores, axis=1, keepdims=True))
        total = jnp.sum(raised, axis=1, keepdims=True)
        parts.append(matmul(raised.astype(bf16), values) / total)
    mix_ref[...] = merged(parts).astype(bf16)


def backward_kernel(
    core_ref,
    q_ref,
    k_ref,
    v_ref,
    mix_ref,
    bias_ref,
    out_w_ref,
    q_w_ref,
    k_w_ref,
    v_w_ref,
    back_ref,
    x_ref,
    *rest,
):
    *source, in_ref, mine_a, mine_b, other_a, other_b = rest
    text_ref, text_grad_ref = source if source else (x_ref, in_ref)
    query = q_ref[...] * bf16(HD**-0.5)
    keys, values, bias = k_ref[...], v_ref[...], bias_ref[0]
    back = back_ref[...]
    grad = outer_cols(back, out_w_ref[...]).astype(bf16)
    gq, gk, gv = [], [], []
    for head in range(QUAD // HD):
        own = own_lanes(head)
        scores = outer_cols(keys, jnp.where(own, query, bf16(0))) + bias
        raised = jnp.exp(scores - jnp.max(scores, axis=0, keepdims=True))
        weights = raised * (1.0 / jnp.sum(raised, axis=0, keepdims=True))
        grad_weights = outer_cols(jnp.where(own, values, bf16(0)), grad)
        mean = jnp.sum(weights * grad_weights, axis=0, keepdims=True)
        grad_scores = (weights * (grad_weights - mean)).astype(bf16)
        gv.append(matmul(weights.astype(bf16), grad))
        gk.append(matmul(grad_scores, query))
        gq.append(inner_rows(grad_scores, keys))
    gq = (merged(gq) * HD**-0.5).astype(bf16)
    gk, gv = merged(gk).astype(bf16), merged(gv).astype(bf16)

    @pl.when(pl.program_id(1) == 0)
    def _():
        in_ref[...] = jnp.zeros_like(in_ref)
        if source:
            text_grad_ref[...] = jnp.zeros_like(text_grad_ref)

    if source:
        in_ref[...] += matmul(gq, q_w_ref[...])
        text_grad_ref[...] += matmul(gk, k_w_ref[...]) + matmul(gv, v_w_ref[...])
    else:
        in_ref[...] += (
            matmul(gq, q_w_ref[...]) + matmul(gk, k_w_ref[...]) + matmul(gv, v_w_ref[...])
        )
    half = mine_a.shape[-1]
    first = core_ref[0] == 0
    mine, other = (mine_a, mine_b), (other_a, other_b)
    pairs = [(mix_ref[...], back), (gq, x_ref[...]), (gk, text_ref[...]), (gv, text_ref[...])]
    for which, (left, right) in enumerate(pairs):
        whole = inner_rows(left, right).astype(bf16)
        low, high = whole[:, :half], whole[:, half:]
        mine[which // 2][which % 2] = jnp.where(first, low, high)
        other[which // 2][which % 2] = jnp.where(first, high, low)


def attend(query, keys, values, bias):
    rows, frames, tokens = bias.shape
    pairs = query.shape[1] // QUAD
    blocks = [pl.BlockSpec((n, QUAD), lambda r, h: (r, h)) for n in (frames, tokens, tokens)]
    return pl.pallas_call(
        forward_kernel,
        grid=(rows, pairs),
        in_specs=blocks + [pl.BlockSpec((1, frames, tokens), lambda r, h: (r, 0, 0))],
        out_specs=blocks[0],
        out_shape=jax.ShapeDtypeStruct(query.shape, bf16),
        compiler_params=pltpu.CompilerParams(vmem_limit_bytes=VMEM),
        cost_estimate=pl.CostEstimate(flops=0, transcendentals=0, bytes_accessed=0),
    )(query, keys, values, bias)


def attend_back(core, query, keys, values, mix, bias, weights, back, x, text=None):
    rows, tokens, frames = bias.shape
    width = query.shape[1]
    pairs, half = width // QUAD, width // 2
    wide = pl.BlockSpec((frames, QUAD), lambda r, h, c: (r, h))
    held = pl.BlockSpec((tokens, QUAD), lambda r, h, c: (r, h))
    matrix = pl.BlockSpec((QUAD, width), lambda r, h, c: (h, 0))
    frames_all = pl.BlockSpec((frames, width), lambda r, h, c: (r, 0))
    tokens_all = pl.BlockSpec((tokens, width), lambda r, h, c: (r, 0))
    grads = pl.BlockSpec((2, QUAD, half), lambda r, h, c: (0, h, 0))
    grads_shape = jax.ShapeDtypeStruct((2, width, half), bf16)
    cross = text is not None
    return pl.pallas_call(
        backward_kernel,
        grid_spec=pltpu.PrefetchScalarGridSpec(
            num_scalar_prefetch=1,
            grid=(rows, pairs),
            in_specs=[wide, held, held, wide]
            + [pl.BlockSpec((1, tokens, frames), lambda r, h, c: (r, 0, 0))]
            + [matrix] * 4
            + [frames_all] * 2
            + [tokens_all] * cross,
            out_specs=[tokens_all] * cross + [frames_all] + [grads] * 4,
        ),
        out_shape=[jax.ShapeDtypeStruct((rows * tokens, width), f32)] * cross
        + [jax.ShapeDtypeStruct(x.shape, f32)]
        + [grads_shape] * 4,
        compiler_params=pltpu.CompilerParams(vmem_limit_bytes=VMEM),
        cost_estimate=pl.CostEstimate(flops=0, transcendentals=0, bytes_accessed=0),
    )(core, query, keys, values, mix, bias, *weights, back, x, *([text] if cross else []))


def feed_kernel(
    core_ref, x_ref, g_ref, up_ref, down_ref, up_far, down_far, out_ref, back_ref, *rest
):
    *grads, xt_ref, gt_ref = rest
    slope = (2.0 / jnp.pi) ** 0.5

    @pl.when(pl.program_id(0) == 0)
    def _():
        out_ref[...] = jnp.zeros_like(out_ref)
        back_ref[...] = jnp.zeros_like(back_ref)
        xt_ref[...] = x_ref[...].T
        gt_ref[...] = g_ref[...].T

    def joined(near, far):
        first = core_ref[0] == 0
        parts = []
        for x in range(near.shape[1]):
            for y in range(near.shape[0]):
                here, there = near[y, x, 0, 0], far[y, x, 0, 0]
                parts += [jnp.where(first, here, there), jnp.where(first, there, here)]
        return jnp.concatenate(parts, axis=0)

    up, down = joined(up_ref, up_far), joined(down_ref, down_far)
    pre = outer_cols(x_ref[...], up)
    square = pre * pre
    bent = jnp.tanh(slope * pre * (1.0 + 0.044715 * square))
    rise = 0.5 * (1.0 + bent)
    active = (pre * rise).astype(bf16)
    steep = rise + 0.5 * pre * (1.0 - bent * bent) * (slope * (1.0 + 0.134145 * square))
    grad_pre = (outer_cols(g_ref[...], down) * steep).astype(bf16)
    out_ref[...] += matmul(active, down)
    back_ref[...] += matmul(grad_pre, up)
    shards, half, block = grads[0].shape
    lanes = [slice(n * block, (n + 1) * block) for n in range(shards)]
    for which, (left, right) in enumerate([(xt_ref, grad_pre), (gt_ref, active)]):
        for target, core in ((grads[which], core_ref[0]), (grads[which + 2], 1 - core_ref[0])):
            rows = left[pl.ds(pl.multiple_of(core * half, half), half), :]
            product = matmul(rows, right).astype(bf16)
            for n in range(shards):
                target[n] = product[:, lanes[n]]


def feed(core, third_in, grad_mlp, weights):
    tokens, width = third_in.shape
    ny, nx, zb, za, rows, _ = weights[0].shape
    nz = za * zb
    block, half = ny * rows * 2, width // 2
    whole = pl.BlockSpec((tokens, width), lambda j, c: (0, 0))
    parts = pl.BlockSpec((nx, half, block), lambda j, c: (j, 0, 0))
    matrix = pl.BlockSpec(
        (ny, nx, 1, 1, rows, width), lambda j, c: (0, 0, j % zb, j // zb, 0, 0)
    )
    hidden = nx * nz * block
    return pl.pallas_call(
        feed_kernel,
        grid_spec=pltpu.PrefetchScalarGridSpec(
            num_scalar_prefetch=1,
            grid=(nz,),
            in_specs=[whole] * 2 + [matrix] * 4,
            out_specs=[whole] * 2 + [parts] * 4,
            scratch_shapes=[pltpu.VMEM((width, tokens), bf16)] * 2,
        ),
        out_shape=[
            jax.ShapeDtypeStruct((tokens, width), f32),
            jax.ShapeDtypeStruct((tokens, width), f32),
        ]
        + [jax.ShapeDtypeStruct((nx * nz, half, block), bf16)] * 4,
        compiler_params=pltpu.CompilerParams(vmem_limit_bytes=VMEM),
        cost_estimate=pl.CostEstimate(flops=0, transcendentals=0, bytes_accessed=0),
    )(core, third_in, grad_mlp, *weights)


def shards(
    frames,
    seg_ids,
    text,
    text_lens,
    step_ids,
    step_table,
    ada_weight,
    ada_bias,
    query_w,
    key_w,
    value_w,
    out_w,
    cross_query_w,
    cross_key_w,
    cross_value_w,
    cross_out_w,
    up_weight,
    down_weight,
    out_grad,
):
    width = frames.shape[1]
    za, zb, nx = (lax.axis_size(axis) for axis in MP_AXES)
    mp = za * zb * nx
    position = (lax.axis_index("za") * zb + lax.axis_index("zb")) * nx + lax.axis_index("x")
    rows_dev = seg_ids.shape[0] // mp
    frames_row = seg_ids.shape[1]
    segs_dev = rows_dev * SEGS
    my_ids = lax.dynamic_slice_in_dim(seg_ids, position * rows_dev, rows_dev, 0)
    my_lens = lax.dynamic_slice_in_dim(text_lens, position * segs_dev, segs_dev, 0)

    half = width // 2
    first, more, feed_part = weight_parts(
        [
            query_w,
            key_w,
            value_w,
            out_w,
            cross_query_w,
            cross_key_w,
            cross_value_w,
            cross_out_w,
        ],
        up_weight,
        down_weight,
    )
    first = gather_axis(gather_axis(first, "za"), "zb")
    more = gather_axis(more, "za", first)
    first_left = gather_axis(first[..., :half], "x")
    first_right = gather_axis(first[..., half:], "y")
    more = gather_axis(more, "zb", first_left, first_right)
    first_left = gather_axis(first_left, "y")
    first_right = gather_axis(first_right, "x")
    feed_part = gather_axis(feed_part, "za", more)
    more_left = gather_axis(more[..., :half], "x", first_left, first_right)
    more_right = gather_axis(more[..., half:], "y", first_left, first_right)
    qkv = assemble(gather_axis(first_left, "core"), gather_axis(first_right, "core"))
    qkv = qkv.reshape(-1, width)
    feed_part = gather_axis(feed_part, "zb", more_left, more_right)

    table_low = step_table
    choose_step = (step_ids[:, None] == jnp.arange(step_table.shape[0])[None, :]).astype(bf16)
    silu_mine = jax.nn.silu(matmul(choose_step, table_low)).astype(bf16)
    partial_mod = matmul(silu_mine, ada_weight)
    partial_mod = partial_mod.reshape(za, zb, nx, segs_dev, partial_mod.shape[1])
    modulation = summed(landed(launch_wide(partial_mod, "x", 2))).astype(bf16)
    modulation = summed(landed(launch([modulation], "zb", 1))).astype(bf16)
    modulation = summed(landed(launch([modulation], "za", 0)))
    modulation = modulation + ada_bias.astype(f32)
    flat_ids = my_ids.reshape(-1)
    row_of = jnp.arange(flat_ids.shape[0]) // frames_row
    clip = flat_ids + row_of * SEGS
    chosen = clip[:, None] == jnp.arange(segs_dev)[None, :]

    def per_frame(index):
        table = modulation[:, index * width : (index + 1) * width]
        value = jnp.broadcast_to(table[0:1], (clip.shape[0], width))
        for segment in range(1, segs_dev):
            value = jnp.where(chosen[:, segment : segment + 1], table[segment : segment + 1], value)
        return value

    shift_one, scale_one, gate_one, shift_two, scale_two, gate_two = map(per_frame, range(6))

    same_seg = my_ids[:, :, None] == my_ids[:, None, :]
    self_bias = jnp.where(same_seg, 0.0, masked_score).astype(f32)
    key_segment = jnp.arange(SEGS * CAPTION) // CAPTION
    valid_key = (
        jnp.arange(CAPTION)[None, None, :] < my_lens.reshape(rows_dev, SEGS)[:, :, None]
    ).reshape(rows_dev, SEGS * CAPTION)
    allowed = (my_ids[:, :, None] == key_segment[None, None, :]) & valid_key[:, None, :]
    cross_bias = jnp.where(allowed, 0.0, masked_score).astype(f32)
    allowed_t = (my_ids[:, None, :] == key_segment[None, :, None]) & valid_key[:, :, None]
    cross_bias_t = jnp.where(allowed_t, 0.0, masked_score).astype(f32)

    base = frames.astype(f32)
    text_flat = text.reshape(-1, width)
    normed_one, inverse_one = normalize(base)
    first_in = (normed_one * (1.0 + scale_one) + shift_one).astype(bf16)
    query, keys, values = (
        outer_cols(first_in, qkv[i * width : (i + 1) * width]).astype(bf16) for i in range(3)
    )
    self_mix = attend(query, keys, values, self_bias)
    more_left = gather_axis(more_left, "y", self_mix)
    more_right = gather_axis(more_right, "x", self_mix)
    feed_up = gather_axis(feed_part[:, :, 0], "x", self_mix)
    feed_down = gather_axis(feed_part[:, :, 1], "y", self_mix)
    whole = assemble(gather_axis(more_left, "core"), gather_axis(more_right, "core"))
    out_full, cquery_t, cout_full = whole[0], whole[1], whole[4]
    ckv_t = whole[2:4].reshape(-1, width)
    self_out = matmul(self_mix, out_full)
    resid_one = base + gate_one * self_out
    normed_two, inverse_two = normalize(resid_one)
    second_in = normed_two.astype(bf16)
    cross_query = outer_cols(second_in, cquery_t).astype(bf16)
    cross_keys = outer_cols(text_flat, ckv_t[:width]).astype(bf16)
    cross_values = outer_cols(text_flat, ckv_t[width:]).astype(bf16)
    cross_mix = attend(cross_query, cross_keys, cross_values, cross_bias)
    resid_two = resid_one + matmul(cross_mix, cout_full)
    normed_three, inverse_three = normalize(resid_two)
    third_in = (normed_three * (1.0 + scale_two) + shift_two).astype(bf16)
    upstream = out_grad.astype(f32)
    grad_mlp = (gate_two * upstream).astype(bf16)
    core = lax.axis_index("core").reshape(1)
    feed_up = gather_axis(feed_up, "y", cross_mix)
    feed_down = gather_axis(feed_down, "x", cross_mix).swapaxes(0, 1)
    feed_weights = [feed_up, feed_down] + [shifted(w, "core", 1) for w in (feed_up, feed_down)]
    mlp_out, grad_third, *ff_parts = feed(core, third_in, grad_mlp, feed_weights)
    layer_out = (resid_two + gate_two * mlp_out).astype(bf16)

    grad_gate_two = upstream * mlp_out
    with jax.named_scope("feed_sums_first_stage"):
        feed_sums = first_stage(*[part[None] for part in ff_parts])
    grad_resid_two = upstream + norm_back(
        normed_three, inverse_three, grad_third * (1.0 + scale_two)
    )
    grad_cross = after(grad_resid_two.astype(bf16), *sends(feed_sums))
    grad_text, grad_second, *cross_parts = attend_back(
        core,
        cross_query,
        cross_keys,
        cross_values,
        cross_mix,
        cross_bias_t,
        [cout_full, cquery_t, ckv_t[:width], ckv_t[width:]],
        grad_cross,
        second_in,
        text_flat,
    )
    with jax.named_scope("cross_sums_first_stage"):
        cross_sums = first_stage(*cross_parts)
    with jax.named_scope("feed_sums_second_stage"):
        feed_sums = second_stage(feed_sums, grad_second)
    grad_resid_one = grad_resid_two + norm_back(normed_two, inverse_two, grad_second)
    grad_gate_one = grad_resid_one * self_out
    grad_self = after(
        (gate_one * grad_resid_one).astype(bf16), *sends(cross_sums), *sends(feed_sums)
    )
    grad_first, *self_parts = attend_back(
        core,
        query,
        keys,
        values,
        self_mix,
        self_bias,
        [out_full, qkv[:width], qkv[width : 2 * width], qkv[2 * width :]],
        grad_self,
        first_in,
    )
    with jax.named_scope("feed_sums_third_stage"):
        feed_sums = third_stage(feed_sums, grad_first)
    with jax.named_scope("self_sums_first_stage"):
        self_sums = first_stage(*self_parts, *feed_sums[1])
    with jax.named_scope("cross_sums_second_stage"):
        cross_sums = second_stage(cross_sums, *sends(self_sums))

    chooser = chosen.astype(f32)
    grad_first = after(grad_first, *sends(cross_sums))
    mod_parts = [
        grad_first,
        grad_first * normed_one,
        grad_gate_one,
        grad_third,
        grad_third * normed_three,
        grad_gate_two,
    ]
    grad_mod = jnp.stack(
        [
            lax.dot_general(chooser, v, (((0,), (0,)), ((), ())), precision=highest)
            for v in mod_parts
        ]
    ).astype(bf16)
    steps_all = after(step_ids.astype(f32), grad_mod)
    with jax.named_scope("self_sums_second_stage"):
        self_sums = second_stage(self_sums, grad_mod)
    with jax.named_scope("cross_sums_third_stage"):
        cross_sums = third_stage(cross_sums, *sends(self_sums))
    gathered = gather_axis(grad_mod, "za", *cross_sums[1])
    with jax.named_scope("self_sums_third_stage"):
        self_sums = third_stage(self_sums, gathered)
    gathered = gather_axis(gathered, "zb", *self_sums[1])
    feed_sums = fourth_stage(feed_sums, gathered)
    gathered = gather_axis(gathered, "x", *feed_sums[1])
    cross_sums = fourth_stage(cross_sums, gathered)
    self_sums = fourth_stage(self_sums, *cross_sums[1])
    feed_done = summed(landed(feed_sums, gathered)).astype(bf16)
    gathered = gather_axis(gathered, "y", feed_done)
    steps_all = gather_axis(steps_all, "y", feed_done)
    cross_done = summed(landed(cross_sums, gathered)).astype(bf16)
    gathered = gather_axis(gathered, "core", cross_done)
    steps_all = gather_axis(steps_all, "core", cross_done).transpose(1, 0, 2).reshape(-1)
    grad_mod_all = gathered.transpose(1, 0, 4, 3, 2, 6, 5, 7).reshape(-1, 6 * width)
    grad_frames = grad_resid_one + norm_back(
        normed_one, inverse_one, after(grad_first, cross_done) * (1.0 + scale_one)
    )
    self_done = summed(landed(self_sums, grad_frames)).astype(bf16)
    shard_up, shard_down = rows_whole(feed_done)
    shard_cout, shard_cquery, shard_ckey, shard_cvalue = columns_whole(cross_done)
    shard_out, shard_query, shard_key, shard_value = columns_whole(self_done)

    choose_all = (
        steps_all[:, None] == jnp.arange(step_table.shape[0]).astype(f32)[None, :]
    ).astype(bf16)
    cond_all = matmul(choose_all, table_low)
    silu_all = jax.nn.silu(cond_all).astype(bf16)
    grad_ada_w = inner_rows(silu_all, grad_mod_all)
    grad_ada_b = jnp.sum(grad_mod_all.astype(f32), axis=0)
    grad_cond = silu_back(cond_all, outer_cols(grad_mod_all, ada_weight))
    grad_table = lax.dot_general(
        choose_all.astype(f32), grad_cond, (((0,), (0,)), ((), ())), precision=highest
    )

    def columns(value):
        return value.T.astype(f32)

    return (
        layer_out,
        grad_frames,
        grad_text.reshape(text.shape),
        grad_table,
        grad_ada_w,
        grad_ada_b,
        columns(shard_query),
        columns(shard_key),
        columns(shard_value),
        shard_out.astype(f32),
        columns(shard_cquery),
        columns(shard_ckey),
        columns(shard_cvalue),
        shard_cout.astype(f32),
        shard_up.astype(f32),
        columns(shard_down),
    )


def solution(mesh):
    dp, mp = mesh.shape["dp"], mesh.shape["mp"]
    fine = Mesh(mesh.devices.reshape(dp // 2, 2, mp // 4, 2, 2), FINE)
    dp_axes, mp_axes = ("y", "core"), MP_AXES
    return jax.shard_map(
        shards,
        mesh=fine,
        in_specs=(
            P(FINE, None),
            P(dp_axes, None),
            P(FINE, None, None),
            P(dp_axes),
            P(dp_axes),
            P(None, mp_axes),
            P(mp_axes, None),
            P(),
            P(None, mp_axes),
            P(None, mp_axes),
            P(None, mp_axes),
            P(mp_axes, None),
            P(None, mp_axes),
            P(None, mp_axes),
            P(None, mp_axes),
            P(mp_axes, None),
            P(None, mp_axes),
            P(mp_axes, None),
            P(FINE, None),
        ),
        out_specs=(
            P(FINE, None),
            P(FINE, None),
            P(FINE, None, None),
            P(None, mp_axes),
            P(mp_axes, None),
            P(),
            P(None, mp_axes),
            P(None, mp_axes),
            P(None, mp_axes),
            P(mp_axes, None),
            P(None, mp_axes),
            P(None, mp_axes),
            P(None, mp_axes),
            P(mp_axes, None),
            P(None, mp_axes),
            P(mp_axes, None),
        ),
        check_vma=False,
    )
```

```python
from functools import partial

import jax
import jax.numpy as jnp
from jax import lax
from jax.experimental import pallas as pl
from jax.experimental.pallas import tpu as pltpu
from jax.sharding import Mesh, PartitionSpec as P

HEADS = 12
HD = 64
CAPTION = 77
SEGS = 4

QUAD = 4 * HD
highest = lax.Precision.HIGHEST
epsilon = 1e-06
masked_score = -1e30
bf16 = jnp.bfloat16
f32 = jnp.float32
FINE = ("y", "core", "za", "zb", "x")
MP_AXES = ("za", "zb", "x")
VMEM = 48 << 20


def shifted(value, axis, steps):
    count = lax.axis_size(axis)
    with jax.named_scope(f"to_{axis}_{steps}"):
        return lax.ppermute(value, axis, [(k, (k + steps) % count) for k in range(count)])


def gather_axis(value, axis, *hold):
    count = lax.axis_size(axis)
    me = lax.axis_index(axis)
    pieces = [shifted(value, axis, s) for s in range(1, count)]
    if hold:
        pieces = [after(piece, *hold) for piece in pieces]
    pieces = [value] + pieces

    def at(place):
        turn = (me - place) % count
        chosen = pieces[0]
        for s in range(1, count):
            chosen = jnp.where(turn == s, pieces[s], chosen)
        return chosen

    return jnp.stack([at(place) for place in range(count)])


def joined_rows(value, axis, *hold):
    return gather_axis(value, axis, *hold).reshape(-1, value.shape[-1])


def after(value, *done):
    return lax.optimization_barrier((value, *done))[0]


def picked(terms, dim, which):
    return [lax.dynamic_index_in_dim(t, which, dim, keepdims=False) for t in terms]


def summed(terms):
    total = terms[0].astype(f32)
    for term in terms[1:]:
        total = total + term.astype(f32)
    return total


def launch(terms, axis, dim):
    count = lax.axis_size(axis)
    me = lax.axis_index(axis)
    sent = [
        summed(picked(terms, dim, (me + s) % count)).astype(bf16) for s in range(1, count)
    ]
    arrived = [shifted(part, axis, s) for s, part in enumerate(sent, 1)]
    return picked(terms, dim, me), sent, arrived


def launch_wide(value, axis, dim):
    count = lax.axis_size(axis)
    me = lax.axis_index(axis)
    sent = [picked([value], dim, (me + s) % count)[0] for s in range(1, count)]
    arrived = [shifted(part, axis, s) for s, part in enumerate(sent, 1)]
    return picked([value], dim, me), sent, arrived


def landed(started, *done):
    kept, _, arrived = started
    if done:
        arrived = [after(part, *done) for part in arrived]
    return kept + arrived


def split_rows(part):
    grid = [lax.axis_size(a) for a in (*MP_AXES, "y")]
    return part.reshape(part.shape[0], *grid, -1, part.shape[-1])


def first_stage(mine_a, mine_b, other_a, other_b, *done):
    other_a, other_b = shifted(other_a, "core", 1), shifted(other_b, "core", 1)
    if done:
        other_a, other_b = after(other_a, *done), after(other_b, *done)
    left = [split_rows(mine_a), split_rows(other_a)]
    right = [split_rows(mine_b), split_rows(other_b)]
    return launch(left, "x", 3), launch(right, "y", 4)


def second_stage(stage, *done):
    left = launch(landed(stage[0], *done), "y", 3)
    right = launch(landed(stage[1], *done), "x", 3)
    return left, right


def third_stage(stage, *done):
    left, right = (summed(landed(part, *done)).astype(bf16) for part in stage)
    return launch([jnp.stack([left, right])], "zb", 3)


def fourth_stage(stage, *done):
    return launch(landed(stage, *done), "za", 2)


def sends(stage):
    return stage[0][1] + stage[1][1]


def assemble(left, right):
    left = left.transpose(5, 4, 3, 2, 1, 0, 6, 7)
    right = right.transpose(5, 4, 3, 1, 2, 0, 6, 7)
    whole = jnp.concatenate([left, right], axis=-1)
    return whole.reshape(whole.shape[0], -1, whole.shape[-1])


def parts_kernel(mine_ref, *refs):
    *sources, up_ref, down_ref, first_ref, more_ref, feed_ref, row_ref, tall_ref = refs
    rows, hidden = first_ref.shape[1], feed_ref.shape[1]

    def own(ref, count):
        return ref[pl.ds(pl.multiple_of(mine_ref[0] * count, 8), count), :].astype(bf16)

    for which, source in enumerate(sources):
        row_ref[...] = source[...].astype(f32)
        target, place = (first_ref, which) if which < 3 else (more_ref, which - 3)
        target[place] = own(row_ref, rows)
    tall_ref[...] = up_ref[...].astype(f32).T
    feed_ref[0] = own(tall_ref, hidden)
    tall_ref[...] = down_ref[...].astype(f32)
    feed_ref[1] = own(tall_ref, hidden)


def weight_parts(weights, up_weight, down_weight):
    copies = lax.axis_size("y") * lax.axis_size("core")
    mine = lax.axis_index("y") * lax.axis_size("core") + lax.axis_index("core")
    hidden, width = down_weight.shape
    shard = weights[0].shape[0]
    rows = shard // copies
    if rows % 8 or hidden // copies % 8:

        def own(value):
            part = value.shape[0] // copies
            return lax.dynamic_slice_in_dim(value, mine * part, part, 0)

        kept = [own(w) for w in weights]
        feed_part = jnp.stack([own(up_weight.T), own(down_weight)])
        return jnp.stack(kept[:3]), jnp.stack(kept[3:]), feed_part
    shapes = [
        (3, rows, width),
        (len(weights) - 3, rows, width),
        (2, hidden // copies, width),
    ]

    def whole(shape):
        return pl.BlockSpec(shape, lambda i: (0,) * len(shape))

    sources = [*weights, up_weight, down_weight]
    return pl.pallas_call(
        parts_kernel,
        grid=(1,),
        in_specs=[pl.BlockSpec(memory_space=pltpu.SMEM)] + [whole(w.shape) for w in sources],
        out_specs=[whole(shape) for shape in shapes],
        out_shape=[jax.ShapeDtypeStruct(shape, bf16) for shape in shapes],
        scratch_shapes=[pltpu.VMEM((shard, width), f32), pltpu.VMEM((hidden, width), f32)],
        compiler_params=pltpu.CompilerParams(vmem_limit_bytes=VMEM),
    )(mine.reshape(1), *sources)


def finish_kernel(me_ref, near, far_y, far_core, far_both, *refs):
    *outs, whole_ref = refs
    y, core = me_ref[0], me_ref[1]
    matrices, rows, lanes = near.shape
    deep = rows == lanes // 2

    def place(which, part, turn_y, turn_core):
        if deep:
            row = (core ^ turn_core) * 2 * rows + (y ^ turn_y) * rows
            whole_ref[pl.ds(pl.multiple_of(row, 8), rows), :] = part[which].astype(f32)
        else:
            row, lane = (y ^ turn_y) * rows, (core ^ turn_core) * lanes
            whole_ref[
                pl.ds(pl.multiple_of(row, 8), rows), pl.ds(pl.multiple_of(lane, 128), lanes)
            ] = part[which].astype(f32)

    for which, out in enumerate(outs):
        for part, turns in ((near, (0, 0)), (far_y, (1, 0)), (far_core, (0, 1)), (far_both, (1, 1))):
            place(which, part, *turns)
        out[...] = whole_ref[...] if out.shape == whole_ref.shape else whole_ref[...].T


def finish(done, shapes):
    done = done.reshape(-1, *done.shape[2:])
    deep = done.shape[1] == done.shape[2] // 2
    if lax.axis_size("y") != 2 or done.shape[1] % 8 or done.shape[2] % 128:
        done = gather_axis(gather_axis(done, "y"), "core")
        axes = (2, 0, 1, 3, 4) if deep else (2, 1, 3, 0, 4)
        done = done.transpose(axes).reshape(done.shape[2], *shapes[0])
        return [d.astype(f32) if s == shapes[0] else d.T.astype(f32) for d, s in zip(done, shapes)]
    far_y = shifted(done, "y", 1)
    far_core, far_both = shifted(done, "core", 1), shifted(far_y, "core", 1)
    me = jnp.stack([lax.axis_index("y"), lax.axis_index("core")])

    def whole(shape):
        return pl.BlockSpec(shape, lambda i: (0,) * len(shape))

    return pl.pallas_call(
        finish_kernel,
        grid=(1,),
        in_specs=[pl.BlockSpec(memory_space=pltpu.SMEM)] + [whole(done.shape)] * 4,
        out_specs=[whole(shape) for shape in shapes],
        out_shape=[jax.ShapeDtypeStruct(shape, f32) for shape in shapes],
        scratch_shapes=[pltpu.VMEM(shapes[0], f32)],
        compiler_params=pltpu.CompilerParams(vmem_limit_bytes=VMEM),
    )(me, done, far_y, far_core, far_both)


def normalize(values):
    centre = values - jnp.mean(values, axis=-1, keepdims=True)
    inverse = lax.rsqrt(jnp.mean(centre * centre, axis=-1, keepdims=True) + epsilon)
    return (centre * inverse, inverse)


def norm_back(normed, inverse, upstream):
    mean_grad = jnp.mean(upstream, axis=-1, keepdims=True)
    mean_both = jnp.mean(upstream * normed, axis=-1, keepdims=True)
    return inverse * (upstream - mean_grad - normed * mean_both)


def matmul(left, right):
    return jnp.dot(left, right, preferred_element_type=f32)


def inner_rows(left, right):
    return lax.dot_general(left, right, (((0,), (0,)), ((), ())), preferred_element_type=f32)


def outer_cols(left, right):
    return lax.dot_general(left, right, (((1,), (1,)), ((), ())), preferred_element_type=f32)


def gelu_back(pre_act, upstream):
    return jax.vjp(partial(jax.nn.gelu, approximate=True), pre_act)[1](upstream)[0]


def silu_back(inputs, upstream):
    return jax.vjp(jax.nn.silu, inputs)[1](upstream)[0]


def own_lanes(head):
    lane = lax.broadcasted_iota(jnp.int32, (1, QUAD), 1)
    return (lane >= head * HD) & (lane < (head + 1) * HD)


def merged(parts):
    whole = parts[0]
    for head in range(1, len(parts)):
        whole = jnp.where(own_lanes(head), parts[head], whole)
    return whole


def forward_kernel(q_ref, k_ref, v_ref, bias_ref, mix_ref):
    query = q_ref[...] * bf16(HD**-0.5)
    keys, values, bias = k_ref[...], v_ref[...], bias_ref[0]
    parts = []
    for head in range(QUAD // HD):
        own = jnp.where(own_lanes(head), query, bf16(0))
        scores = outer_cols(own, keys) + bias
        raised = jnp.exp(scores - jnp.max(scores, axis=1, keepdims=True))
        total = jnp.sum(raised, axis=1, keepdims=True)
        parts.append(matmul(raised.astype(bf16), values) / total)
    mix_ref[...] = merged(parts).astype(bf16)


def backward_kernel(
    core_ref,
    q_ref,
    k_ref,
    v_ref,
    mix_ref,
    bias_ref,
    out_w_ref,
    q_w_ref,
    k_w_ref,
    v_w_ref,
    back_ref,
    x_ref,
    *rest,
):
    cross = len(rest) > 5
    if cross:
        text_ref, text_grad_ref, in_ref, mine_a, mine_b, other_a, other_b = rest
    else:
        in_ref, mine_a, mine_b, other_a, other_b = rest
        text_ref = x_ref
    query = q_ref[...] * bf16(HD**-0.5)
    keys, values, bias = k_ref[...], v_ref[...], bias_ref[0]
    back = back_ref[...]
    grad = outer_cols(back, out_w_ref[...]).astype(bf16)
    gq, gk, gv = [], [], []
    for head in range(QUAD // HD):
        own = own_lanes(head)
        scores = outer_cols(keys, jnp.where(own, query, bf16(0))) + bias
        raised = jnp.exp(scores - jnp.max(scores, axis=0, keepdims=True))
        weights = raised * (1.0 / jnp.sum(raised, axis=0, keepdims=True))
        grad_weights = outer_cols(jnp.where(own, values, bf16(0)), grad)
        mean = jnp.sum(weights * grad_weights, axis=0, keepdims=True)
        grad_scores = (weights * (grad_weights - mean)).astype(bf16)
        gv.append(matmul(weights.astype(bf16), grad))
        gk.append(matmul(grad_scores, query))
        gq.append(inner_rows(grad_scores, keys))
    gq = (merged(gq) * HD**-0.5).astype(bf16)
    gk, gv = merged(gk).astype(bf16), merged(gv).astype(bf16)

    @pl.when(pl.program_id(1) == 0)
    def _():
        in_ref[...] = jnp.zeros_like(in_ref)
        if cross:
            text_grad_ref[...] = jnp.zeros_like(text_grad_ref)

    if cross:
        in_ref[...] += matmul(gq, q_w_ref[...])
        text_grad_ref[...] += matmul(gk, k_w_ref[...]) + matmul(gv, v_w_ref[...])
    else:
        in_ref[...] += (
            matmul(gq, q_w_ref[...]) + matmul(gk, k_w_ref[...]) + matmul(gv, v_w_ref[...])
        )
    half = mine_a.shape[-1]
    first = core_ref[0] == 0
    mine, other = (mine_a, mine_b), (other_a, other_b)
    pairs = [(mix_ref[...], back), (gq, x_ref[...]), (gk, text_ref[...]), (gv, text_ref[...])]
    for which, (left, right) in enumerate(pairs):
        whole = inner_rows(left, right).astype(bf16)
        low, high = whole[:, :half], whole[:, half:]
        mine[which // 2][which % 2] = jnp.where(first, low, high)
        other[which // 2][which % 2] = jnp.where(first, high, low)


def attend(query, keys, values, bias):
    rows, frames, tokens = bias.shape
    pairs = query.shape[1] // QUAD
    blocks = [pl.BlockSpec((n, QUAD), lambda r, h: (r, h)) for n in (frames, tokens, tokens)]
    return pl.pallas_call(
        forward_kernel,
        grid=(rows, pairs),
        in_specs=blocks + [pl.BlockSpec((1, frames, tokens), lambda r, h: (r, 0, 0))],
        out_specs=blocks[0],
        out_shape=jax.ShapeDtypeStruct(query.shape, bf16),
        compiler_params=pltpu.CompilerParams(vmem_limit_bytes=VMEM),
        cost_estimate=pl.CostEstimate(flops=0, transcendentals=0, bytes_accessed=0),
    )(query, keys, values, bias)


def attend_back(core, query, keys, values, mix, bias, weights, back, x, text=None):
    rows, tokens, frames = bias.shape
    width = query.shape[1]
    pairs, half = width // QUAD, width // 2
    wide = pl.BlockSpec((frames, QUAD), lambda r, h, c: (r, h))
    held = pl.BlockSpec((tokens, QUAD), lambda r, h, c: (r, h))
    matrix = pl.BlockSpec((QUAD, width), lambda r, h, c: (h, 0))
    frames_all = pl.BlockSpec((frames, width), lambda r, h, c: (r, 0))
    tokens_all = pl.BlockSpec((tokens, width), lambda r, h, c: (r, 0))
    grads = pl.BlockSpec((2, QUAD, half), lambda r, h, c: (0, h, 0))
    grads_shape = jax.ShapeDtypeStruct((2, width, half), bf16)
    cross = text is not None
    return pl.pallas_call(
        backward_kernel,
        grid_spec=pltpu.PrefetchScalarGridSpec(
            num_scalar_prefetch=1,
            grid=(rows, pairs),
            in_specs=[wide, held, held, wide]
            + [pl.BlockSpec((1, tokens, frames), lambda r, h, c: (r, 0, 0))]
            + [matrix] * 4
            + [frames_all] * 2
            + [tokens_all] * cross,
            out_specs=[tokens_all] * cross + [frames_all] + [grads] * 4,
        ),
        out_shape=[jax.ShapeDtypeStruct((rows * tokens, width), f32)] * cross
        + [jax.ShapeDtypeStruct(x.shape, f32)]
        + [grads_shape] * 4,
        compiler_params=pltpu.CompilerParams(vmem_limit_bytes=VMEM),
        cost_estimate=pl.CostEstimate(flops=0, transcendentals=0, bytes_accessed=0),
    )(core, query, keys, values, mix, bias, *weights, back, x, *([text] if cross else []))


def feed_kernel(
    core_ref, x_ref, g_ref, up_ref, down_ref, up_far, down_far, out_ref, back_ref, *rest
):
    *grads, xt_ref, gt_ref = rest
    slope = (2.0 / jnp.pi) ** 0.5

    @pl.when(pl.program_id(0) == 0)
    def _():
        out_ref[...] = jnp.zeros_like(out_ref)
        back_ref[...] = jnp.zeros_like(back_ref)
        xt_ref[...] = x_ref[...].T
        gt_ref[...] = g_ref[...].T

    def joined(near, far):
        first = core_ref[0] == 0
        parts = []
        for x in range(near.shape[1]):
            for y in range(near.shape[0]):
                here, there = near[y, x, 0, 0], far[y, x, 0, 0]
                parts += [jnp.where(first, here, there), jnp.where(first, there, here)]
        return jnp.concatenate(parts, axis=0)

    up, down = joined(up_ref, up_far), joined(down_ref, down_far)
    pre = outer_cols(x_ref[...], up)
    square = pre * pre
    bent = jnp.tanh(slope * pre * (1.0 + 0.044715 * square))
    rise = 0.5 * (1.0 + bent)
    active = (pre * rise).astype(bf16)
    steep = rise + 0.5 * pre * (1.0 - bent * bent) * (slope * (1.0 + 0.134145 * square))
    grad_pre = (outer_cols(g_ref[...], down) * steep).astype(bf16)
    out_ref[...] += matmul(active, down)
    back_ref[...] += matmul(grad_pre, up)
    shards, half, block = grads[0].shape
    lanes = [slice(n * block, (n + 1) * block) for n in range(shards)]
    for which, (left, right) in enumerate([(xt_ref, grad_pre), (gt_ref, active)]):
        for target, core in ((grads[which], core_ref[0]), (grads[which + 2], 1 - core_ref[0])):
            rows = left[pl.ds(pl.multiple_of(core * half, half), half), :]
            product = matmul(rows, right).astype(bf16)
            for n in range(shards):
                target[n] = product[:, lanes[n]]


def feed(core, third_in, grad_mlp, weights):
    tokens, width = third_in.shape
    ny, nx, zb, za, rows, _ = weights[0].shape
    nz = za * zb
    block, half = ny * rows * 2, width // 2
    whole = pl.BlockSpec((tokens, width), lambda j, c: (0, 0))
    parts = pl.BlockSpec((nx, half, block), lambda j, c: (j, 0, 0))
    matrix = pl.BlockSpec(
        (ny, nx, 1, 1, rows, width), lambda j, c: (0, 0, j % zb, j // zb, 0, 0)
    )
    hidden = nx * nz * block
    return pl.pallas_call(
        feed_kernel,
        grid_spec=pltpu.PrefetchScalarGridSpec(
            num_scalar_prefetch=1,
            grid=(nz,),
            in_specs=[whole] * 2 + [matrix] * 4,
            out_specs=[whole] * 2 + [parts] * 4,
            scratch_shapes=[pltpu.VMEM((width, tokens), bf16)] * 2,
        ),
        out_shape=[
            jax.ShapeDtypeStruct((tokens, width), f32),
            jax.ShapeDtypeStruct((tokens, width), f32),
        ]
        + [jax.ShapeDtypeStruct((nx * nz, half, block), bf16)] * 4,
        compiler_params=pltpu.CompilerParams(vmem_limit_bytes=VMEM),
        cost_estimate=pl.CostEstimate(flops=0, transcendentals=0, bytes_accessed=0),
    )(core, third_in, grad_mlp, *weights)


def shards(
    frames,
    seg_ids,
    text,
    text_lens,
    step_ids,
    step_table,
    ada_weight,
    ada_bias,
    query_w,
    key_w,
    value_w,
    out_w,
    cross_query_w,
    cross_key_w,
    cross_value_w,
    cross_out_w,
    up_weight,
    down_weight,
    out_grad,
):
    width = frames.shape[1]
    za, zb, nx = (lax.axis_size(axis) for axis in MP_AXES)
    mp = za * zb * nx
    position = (lax.axis_index("za") * zb + lax.axis_index("zb")) * nx + lax.axis_index("x")
    rows_dev = seg_ids.shape[0] // mp
    frames_row = seg_ids.shape[1]
    segs_dev = rows_dev * SEGS
    my_ids = lax.dynamic_slice_in_dim(seg_ids, position * rows_dev, rows_dev, 0)
    my_lens = lax.dynamic_slice_in_dim(text_lens, position * segs_dev, segs_dev, 0)

    half = width // 2
    first, more, feed_part = weight_parts(
        [
            query_w.T,
            key_w.T,
            value_w.T,
            out_w,
            cross_query_w.T,
            cross_key_w.T,
            cross_value_w.T,
            cross_out_w,
        ],
        up_weight,
        down_weight,
    )
    more_rows = more.shape[0] * more.shape[1]
    gathered_more = lax.all_gather(
        more.reshape(more_rows, width), (*MP_AXES, "y", "core"), axis=0, tiled=True
    )
    first_in_column = gather_axis(gather_axis(first, "za"), "zb")
    feed_part = after(feed_part, first_in_column)
    first_left = gather_axis(first_in_column[..., :half], "x")
    first_right = gather_axis(first_in_column[..., half:], "y")
    feed_part = gather_axis(feed_part, "za", first_left, first_right)
    first_left = gather_axis(first_left, "y")
    first_right = gather_axis(first_right, "x")
    feed_part = gather_axis(feed_part, "zb", first_left, first_right)
    qkv = assemble(gather_axis(first_left, "core"), gather_axis(first_right, "core"))
    qkv = qkv.reshape(-1, width)

    table_low = step_table
    step_ids = after(step_ids, first)
    choose_step = (step_ids[:, None] == jnp.arange(step_table.shape[0])[None, :]).astype(bf16)
    silu_mine = jax.nn.silu(matmul(choose_step, table_low)).astype(bf16)
    partial_mod = matmul(silu_mine, ada_weight)
    partial_mod = partial_mod.reshape(za, zb, nx, segs_dev, partial_mod.shape[1])
    modulation = summed(landed(launch_wide(partial_mod, "x", 2))).astype(bf16)
    modulation = summed(landed(launch([modulation], "zb", 1))).astype(bf16)
    modulation = summed(landed(launch([modulation], "za", 0)))
    modulation = modulation + ada_bias.astype(f32)
    flat_ids = my_ids.reshape(-1)
    row_of = jnp.arange(flat_ids.shape[0]) // frames_row
    clip = flat_ids + row_of * SEGS
    chosen = clip[:, None] == jnp.arange(segs_dev)[None, :]

    def per_frame(index):
        table = modulation[:, index * width : (index + 1) * width]
        value = jnp.broadcast_to(table[0:1], (clip.shape[0], width))
        for segment in range(1, segs_dev):
            value = jnp.where(chosen[:, segment : segment + 1], table[segment : segment + 1], value)
        return value

    shift_one, scale_one, gate_one, shift_two, scale_two, gate_two = map(per_frame, range(6))

    my_steps = lax.dynamic_slice_in_dim(step_ids, position * segs_dev, segs_dev, 0)
    digits = jnp.stack([my_steps // 256, my_steps % 256], axis=1).astype(bf16)
    digits = jnp.pad(digits, ((0, 0), (0, 126)))

    same_seg = my_ids[:, :, None] == my_ids[:, None, :]
    self_bias = jnp.where(same_seg, 0.0, masked_score).astype(f32)
    key_segment = jnp.arange(SEGS * CAPTION) % SEGS
    valid_key = (
        jnp.arange(CAPTION)[None, :, None] < my_lens.reshape(rows_dev, SEGS)[:, None, :]
    ).reshape(rows_dev, SEGS * CAPTION)
    allowed = (my_ids[:, :, None] == key_segment[None, None, :]) & valid_key[:, None, :]
    cross_bias = jnp.where(allowed, 0.0, masked_score).astype(f32)
    allowed_t = (my_ids[:, None, :] == key_segment[None, :, None]) & valid_key[:, :, None]
    cross_bias_t = jnp.where(allowed_t, 0.0, masked_score).astype(f32)
    cross_bias = after(cross_bias, cross_bias_t, digits)

    base = frames.astype(f32)
    text_flat = text.reshape(rows_dev, SEGS, CAPTION, width).swapaxes(1, 2).reshape(-1, width)
    normed_one, inverse_one = normalize(base)
    first_in = (normed_one * (1.0 + scale_one) + shift_one).astype(bf16)
    query, keys, values = (
        outer_cols(first_in, qkv[i * width : (i + 1) * width]).astype(bf16) for i in range(3)
    )
    self_mix = attend(query, keys, values, self_bias)
    feed_up = gather_axis(feed_part[:, :, 0], "x", self_mix)
    feed_down = gather_axis(feed_part[:, :, 1], "y", self_mix)
    whole = gathered_more.reshape(-1, *more.shape).swapaxes(0, 1).reshape(more.shape[0], -1, width)
    out_full, cquery_t, cout_full = whole[0], whole[1], whole[4]
    ckv_t = whole[2:4].reshape(-1, width)
    self_out = matmul(self_mix, out_full)
    resid_one = base + gate_one * self_out
    normed_two, inverse_two = normalize(resid_one)
    second_in = normed_two.astype(bf16)
    cross_query = outer_cols(second_in, cquery_t).astype(bf16)
    cross_keys = outer_cols(text_flat, ckv_t[:width]).astype(bf16)
    cross_values = outer_cols(text_flat, ckv_t[width:]).astype(bf16)
    cross_mix = attend(cross_query, cross_keys, cross_values, cross_bias)
    resid_two = resid_one + matmul(cross_mix, cout_full)
    normed_three, inverse_three = normalize(resid_two)
    third_in = (normed_three * (1.0 + scale_two) + shift_two).astype(bf16)
    upstream = out_grad.astype(f32)
    grad_mlp = (gate_two * upstream).astype(bf16)
    core = lax.axis_index("core").reshape(1)
    feed_up = gather_axis(feed_up, "y", cross_mix)
    feed_down = gather_axis(feed_down, "x", cross_mix).swapaxes(0, 1)
    feed_weights = [feed_up, feed_down] + [shifted(w, "core", 1) for w in (feed_up, feed_down)]
    mlp_out, grad_third, *ff_parts = feed(core, third_in, grad_mlp, feed_weights)
    layer_out = (resid_two + gate_two * mlp_out).astype(bf16)

    grad_gate_two = upstream * mlp_out
    with jax.named_scope("feed_sums_first_stage"):
        feed_sums = first_stage(*[part[None] for part in ff_parts])
    grad_resid_two = upstream + norm_back(
        normed_three, inverse_three, grad_third * (1.0 + scale_two)
    )
    grad_cross = after(grad_resid_two.astype(bf16), *sends(feed_sums))
    grad_text, grad_second, *cross_parts = attend_back(
        core,
        cross_query,
        cross_keys,
        cross_values,
        cross_mix,
        cross_bias_t,
        [cout_full, cquery_t, ckv_t[:width], ckv_t[width:]],
        grad_cross,
        second_in,
        text_flat,
    )
    with jax.named_scope("cross_sums_first_stage"):
        cross_sums = first_stage(*cross_parts)
    with jax.named_scope("feed_sums_second_stage"):
        feed_sums = second_stage(feed_sums, grad_second)
    grad_resid_one = grad_resid_two + norm_back(normed_two, inverse_two, grad_second)
    grad_gate_one = grad_resid_one * self_out
    grad_self = after(
        (gate_one * grad_resid_one).astype(bf16), *sends(cross_sums), *sends(feed_sums)
    )
    grad_first, *self_parts = attend_back(
        core,
        query,
        keys,
        values,
        self_mix,
        self_bias,
        [out_full, qkv[:width], qkv[width : 2 * width], qkv[2 * width :]],
        grad_self,
        first_in,
    )
    with jax.named_scope("feed_sums_third_stage"):
        feed_sums = third_stage(feed_sums, grad_first)
    with jax.named_scope("cross_sums_second_stage"):
        cross_sums = second_stage(cross_sums, grad_first)
    with jax.named_scope("self_sums_first_stage"):
        self_sums = first_stage(*self_parts, *sends(cross_sums), *feed_sums[1])

    chooser = chosen.astype(bf16)
    grad_first = after(grad_first, *sends(self_sums))
    mod_parts = [
        grad_first,
        grad_first * normed_one,
        grad_gate_one,
        grad_third,
        grad_third * normed_three,
        grad_gate_two,
    ]
    grad_mod = jnp.concatenate(
        [inner_rows(chooser, v.astype(bf16)).astype(bf16) for v in mod_parts] + [digits], axis=1
    )
    with jax.named_scope("feed_sums_fourth_stage"):
        feed_sums = fourth_stage(feed_sums, grad_mod)
    with jax.named_scope("cross_sums_third_stage"):
        cross_sums = third_stage(cross_sums, *feed_sums[1])
    with jax.named_scope("self_sums_second_stage"):
        self_sums = second_stage(self_sums, *cross_sums[1])
    with jax.named_scope("gather_mod"):
        gathered = joined_rows(grad_mod, "za", *sends(self_sums))
    with jax.named_scope("cross_sums_fourth_stage"):
        cross_sums = fourth_stage(cross_sums, gathered)
    feed_done = summed(landed(feed_sums, *cross_sums[1])).astype(bf16)
    with jax.named_scope("self_sums_third_stage"):
        self_sums = third_stage(self_sums, feed_done)
    with jax.named_scope("gather_mod"):
        gathered = joined_rows(gathered, "zb", *self_sums[1])
    cross_done = summed(landed(cross_sums, gathered)).astype(bf16)
    with jax.named_scope("self_sums_fourth_stage"):
        self_sums = fourth_stage(self_sums, cross_done)
    with jax.named_scope("gather_mod"):
        gathered = joined_rows(gathered, "x", *self_sums[1])
    grad_frames = grad_resid_one + norm_back(
        normed_one, inverse_one, after(grad_first, gathered) * (1.0 + scale_one)
    )
    with jax.named_scope("gather_mod"):
        gathered = joined_rows(gathered, "y", grad_frames)
    self_done = summed(landed(self_sums, gathered)).astype(bf16)
    with jax.named_scope("gather_mod"):
        gathered = joined_rows(gathered, "core", self_done)
    grad_mod_all = gathered[:, : 6 * width]
    digits = gathered[:, 6 * width : 6 * width + 2].astype(f32)
    steps_all = digits[:, 0] * 256.0 + digits[:, 1]
    up_shape, low_shape = up_weight.shape, out_w.shape
    shard_up, shard_down = finish(feed_done, [up_shape, down_weight.shape])
    shard_cout, shard_cquery, shard_ckey, shard_cvalue = finish(cross_done, [low_shape] * 4)
    shard_out, shard_query, shard_key, shard_value = finish(self_done, [low_shape] * 4)

    choose_all = (
        steps_all[:, None] == jnp.arange(step_table.shape[0]).astype(f32)[None, :]
    ).astype(bf16)
    cond_all = matmul(choose_all, table_low)
    silu_all = jax.nn.silu(cond_all).astype(bf16)
    grad_ada_w = inner_rows(silu_all, grad_mod_all)
    grad_ada_b = jnp.sum(grad_mod_all.astype(f32), axis=0)
    grad_cond = silu_back(cond_all, outer_cols(grad_mod_all, ada_weight))
    grad_table = lax.dot_general(
        choose_all.astype(f32), grad_cond, (((0,), (0,)), ((), ())), precision=highest
    )

    return (
        layer_out,
        grad_frames,
        grad_text.reshape(rows_dev, CAPTION, SEGS, width).swapaxes(1, 2).reshape(text.shape),
        grad_table,
        grad_ada_w,
        grad_ada_b,
        shard_query.T,
        shard_key.T,
        shard_value.T,
        shard_out,
        shard_cquery.T,
        shard_ckey.T,
        shard_cvalue.T,
        shard_cout,
        shard_up,
        shard_down,
    )


def solution(mesh):
    dp, mp = mesh.shape["dp"], mesh.shape["mp"]
    fine = Mesh(mesh.devices.reshape(dp // 2, 2, mp // 4, 2, 2), FINE)
    dp_axes, mp_axes = ("y", "core"), MP_AXES
    return jax.shard_map(
        shards,
        mesh=fine,
        in_specs=(
            P(FINE, None),
            P(dp_axes, None),
            P(FINE, None, None),
            P(dp_axes),
            P(dp_axes),
            P(None, mp_axes),
            P(mp_axes, None),
            P(),
            P(None, mp_axes),
            P(None, mp_axes),
            P(None, mp_axes),
            P(mp_axes, None),
            P(None, mp_axes),
            P(None, mp_axes),
            P(None, mp_axes),
            P(mp_axes, None),
            P(None, mp_axes),
            P(mp_axes, None),
            P(FINE, None),
        ),
        out_specs=(
            P(FINE, None),
            P(FINE, None),
            P(FINE, None, None),
            P(None, mp_axes),
            P(mp_axes, None),
            P(),
            P(None, mp_axes),
            P(None, mp_axes),
            P(None, mp_axes),
            P(mp_axes, None),
            P(None, mp_axes),
            P(None, mp_axes),
            P(None, mp_axes),
            P(mp_axes, None),
            P(None, mp_axes),
            P(mp_axes, None),
        ),
        check_vma=False,
    )
```

```python
from functools import partial

import jax
import jax.numpy as jnp
from jax import lax
from jax.experimental import pallas as pl
from jax.experimental.pallas import tpu as pltpu
from jax.sharding import Mesh, PartitionSpec as P

HEADS = 12
HD = 64
CAPTION = 77
SEGS = 4

QUAD = 4 * HD
highest = lax.Precision.HIGHEST
epsilon = 1e-06
masked_score = -1e30
bf16 = jnp.bfloat16
f32 = jnp.float32
FINE = ("y", "core", "za", "zb", "x")
MP_AXES = ("za", "zb", "x")
VMEM = 48 << 20


def shifted(value, axis, steps):
    count = lax.axis_size(axis)
    with jax.named_scope(f"to_{axis}_{steps}"):
        return lax.ppermute(value, axis, [(k, (k + steps) % count) for k in range(count)])


def gather_axis(value, axis, *hold):
    count = lax.axis_size(axis)
    me = lax.axis_index(axis)
    pieces = [shifted(value, axis, s) for s in range(1, count)]
    if hold:
        pieces = [after(piece, *hold) for piece in pieces]
    pieces = [value] + pieces

    def at(place):
        turn = (me - place) % count
        chosen = pieces[0]
        for s in range(1, count):
            chosen = jnp.where(turn == s, pieces[s], chosen)
        return chosen

    return jnp.stack([at(place) for place in range(count)])


def joined_rows(value, axis, *hold):
    return gather_axis(value, axis, *hold).reshape(-1, value.shape[-1])


def after(value, *done):
    return lax.optimization_barrier((value, *done))[0]


def picked(terms, dim, which):
    return [lax.dynamic_index_in_dim(t, which, dim, keepdims=False) for t in terms]


def summed(terms):
    total = terms[0].astype(f32)
    for term in terms[1:]:
        total = total + term.astype(f32)
    return total


def launch(terms, axis, dim):
    count = lax.axis_size(axis)
    me = lax.axis_index(axis)
    sent = [
        summed(picked(terms, dim, (me + s) % count)).astype(bf16) for s in range(1, count)
    ]
    arrived = [shifted(part, axis, s) for s, part in enumerate(sent, 1)]
    return picked(terms, dim, me), sent, arrived


def launch_wide(value, axis, dim):
    count = lax.axis_size(axis)
    me = lax.axis_index(axis)
    sent = [picked([value], dim, (me + s) % count)[0] for s in range(1, count)]
    arrived = [shifted(part, axis, s) for s, part in enumerate(sent, 1)]
    return picked([value], dim, me), sent, arrived


def landed(started, *done):
    kept, _, arrived = started
    if done:
        arrived = [after(part, *done) for part in arrived]
    return kept + arrived


def split_rows(part):
    grid = [lax.axis_size(a) for a in (*MP_AXES, "y")]
    return part.reshape(part.shape[0], *grid, -1, part.shape[-1])


def first_stage(mine_a, mine_b, other_a, other_b, *done):
    other_a, other_b = shifted(other_a, "core", 1), shifted(other_b, "core", 1)
    if done:
        other_a, other_b = after(other_a, *done), after(other_b, *done)
    left = [split_rows(mine_a), split_rows(other_a)]
    right = [split_rows(mine_b), split_rows(other_b)]
    return launch(left, "x", 3), launch(right, "y", 4)


def second_stage(stage, *done):
    left = launch(landed(stage[0], *done), "y", 3)
    right = launch(landed(stage[1], *done), "x", 3)
    return left, right


def third_stage(stage, *done):
    left, right = (summed(landed(part, *done)).astype(bf16) for part in stage)
    return launch([jnp.stack([left, right])], "zb", 3)


def fourth_stage(stage, *done):
    return launch(landed(stage, *done), "za", 2)


def sends(stage):
    return stage[0][1] + stage[1][1]


def assemble(left, right):
    left = left.transpose(5, 4, 3, 2, 1, 0, 6, 7)
    right = right.transpose(5, 4, 3, 1, 2, 0, 6, 7)
    whole = jnp.concatenate([left, right], axis=-1)
    return whole.reshape(whole.shape[0], -1, whole.shape[-1])


def rows_kernel(mine_ref, *refs):
    *sources, first_ref, more_ref, sems = refs
    rows = first_ref.shape[1]
    own = pl.ds(pl.multiple_of(mine_ref[0] * rows, 8), rows)
    copies = []
    for which, source in enumerate(sources):
        target = first_ref.at[which] if which < 3 else more_ref.at[which - 3]
        copies.append(pltpu.make_async_copy(source.at[own, :], target, sems.at[which]))
    for copy in copies:
        copy.start()
    for copy in copies:
        copy.wait()


def feed_rows_kernel(mine_ref, up_ref, down_ref, feed_ref, wide_ref, tall_ref, sems):
    rows = feed_ref.shape[1]
    own = pl.ds(pl.multiple_of(mine_ref[0] * rows, 8), rows)
    down = pltpu.make_async_copy(down_ref.at[own, :], feed_ref.at[1], sems.at[0])
    up = pltpu.make_async_copy(up_ref, wide_ref, sems.at[1])
    down.start()
    up.start()
    up.wait()
    tall_ref[...] = wide_ref[...].astype(f32).T
    down.wait()
    feed_ref[0] = tall_ref[own, :].astype(bf16)


def weight_parts(weights, up_weight, down_weight):
    copies = lax.axis_size("y") * lax.axis_size("core")
    mine = lax.axis_index("y") * lax.axis_size("core") + lax.axis_index("core")
    hidden, width = down_weight.shape
    rows = weights[0].shape[0] // copies
    if rows % 8 or hidden // copies % 8:

        def own(value):
            part = value.shape[0] // copies
            return lax.dynamic_slice_in_dim(value, mine * part, part, 0)

        kept = [own(w) for w in weights]
        feed_part = jnp.stack([own(up_weight.T), own(down_weight)])
        return jnp.stack(kept[:3]), jnp.stack(kept[3:]), feed_part
    smem, hbm = pl.BlockSpec(memory_space=pltpu.SMEM), pl.BlockSpec(memory_space=pltpu.HBM)
    vmem = pl.BlockSpec(memory_space=pltpu.VMEM)
    first, more = pl.pallas_call(
        rows_kernel,
        in_specs=[smem] + [hbm] * len(weights),
        out_specs=[vmem] * 2,
        out_shape=[
            jax.ShapeDtypeStruct((3, rows, width), bf16),
            jax.ShapeDtypeStruct((len(weights) - 3, rows, width), bf16),
        ],
        scratch_shapes=[pltpu.SemaphoreType.DMA((len(weights),))],
    )(mine.reshape(1), *weights)
    feed_part = pl.pallas_call(
        feed_rows_kernel,
        in_specs=[smem, hbm, hbm],
        out_specs=vmem,
        out_shape=jax.ShapeDtypeStruct((2, hidden // copies, width), bf16),
        scratch_shapes=[
            pltpu.VMEM((width, hidden), bf16),
            pltpu.VMEM((hidden, width), f32),
            pltpu.SemaphoreType.DMA((2,)),
        ],
    )(mine.reshape(1), up_weight, down_weight)
    return first, more, feed_part


def finish_kernel(me_ref, near, far_y, far_core, far_both, *refs):
    *outs, whole_ref = refs
    y, core = me_ref[0], me_ref[1]
    matrices, rows, lanes = near.shape
    by_rows = lanes == whole_ref.shape[1]

    def place(which, part, turn_y, turn_core):
        here_y, here_core = y ^ turn_y, core ^ turn_core
        row = (2 * here_y + here_core) * rows if by_rows else here_y * rows
        row = pl.ds(pl.multiple_of(row, 8), rows)
        if by_rows:
            whole_ref[row, :] = part[which].astype(f32)
        else:
            lane = pl.ds(pl.multiple_of(here_core * lanes, 128), lanes)
            whole_ref[row, lane] = part[which].astype(f32)

    for which, out in enumerate(outs):
        for part, turns in ((near, (0, 0)), (far_y, (1, 0)), (far_core, (0, 1)), (far_both, (1, 1))):
            place(which, part, *turns)
        out[...] = whole_ref[...] if out.shape == whole_ref.shape else whole_ref[...].T


def spread(done):
    done = done.reshape(-1, *done.shape[2:])
    far_y = shifted(done, "y", 1)
    return done, far_y, shifted(done, "core", 1), shifted(far_y, "core", 1)


def finish(quarters, rows, shapes, *hold):
    done, far_y, far_core, far_both = quarters
    by_rows = lax.axis_size("y") * lax.axis_size("core") * done.shape[1] == rows
    width = done.shape[2] if by_rows else 2 * done.shape[2]
    if lax.axis_size("y") != 2 or done.shape[1] % 8 or done.shape[2] % 128:
        done = gather_axis(gather_axis(done, "core"), "y")
        axes = (2, 0, 1, 3, 4) if by_rows else (2, 0, 3, 1, 4)
        done = done.transpose(axes).reshape(done.shape[2], rows, width)
        return [
            (d if s == (rows, width) else d.T).astype(f32) for d, s in zip(done, shapes)
        ]
    if hold:
        far_core, far_both = after(far_core, *hold), after(far_both, *hold)
    me = jnp.stack([lax.axis_index("y"), lax.axis_index("core")])

    def whole(shape):
        return pl.BlockSpec(shape, lambda i: (0,) * len(shape))

    return pl.pallas_call(
        finish_kernel,
        grid=(1,),
        in_specs=[pl.BlockSpec(memory_space=pltpu.SMEM)] + [whole(done.shape)] * 4,
        out_specs=[whole(shape) for shape in shapes],
        out_shape=[jax.ShapeDtypeStruct(shape, f32) for shape in shapes],
        scratch_shapes=[pltpu.VMEM((rows, width), f32)],
        compiler_params=pltpu.CompilerParams(vmem_limit_bytes=VMEM),
    )(me, done, far_y, far_core, far_both)


def normalize(values):
    centre = values - jnp.mean(values, axis=-1, keepdims=True)
    inverse = lax.rsqrt(jnp.mean(centre * centre, axis=-1, keepdims=True) + epsilon)
    return (centre * inverse, inverse)


def norm_back(normed, inverse, upstream):
    mean_grad = jnp.mean(upstream, axis=-1, keepdims=True)
    mean_both = jnp.mean(upstream * normed, axis=-1, keepdims=True)
    return inverse * (upstream - mean_grad - normed * mean_both)


def matmul(left, right):
    return jnp.dot(left, right, preferred_element_type=f32)


def inner_rows(left, right):
    return lax.dot_general(left, right, (((0,), (0,)), ((), ())), preferred_element_type=f32)


def outer_cols(left, right):
    return lax.dot_general(left, right, (((1,), (1,)), ((), ())), preferred_element_type=f32)


def gelu_back(pre_act, upstream):
    return jax.vjp(partial(jax.nn.gelu, approximate=True), pre_act)[1](upstream)[0]


def silu_back(inputs, upstream):
    return jax.vjp(jax.nn.silu, inputs)[1](upstream)[0]


def own_lanes(head):
    lane = lax.broadcasted_iota(jnp.int32, (1, QUAD), 1)
    return (lane >= head * HD) & (lane < (head + 1) * HD)


def merged(parts):
    whole = parts[0]
    for head in range(1, len(parts)):
        whole = jnp.where(own_lanes(head), parts[head], whole)
    return whole


def forward_kernel(q_ref, k_ref, v_ref, bias_ref, mix_ref):
    query = q_ref[...] * bf16(HD**-0.5)
    keys, values, bias = k_ref[...], v_ref[...], bias_ref[0]
    parts = []
    for head in range(QUAD // HD):
        own = jnp.where(own_lanes(head), query, bf16(0))
        scores = outer_cols(own, keys) + bias
        raised = jnp.exp(scores - jnp.max(scores, axis=1, keepdims=True))
        total = jnp.sum(raised, axis=1, keepdims=True)
        parts.append(matmul(raised.astype(bf16), values) / total)
    mix_ref[...] = merged(parts).astype(bf16)


def backward_kernel(
    core_ref,
    q_ref,
    k_ref,
    v_ref,
    mix_ref,
    bias_ref,
    out_w_ref,
    q_w_ref,
    k_w_ref,
    v_w_ref,
    back_ref,
    x_ref,
    *rest,
):
    cross = len(rest) > 5
    if cross:
        text_ref, text_grad_ref, in_ref, mine_a, mine_b, other_a, other_b = rest
    else:
        in_ref, mine_a, mine_b, other_a, other_b = rest
        text_ref = x_ref
    query = q_ref[...] * bf16(HD**-0.5)
    keys, values, bias = k_ref[...], v_ref[...], bias_ref[0]
    back = back_ref[...]
    grad = outer_cols(back, out_w_ref[...]).astype(bf16)
    gq, gk, gv = [], [], []
    for head in range(QUAD // HD):
        own = own_lanes(head)
        scores = outer_cols(keys, jnp.where(own, query, bf16(0))) + bias
        raised = jnp.exp(scores - jnp.max(scores, axis=0, keepdims=True))
        weights = raised * (1.0 / jnp.sum(raised, axis=0, keepdims=True))
        grad_weights = outer_cols(jnp.where(own, values, bf16(0)), grad)
        mean = jnp.sum(weights * grad_weights, axis=0, keepdims=True)
        grad_scores = (weights * (grad_weights - mean)).astype(bf16)
        gv.append(matmul(weights.astype(bf16), grad))
        gk.append(matmul(grad_scores, query))
        gq.append(inner_rows(grad_scores, keys))
    gq = (merged(gq) * HD**-0.5).astype(bf16)
    gk, gv = merged(gk).astype(bf16), merged(gv).astype(bf16)

    @pl.when(pl.program_id(1) == 0)
    def _():
        in_ref[...] = jnp.zeros_like(in_ref)
        if cross:
            text_grad_ref[...] = jnp.zeros_like(text_grad_ref)

    if cross:
        in_ref[...] += matmul(gq, q_w_ref[...])
        text_grad_ref[...] += matmul(gk, k_w_ref[...]) + matmul(gv, v_w_ref[...])
    else:
        in_ref[...] += (
            matmul(gq, q_w_ref[...]) + matmul(gk, k_w_ref[...]) + matmul(gv, v_w_ref[...])
        )
    half = mine_a.shape[-1]
    first = core_ref[0] == 0
    mine, other = (mine_a, mine_b), (other_a, other_b)
    pairs = [(mix_ref[...], back), (gq, x_ref[...]), (gk, text_ref[...]), (gv, text_ref[...])]
    for which, (left, right) in enumerate(pairs):
        whole = inner_rows(left, right).astype(bf16)
        low, high = whole[:, :half], whole[:, half:]
        mine[which // 2][which % 2] = jnp.where(first, low, high)
        other[which // 2][which % 2] = jnp.where(first, high, low)


def attend(query, keys, values, bias):
    rows, frames, tokens = bias.shape
    pairs = query.shape[1] // QUAD
    blocks = [pl.BlockSpec((n, QUAD), lambda r, h: (r, h)) for n in (frames, tokens, tokens)]
    return pl.pallas_call(
        forward_kernel,
        grid=(rows, pairs),
        in_specs=blocks + [pl.BlockSpec((1, frames, tokens), lambda r, h: (r, 0, 0))],
        out_specs=blocks[0],
        out_shape=jax.ShapeDtypeStruct(query.shape, bf16),
        compiler_params=pltpu.CompilerParams(vmem_limit_bytes=VMEM),
        cost_estimate=pl.CostEstimate(flops=0, transcendentals=0, bytes_accessed=0),
    )(query, keys, values, bias)


def attend_back(core, query, keys, values, mix, bias, weights, back, x, text=None):
    rows, tokens, frames = bias.shape
    width = query.shape[1]
    pairs, half = width // QUAD, width // 2
    wide = pl.BlockSpec((frames, QUAD), lambda r, h, c: (r, h))
    held = pl.BlockSpec((tokens, QUAD), lambda r, h, c: (r, h))
    matrix = pl.BlockSpec((QUAD, width), lambda r, h, c: (h, 0))
    frames_all = pl.BlockSpec((frames, width), lambda r, h, c: (r, 0))
    tokens_all = pl.BlockSpec((tokens, width), lambda r, h, c: (r, 0))
    grads = pl.BlockSpec((2, QUAD, half), lambda r, h, c: (0, h, 0))
    grads_shape = jax.ShapeDtypeStruct((2, width, half), bf16)
    cross = text is not None
    return pl.pallas_call(
        backward_kernel,
        grid_spec=pltpu.PrefetchScalarGridSpec(
            num_scalar_prefetch=1,
            grid=(rows, pairs),
            in_specs=[wide, held, held, wide]
            + [pl.BlockSpec((1, tokens, frames), lambda r, h, c: (r, 0, 0))]
            + [matrix] * 4
            + [frames_all] * 2
            + [tokens_all] * cross,
            out_specs=[tokens_all] * cross + [frames_all] + [grads] * 4,
        ),
        out_shape=[jax.ShapeDtypeStruct((rows * tokens, width), f32)] * cross
        + [jax.ShapeDtypeStruct(x.shape, f32)]
        + [grads_shape] * 4,
        compiler_params=pltpu.CompilerParams(vmem_limit_bytes=VMEM),
        cost_estimate=pl.CostEstimate(flops=0, transcendentals=0, bytes_accessed=0),
    )(core, query, keys, values, mix, bias, *weights, back, x, *([text] if cross else []))


def feed_kernel(paired, me_ref, x_ref, x_far, g_ref, g_far, *refs):
    inputs, outs = refs[: 4 if paired else 2], refs[4 if paired else 2 :]
    out_ref, back_ref, out_far, back_far, *grad_refs, out_sum, back_sum = outs
    slope = (2.0 / jnp.pi) ** 0.5
    step = pl.program_id(0)

    @pl.when(step == 0)
    def _():
        for ref in (out_ref, back_ref, out_sum, back_sum):
            ref[...] = jnp.zeros_like(ref)

    my_y, my_x = me_ref[0], me_ref[1]
    if paired:
        up_near, up_far, down_near, down_far = inputs
        (nx, zb, _, rows, _), ny = up_near.shape, 2
        up_at = lambda b, x, y: jnp.where(my_y == y, up_near[x, b, 0], up_far[x, b, 0])
        down_at = lambda b, x, y: jnp.where(my_x == x, down_near[y, b, 0], down_far[y, b, 0])
    else:
        up_ref, down_ref = inputs
        ny, nx, zb, _, rows, _ = up_ref.shape
        up_at = lambda b, x, y: up_ref[y, x, b, 0]
        down_at = lambda b, x, y: down_ref[y, x, b, 0]
    places = [(b, x, y) for b in range(zb) for x in range(nx) for y in range(ny)]
    up = jnp.concatenate([up_at(*p) for p in places], axis=0)
    down = jnp.concatenate([down_at(*p) for p in places], axis=0)
    up_parts, down_parts = [], []
    for third, grad, out, back in (
        (x_ref, g_ref, out_ref, back_ref),
        (x_far, g_far, out_sum, back_sum),
    ):
        pre = outer_cols(third[...], up)
        square = pre * pre
        bent = jnp.tanh(slope * pre * (1.0 + 0.044715 * square))
        rise = 0.5 * (1.0 + bent)
        active = (pre * rise).astype(bf16)
        steep = rise + 0.5 * pre * (1.0 - bent * bent) * (slope * (1.0 + 0.134145 * square))
        grad_pre = (outer_cols(grad[...], down) * steep).astype(bf16)
        out[...] += matmul(active, down)
        back[...] += matmul(grad_pre, up)
        up_parts.append(inner_rows(grad_pre, third[...]))
        down_parts.append(inner_rows(active, grad[...]))
    up_total = (up_parts[0] + up_parts[1]).astype(bf16)
    down_total = (down_parts[0] + down_parts[1]).astype(bf16)
    at = {p: slice(n * rows, (n + 1) * rows) for n, p in enumerate(places)}
    if paired:
        up_kept, up_sent, down_kept, down_sent = grad_refs
        for b in range(zb):
            for k in range(2):
                zero, one = up_total[at[b, 0, k]], up_total[at[b, 1, k]]
                up_kept[k, 0, b] = jnp.where(my_x == 0, zero, one)
                up_sent[k, 0, b] = jnp.where(my_x == 0, one, zero)
                zero, one = down_total[at[b, k, 0]], down_total[at[b, k, 1]]
                down_kept[k, 0, b] = jnp.where(my_y == 0, zero, one)
                down_sent[k, 0, b] = jnp.where(my_y == 0, one, zero)
    else:
        for ref, total in zip(grad_refs, (up_total, down_total)):
            for b, x, y in places:
                ref[0, b, x, y] = total[at[b, x, y]]

    @pl.when(step == pl.num_programs(0) - 1)
    def _():
        out_far[...] = out_sum[...].astype(bf16)
        back_far[...] = back_sum[...].astype(bf16)


def feed(third_in, grad_mlp, up, down):
    tokens, width = third_in.shape
    nx, zb, za, rows, _ = up.shape
    ny = lax.axis_size("y")
    paired = nx == 2 and ny == 2
    if paired:
        weights = [up, shifted(up, "y", 1), down, shifted(down, "x", 1)]
    else:
        weights = [gather_axis(up, "y"), gather_axis(down, "x").swapaxes(0, 1)]
    whole = pl.BlockSpec((tokens, width), lambda j, c: (0, 0))
    half_shape, whole_shape = (2, za, zb, rows, width), (za, zb, nx, ny, rows, width)
    grads_shape = half_shape if paired else whole_shape
    matrix_shape = (2, zb, 1, rows, width) if paired else (ny, nx, zb, 1, rows, width)
    zeros = len(matrix_shape) - 3
    matrix = pl.BlockSpec(matrix_shape, lambda j, c: (0,) * zeros + (j, 0, 0))
    if paired:
        grads = pl.BlockSpec((2, 1, zb, rows, width), lambda j, c: (0, j, 0, 0, 0))
    else:
        grads = pl.BlockSpec((1, *whole_shape[1:]), lambda j, c: (j, 0, 0, 0, 0, 0))
    count = 4 if paired else 2
    me = jnp.stack([lax.axis_index("y"), lax.axis_index("x")])
    out, back, out_far, back_far, *parts = pl.pallas_call(
        partial(feed_kernel, paired),
        grid_spec=pltpu.PrefetchScalarGridSpec(
            num_scalar_prefetch=1,
            grid=(za,),
            in_specs=[whole] * 4 + [matrix] * count,
            out_specs=[whole] * 4 + [grads] * count,
            scratch_shapes=[pltpu.VMEM((tokens, width), f32)] * 2,
        ),
        out_shape=[jax.ShapeDtypeStruct((tokens, width), f32)] * 2
        + [jax.ShapeDtypeStruct((tokens, width), bf16)] * 2
        + [jax.ShapeDtypeStruct(grads_shape, bf16)] * count,
        compiler_params=pltpu.CompilerParams(vmem_limit_bytes=56 << 20),
        cost_estimate=pl.CostEstimate(flops=0, transcendentals=0, bytes_accessed=0),
    )(me, third_in, shifted(third_in, "core", 1), grad_mlp, shifted(grad_mlp, "core", 1), *weights)
    if paired:
        up_kept, up_sent, down_kept, down_sent = parts

        def as_grid(part):
            return part.transpose(1, 2, 0, 3, 4)[None]

        sums = (
            ([as_grid(up_kept)], [], [as_grid(shifted(up_sent, "x", 1))]),
            ([as_grid(down_kept)], [], [as_grid(shifted(down_sent, "y", 1))]),
        )
    else:
        sums = launch([parts[0][None]], "x", 3), launch([parts[1][None]], "y", 4)
    out = out + shifted(out_far, "core", 1).astype(f32)
    back = back + shifted(back_far, "core", 1).astype(f32)
    return out, back, sums


def clips_kernel(clip_ref, digits_ref, first, one, resid, mixed, third, three, up, mlp, out_ref):
    clips, width = out_ref.shape[0], first.shape[1]
    row = lax.broadcasted_iota(jnp.int32, (16, 1), 0)
    chooser = (clip_ref[...] == row).astype(f32).astype(bf16)
    parts = [
        first[...],
        first[...] * one[...],
        resid[...] * mixed[...],
        third[...],
        third[...] * three[...],
        up[...].astype(f32) * mlp[...],
    ]
    for place, part in enumerate(parts):
        total = matmul(chooser, part.astype(bf16))[:clips]
        out_ref[:, place * width : (place + 1) * width] = total.astype(bf16)
    out_ref[:, len(parts) * width :] = digits_ref[...]


def clip_sums(clips, clip, digits, *values):
    width = values[0].shape[1]
    return pl.pallas_call(
        clips_kernel,
        out_shape=jax.ShapeDtypeStruct((clips, 6 * width + digits.shape[1]), bf16),
        compiler_params=pltpu.CompilerParams(vmem_limit_bytes=VMEM),
    )(clip[None, :], digits, *values)


def shards(
    frames,
    seg_ids,
    text,
    text_lens,
    step_ids,
    step_table,
    ada_weight,
    ada_bias,
    query_w,
    key_w,
    value_w,
    out_w,
    cross_query_w,
    cross_key_w,
    cross_value_w,
    cross_out_w,
    up_weight,
    down_weight,
    out_grad,
):
    width = frames.shape[1]
    za, zb, nx = (lax.axis_size(axis) for axis in MP_AXES)
    mp = za * zb * nx
    position = (lax.axis_index("za") * zb + lax.axis_index("zb")) * nx + lax.axis_index("x")
    rows_dev = seg_ids.shape[0] // mp
    frames_row = seg_ids.shape[1]
    segs_dev = rows_dev * SEGS
    my_ids = lax.dynamic_slice_in_dim(seg_ids, position * rows_dev, rows_dev, 0)
    my_lens = lax.dynamic_slice_in_dim(text_lens, position * segs_dev, segs_dev, 0)

    half = width // 2
    first, more, feed_part = weight_parts(
        [
            query_w.T,
            key_w.T,
            value_w.T,
            out_w,
            cross_query_w.T,
            cross_key_w.T,
            cross_value_w.T,
            cross_out_w,
        ],
        up_weight,
        down_weight,
    )
    column = gather_axis(first, "za")
    first_column = column
    column = gather_axis(column, "zb")
    more = gather_axis(after(more, column), "za")
    feed_part = after(feed_part, more)
    first_left = gather_axis(column[..., :half], "x")
    first_right = gather_axis(column[..., half:], "y")
    my_steps = lax.dynamic_slice_in_dim(after(step_ids, first_left, first_right), position * segs_dev, segs_dev, 0)
    digits = jnp.stack([my_steps // 256, my_steps % 256], axis=1).astype(bf16)
    digits = jnp.pad(digits, ((0, 0), (0, 126)))

    same_seg = my_ids[:, :, None] == my_ids[:, None, :]
    self_bias = jnp.where(same_seg, 0.0, masked_score).astype(f32)
    key_segment = jnp.arange(SEGS * CAPTION) % SEGS
    valid_key = (
        jnp.arange(CAPTION)[None, :, None] < my_lens.reshape(rows_dev, SEGS)[:, None, :]
    ).reshape(rows_dev, SEGS * CAPTION)
    allowed = (my_ids[:, :, None] == key_segment[None, None, :]) & valid_key[:, None, :]
    cross_bias = jnp.where(allowed, 0.0, masked_score).astype(f32)
    allowed_t = (my_ids[:, None, :] == key_segment[None, :, None]) & valid_key[:, :, None]
    cross_bias_t = jnp.where(allowed_t, 0.0, masked_score).astype(f32)

    text = after(text, first_left, first_right)
    text_flat = text.reshape(rows_dev, SEGS, CAPTION, width).swapaxes(1, 2).reshape(-1, width)
    prepared = (digits, text_flat)
    more = gather_axis(more, "zb", first_left, first_right, *prepared)
    first_left = gather_axis(first_left, "y")
    first_right = gather_axis(first_right, "x")
    feed_part = gather_axis(feed_part, "za", first_left, first_right)
    more_left = gather_axis(more[..., :half], "x", first_left, first_right)
    more_right = gather_axis(more[..., half:], "y", first_left, first_right)
    qkv = assemble(gather_axis(first_left, "core"), gather_axis(first_right, "core"))
    qkv = qkv.reshape(-1, width)
    table_low = step_table
    step_ids = after(step_ids, first)
    choose_step = (step_ids[:, None] == jnp.arange(step_table.shape[0])[None, :]).astype(bf16)
    silu_mine = jax.nn.silu(matmul(choose_step, table_low)).astype(bf16)
    partial_mod = matmul(silu_mine, ada_weight)
    partial_mod = partial_mod.reshape(za, zb, nx, segs_dev, partial_mod.shape[1])
    modulation = summed(landed(launch_wide(partial_mod, "x", 2), first_column)).astype(bf16)
    modulation = summed(landed(launch([modulation], "zb", 1), column)).astype(bf16)
    modulation = summed(landed(launch([modulation], "za", 0), first_left, first_right))
    modulation = modulation + ada_bias.astype(f32)
    flat_ids = my_ids.reshape(-1)
    row_of = jnp.arange(flat_ids.shape[0]) // frames_row
    clip = flat_ids + row_of * SEGS
    chosen = clip[:, None] == jnp.arange(segs_dev)[None, :]

    def per_frame(index):
        table = modulation[:, index * width : (index + 1) * width]
        value = jnp.broadcast_to(table[0:1], (clip.shape[0], width))
        for segment in range(1, segs_dev):
            value = jnp.where(chosen[:, segment : segment + 1], table[segment : segment + 1], value)
        return value

    shift_one, scale_one, gate_one, shift_two, scale_two, gate_two = map(per_frame, range(6))

    base = frames.astype(f32)
    normed_one, inverse_one = normalize(base)
    first_in = (normed_one * (1.0 + scale_one) + shift_one).astype(bf16)
    query, keys, values = (
        outer_cols(first_in, qkv[i * width : (i + 1) * width]).astype(bf16) for i in range(3)
    )
    self_mix = attend(query, keys, values, self_bias)
    more_left = gather_axis(more_left, "y", self_mix)
    more_right = gather_axis(more_right, "x", self_mix)
    feed_part = gather_axis(feed_part, "zb", self_mix)
    feed_up = gather_axis(feed_part[:, :, 0], "x", more_left, more_right)
    feed_down = gather_axis(feed_part[:, :, 1], "y", more_left, more_right)
    whole = assemble(gather_axis(more_left, "core"), gather_axis(more_right, "core"))
    out_full, cquery_t, cout_full = whole[0], whole[1], whole[4]
    ckv_t = whole[2:4].reshape(-1, width)
    self_out = matmul(self_mix, out_full)
    resid_one = base + gate_one * self_out
    normed_two, inverse_two = normalize(resid_one)
    second_in = normed_two.astype(bf16)
    cross_query = outer_cols(second_in, cquery_t).astype(bf16)
    cross_keys = outer_cols(text_flat, ckv_t[:width]).astype(bf16)
    cross_values = outer_cols(text_flat, ckv_t[width:]).astype(bf16)
    cross_mix = attend(cross_query, cross_keys, cross_values, cross_bias)
    resid_two = resid_one + matmul(cross_mix, cout_full)
    normed_three, inverse_three = normalize(resid_two)
    third_in = (normed_three * (1.0 + scale_two) + shift_two).astype(bf16)
    upstream = out_grad.astype(f32)
    grad_mlp = (gate_two * upstream).astype(bf16)
    core = lax.axis_index("core").reshape(1)
    mlp_out, grad_third, feed_sums = feed(third_in, grad_mlp, feed_up, feed_down)
    layer_out = (resid_two + gate_two * mlp_out).astype(bf16)

    grad_resid_two = upstream + norm_back(
        normed_three, inverse_three, grad_third * (1.0 + scale_two)
    )
    grad_cross = after(grad_resid_two.astype(bf16), *sends(feed_sums))
    grad_text, grad_second, *cross_parts = attend_back(
        core,
        cross_query,
        cross_keys,
        cross_values,
        cross_mix,
        cross_bias_t,
        [cout_full, cquery_t, ckv_t[:width], ckv_t[width:]],
        grad_cross,
        second_in,
        text_flat,
    )
    with jax.named_scope("cross_sums_first_stage"):
        cross_sums = first_stage(*cross_parts)
    with jax.named_scope("feed_sums_second_stage"):
        feed_sums = second_stage(feed_sums, grad_second)
    grad_resid_one = grad_resid_two + norm_back(normed_two, inverse_two, grad_second)
    grad_self = after(
        (gate_one * grad_resid_one).astype(bf16), *sends(cross_sums), *sends(feed_sums)
    )
    grad_first, *self_parts = attend_back(
        core,
        query,
        keys,
        values,
        self_mix,
        self_bias,
        [out_full, qkv[:width], qkv[width : 2 * width], qkv[2 * width :]],
        grad_self,
        first_in,
    )
    with jax.named_scope("feed_sums_third_stage"):
        feed_sums = third_stage(feed_sums, grad_first)
    with jax.named_scope("cross_sums_second_stage"):
        cross_sums = second_stage(cross_sums, grad_first)
    with jax.named_scope("self_sums_first_stage"):
        self_sums = first_stage(*self_parts, *sends(cross_sums), *feed_sums[1])

    grad_first = after(grad_first, *sends(self_sums))
    grad_mod = clip_sums(
        segs_dev,
        clip,
        digits,
        grad_first,
        normed_one,
        grad_resid_one,
        self_out,
        grad_third,
        normed_three,
        out_grad,
        mlp_out,
    )
    with jax.named_scope("feed_sums_fourth_stage"):
        feed_sums = fourth_stage(feed_sums, grad_mod)
    with jax.named_scope("cross_sums_third_stage"):
        cross_sums = third_stage(cross_sums, *feed_sums[1])
    with jax.named_scope("self_sums_second_stage"):
        self_sums = second_stage(self_sums, *cross_sums[1])
    with jax.named_scope("gather_mod"):
        gathered = joined_rows(grad_mod, "za", *sends(self_sums))
    with jax.named_scope("cross_sums_fourth_stage"):
        cross_sums = fourth_stage(cross_sums, gathered)
    feed_done = summed(landed(feed_sums, *cross_sums[1])).astype(bf16)
    with jax.named_scope("feed_spread"):
        feed_quarters = spread(feed_done)
    with jax.named_scope("self_sums_third_stage"):
        self_sums = third_stage(self_sums, feed_done)
    with jax.named_scope("gather_mod"):
        gathered = joined_rows(gathered, "zb", *self_sums[1])
    cross_done = summed(landed(cross_sums, gathered)).astype(bf16)
    with jax.named_scope("self_sums_fourth_stage"):
        self_sums = fourth_stage(self_sums, cross_done, feed_quarters[1])
    with jax.named_scope("cross_spread"):
        cross_quarters = spread(cross_done)
    with jax.named_scope("gather_mod"):
        gathered = joined_rows(gathered, "x", *self_sums[1])
    grad_frames = grad_resid_one + norm_back(
        normed_one, inverse_one, after(grad_first, gathered) * (1.0 + scale_one)
    )
    with jax.named_scope("gather_mod"):
        gathered = joined_rows(gathered, "y", grad_frames)
    self_done = summed(landed(self_sums, gathered, cross_quarters[1])).astype(bf16)
    with jax.named_scope("self_spread"):
        self_quarters = spread(self_done)
    with jax.named_scope("gather_mod"):
        gathered = joined_rows(gathered, "core", self_done)
    grad_mod_all = gathered[:, : 6 * width]
    digits = gathered[:, 6 * width : 6 * width + 2].astype(f32)
    steps_all = digits[:, 0] * 256.0 + digits[:, 1]
    choose_all = (
        steps_all[:, None] == jnp.arange(step_table.shape[0]).astype(f32)[None, :]
    ).astype(bf16)
    cond_all = matmul(choose_all, table_low)
    silu_all = jax.nn.silu(cond_all).astype(bf16)
    grad_ada_w = inner_rows(silu_all, grad_mod_all)
    grad_ada_b = jnp.sum(grad_mod_all.astype(f32), axis=0)
    grad_cond = silu_back(cond_all, outer_cols(grad_mod_all, ada_weight))
    grad_table = lax.dot_general(
        choose_all.astype(f32), grad_cond, (((0,), (0,)), ((), ())), precision=highest
    )

    hidden, low = down_weight.shape[0], out_w.shape[0]
    made = (grad_ada_w, grad_table)
    shard_up, shard_down = finish(feed_quarters, hidden, [up_weight.shape, down_weight.shape])
    shard_cout, shard_cquery, shard_ckey, shard_cvalue = finish(
        cross_quarters, low, [out_w.shape] * 4
    )
    shard_out, shard_query, shard_key, shard_value = finish(
        self_quarters, low, [out_w.shape] * 4, *made, shard_up, shard_cout
    )

    return (
        layer_out,
        grad_frames,
        grad_text.reshape(rows_dev, CAPTION, SEGS, width).swapaxes(1, 2).reshape(text.shape),
        grad_table,
        grad_ada_w,
        grad_ada_b,
        shard_query.T,
        shard_key.T,
        shard_value.T,
        shard_out,
        shard_cquery.T,
        shard_ckey.T,
        shard_cvalue.T,
        shard_cout,
        shard_up,
        shard_down,
    )


def solution(mesh):
    dp, mp = mesh.shape["dp"], mesh.shape["mp"]
    fine = Mesh(mesh.devices.reshape(dp // 2, 2, mp // 4, 2, 2), FINE)
    dp_axes, mp_axes = ("y", "core"), MP_AXES
    return jax.shard_map(
        shards,
        mesh=fine,
        in_specs=(
            P(FINE, None),
            P(dp_axes, None),
            P(FINE, None, None),
            P(dp_axes),
            P(dp_axes),
            P(None, mp_axes),
            P(mp_axes, None),
            P(),
            P(None, mp_axes),
            P(None, mp_axes),
            P(None, mp_axes),
            P(mp_axes, None),
            P(None, mp_axes),
            P(None, mp_axes),
            P(None, mp_axes),
            P(mp_axes, None),
            P(None, mp_axes),
            P(mp_axes, None),
            P(FINE, None),
        ),
        out_specs=(
            P(FINE, None),
            P(FINE, None),
            P(FINE, None, None),
            P(None, mp_axes),
            P(mp_axes, None),
            P(),
            P(None, mp_axes),
            P(None, mp_axes),
            P(None, mp_axes),
            P(mp_axes, None),
            P(None, mp_axes),
            P(None, mp_axes),
            P(None, mp_axes),
            P(mp_axes, None),
            P(None, mp_axes),
            P(mp_axes, None),
        ),
        check_vma=False,
    )
```

```python
from functools import partial

import jax
import jax.numpy as jnp
from jax import lax
from jax.experimental import pallas as pl
from jax.experimental.pallas import tpu as pltpu
from jax.sharding import Mesh, PartitionSpec as P

HEADS = 12
HD = 64
CAPTION = 77
SEGS = 4

QUAD = 4 * HD
highest = lax.Precision.HIGHEST
epsilon = 1e-06
masked_score = -1e30
bf16 = jnp.bfloat16
f32 = jnp.float32
FINE = ("y", "core", "za", "zb", "x")
MP_AXES = ("za", "zb", "x")
VMEM = 48 << 20


def shifted(value, axis, steps):
    count = lax.axis_size(axis)
    with jax.named_scope(f"to_{axis}_{steps}"):
        return lax.ppermute(value, axis, [(k, (k + steps) % count) for k in range(count)])


def gather_axis(value, axis, *hold):
    count = lax.axis_size(axis)
    me = lax.axis_index(axis)
    pieces = [shifted(value, axis, s) for s in range(1, count)]
    if hold:
        pieces = [after(piece, *hold) for piece in pieces]
    pieces = [value] + pieces

    def at(place):
        turn = (me - place) % count
        chosen = pieces[0]
        for s in range(1, count):
            chosen = jnp.where(turn == s, pieces[s], chosen)
        return chosen

    return jnp.stack([at(place) for place in range(count)])


def joined_rows(value, axis, *hold):
    return gather_axis(value, axis, *hold).reshape(-1, value.shape[-1])


def after(value, *done):
    return lax.optimization_barrier((value, *done))[0]


def picked(terms, dim, which):
    return [lax.dynamic_index_in_dim(t, which, dim, keepdims=False) for t in terms]


def summed(terms):
    total = terms[0].astype(f32)
    for term in terms[1:]:
        total = total + term.astype(f32)
    return total


def launch(terms, axis, dim):
    count = lax.axis_size(axis)
    me = lax.axis_index(axis)
    sent = [
        summed(picked(terms, dim, (me + s) % count)).astype(bf16) for s in range(1, count)
    ]
    arrived = [shifted(part, axis, s) for s, part in enumerate(sent, 1)]
    return picked(terms, dim, me), sent, arrived


def launch_wide(value, axis, dim):
    count = lax.axis_size(axis)
    me = lax.axis_index(axis)
    sent = [picked([value], dim, (me + s) % count)[0] for s in range(1, count)]
    arrived = [shifted(part, axis, s) for s, part in enumerate(sent, 1)]
    return picked([value], dim, me), sent, arrived


def landed(started, *done):
    kept, _, arrived = started
    if done:
        arrived = [after(part, *done) for part in arrived]
    return kept + arrived


def split_rows(part):
    grid = [lax.axis_size(a) for a in (*MP_AXES, "y")]
    return part.reshape(part.shape[0], *grid, -1, part.shape[-1])


def first_stage(mine_a, mine_b, other_a, other_b, *done):
    other_a, other_b = shifted(other_a, "core", 1), shifted(other_b, "core", 1)
    if done:
        other_a, other_b = after(other_a, *done), after(other_b, *done)
    left = [split_rows(mine_a), split_rows(other_a)]
    right = [split_rows(mine_b), split_rows(other_b)]
    return launch(left, "x", 3), launch(right, "y", 4)


def second_stage(stage, *done):
    left = launch(landed(stage[0], *done), "y", 3)
    right = launch(landed(stage[1], *done), "x", 3)
    return left, right


def third_stage(stage, *done):
    left, right = (summed(landed(part, *done)).astype(bf16) for part in stage)
    return launch([jnp.stack([left, right])], "zb", 3)


def fourth_stage(stage, *done):
    return launch(landed(stage, *done), "za", 2)


def sends(stage):
    return stage[0][1] + stage[1][1]


def assemble(left, right):
    left = left.transpose(5, 4, 3, 2, 1, 0, 6, 7)
    right = right.transpose(5, 4, 3, 1, 2, 0, 6, 7)
    whole = jnp.concatenate([left, right], axis=-1)
    return whole.reshape(whole.shape[0], -1, whole.shape[-1])


def rows_kernel(mine_ref, *refs):
    *sources, first_ref, more_ref, sems = refs
    rows = first_ref.shape[1]
    own = pl.ds(pl.multiple_of(mine_ref[0] * rows, 8), rows)
    copies = []
    for which, source in enumerate(sources):
        target = first_ref.at[which] if which < 3 else more_ref.at[which - 3]
        copies.append(pltpu.make_async_copy(source.at[own, :], target, sems.at[which]))
    for copy in copies:
        copy.start()
    for copy in copies:
        copy.wait()


def feed_rows_kernel(mine_ref, up_ref, down_ref, feed_ref, wide_ref, tall_ref, sems):
    rows = feed_ref.shape[1]
    own = pl.ds(pl.multiple_of(mine_ref[0] * rows, 8), rows)
    down = pltpu.make_async_copy(down_ref.at[own, :], feed_ref.at[1], sems.at[0])
    up = pltpu.make_async_copy(up_ref, wide_ref, sems.at[1])
    down.start()
    up.start()
    up.wait()
    tall_ref[...] = wide_ref[...].astype(f32).T
    down.wait()
    feed_ref[0] = tall_ref[own, :].astype(bf16)


def own_rows(value, mine):
    part = value.shape[0] // (lax.axis_size("y") * lax.axis_size("core"))
    return lax.dynamic_slice_in_dim(value, mine * part, part, 0)


def weight_parts(weights):
    copies = lax.axis_size("y") * lax.axis_size("core")
    mine = lax.axis_index("y") * lax.axis_size("core") + lax.axis_index("core")
    width, rows = weights[0].shape[1], weights[0].shape[0] // copies
    if rows % 8:
        kept = [own_rows(w, mine) for w in weights]
        return jnp.stack(kept[:3]), jnp.stack(kept[3:])
    smem, hbm = pl.BlockSpec(memory_space=pltpu.SMEM), pl.BlockSpec(memory_space=pltpu.HBM)
    vmem = pl.BlockSpec(memory_space=pltpu.VMEM)
    return pl.pallas_call(
        rows_kernel,
        in_specs=[smem] + [hbm] * len(weights),
        out_specs=[vmem] * 2,
        out_shape=[
            jax.ShapeDtypeStruct((3, rows, width), bf16),
            jax.ShapeDtypeStruct((len(weights) - 3, rows, width), bf16),
        ],
        scratch_shapes=[pltpu.SemaphoreType.DMA((len(weights),))],
    )(mine.reshape(1), *weights)


def feed_parts(up_weight, down_weight, *done):
    copies = lax.axis_size("y") * lax.axis_size("core")
    mine = lax.axis_index("y") * lax.axis_size("core") + lax.axis_index("core")
    mine = after(mine, *done)
    hidden, width = down_weight.shape
    if hidden // copies % 8:
        return jnp.stack([own_rows(up_weight.T, mine), own_rows(down_weight, mine)])
    smem, hbm = pl.BlockSpec(memory_space=pltpu.SMEM), pl.BlockSpec(memory_space=pltpu.HBM)
    vmem = pl.BlockSpec(memory_space=pltpu.VMEM)
    return pl.pallas_call(
        feed_rows_kernel,
        in_specs=[smem, hbm, hbm],
        out_specs=vmem,
        out_shape=jax.ShapeDtypeStruct((2, hidden // copies, width), bf16),
        scratch_shapes=[
            pltpu.VMEM((width, hidden), bf16),
            pltpu.VMEM((hidden, width), f32),
            pltpu.SemaphoreType.DMA((2,)),
        ],
    )(mine.reshape(1), up_weight, down_weight)


def finish_kernel(me_ref, near, far_y, far_core, far_both, *refs):
    *outs, whole_ref = refs
    y, core = me_ref[0], me_ref[1]
    matrices, rows, lanes = near.shape
    by_rows = lanes == whole_ref.shape[1]

    def place(which, part, turn_y, turn_core):
        here_y, here_core = y ^ turn_y, core ^ turn_core
        row = (2 * here_y + here_core) * rows if by_rows else here_y * rows
        row = pl.ds(pl.multiple_of(row, 8), rows)
        if by_rows:
            whole_ref[row, :] = part[which].astype(f32)
        else:
            lane = pl.ds(pl.multiple_of(here_core * lanes, 128), lanes)
            whole_ref[row, lane] = part[which].astype(f32)

    for which, out in enumerate(outs):
        for part, turns in ((near, (0, 0)), (far_y, (1, 0)), (far_core, (0, 1)), (far_both, (1, 1))):
            place(which, part, *turns)
        out[...] = whole_ref[...] if out.shape == whole_ref.shape else whole_ref[...].T


def spread(done, *hold):
    done = done.reshape(-1, *done.shape[2:])
    far_y = shifted(done, "y", 1)
    if hold:
        far_y = after(far_y, *hold)
    return done, far_y, shifted(done, "core", 1), shifted(far_y, "core", 1)


def finish(quarters, rows, shapes, *hold):
    done, far_y, far_core, far_both = quarters
    by_rows = lax.axis_size("y") * lax.axis_size("core") * done.shape[1] == rows
    width = done.shape[2] if by_rows else 2 * done.shape[2]
    if lax.axis_size("y") != 2 or done.shape[1] % 8 or done.shape[2] % 128:
        done = gather_axis(gather_axis(done, "core"), "y")
        axes = (2, 0, 1, 3, 4) if by_rows else (2, 0, 3, 1, 4)
        done = done.transpose(axes).reshape(done.shape[2], rows, width)
        return [
            (d if s == (rows, width) else d.T).astype(f32) for d, s in zip(done, shapes)
        ]
    if hold:
        far_core, far_both = after(far_core, *hold), after(far_both, *hold)
    me = jnp.stack([lax.axis_index("y"), lax.axis_index("core")])

    def whole(shape):
        return pl.BlockSpec(shape, lambda i: (0,) * len(shape))

    return pl.pallas_call(
        finish_kernel,
        grid=(1,),
        in_specs=[pl.BlockSpec(memory_space=pltpu.SMEM)] + [whole(done.shape)] * 4,
        out_specs=[whole(shape) for shape in shapes],
        out_shape=[jax.ShapeDtypeStruct(shape, f32) for shape in shapes],
        scratch_shapes=[pltpu.VMEM((rows, width), f32)],
        compiler_params=pltpu.CompilerParams(vmem_limit_bytes=VMEM),
    )(me, done, far_y, far_core, far_both)


def normalize(values):
    centre = values - jnp.mean(values, axis=-1, keepdims=True)
    inverse = lax.rsqrt(jnp.mean(centre * centre, axis=-1, keepdims=True) + epsilon)
    return (centre * inverse, inverse)


def norm_back(normed, inverse, upstream):
    mean_grad = jnp.mean(upstream, axis=-1, keepdims=True)
    mean_both = jnp.mean(upstream * normed, axis=-1, keepdims=True)
    return inverse * (upstream - mean_grad - normed * mean_both)


def matmul(left, right):
    return jnp.dot(left, right, preferred_element_type=f32)


def inner_rows(left, right):
    return lax.dot_general(left, right, (((0,), (0,)), ((), ())), preferred_element_type=f32)


def outer_cols(left, right):
    return lax.dot_general(left, right, (((1,), (1,)), ((), ())), preferred_element_type=f32)


def gelu_back(pre_act, upstream):
    return jax.vjp(partial(jax.nn.gelu, approximate=True), pre_act)[1](upstream)[0]


def silu_back(inputs, upstream):
    return jax.vjp(jax.nn.silu, inputs)[1](upstream)[0]


def own_lanes(head):
    lane = lax.broadcasted_iota(jnp.int32, (1, QUAD), 1)
    return (lane >= head * HD) & (lane < (head + 1) * HD)


def merged(parts):
    whole = parts[0]
    for head in range(1, len(parts)):
        whole = jnp.where(own_lanes(head), parts[head], whole)
    return whole


def forward_kernel(q_ref, k_ref, v_ref, bias_ref, mix_ref):
    query = q_ref[...] * bf16(HD**-0.5)
    keys, values, bias = k_ref[...], v_ref[...], bias_ref[0]
    parts = []
    for head in range(QUAD // HD):
        own = jnp.where(own_lanes(head), query, bf16(0))
        scores = outer_cols(own, keys) + bias
        raised = jnp.exp(scores - jnp.max(scores, axis=1, keepdims=True))
        total = jnp.sum(raised, axis=1, keepdims=True)
        parts.append(matmul(raised.astype(bf16), values) / total)
    mix_ref[...] = merged(parts).astype(bf16)


def backward_kernel(
    core_ref,
    q_ref,
    k_ref,
    v_ref,
    mix_ref,
    bias_ref,
    out_w_ref,
    q_w_ref,
    k_w_ref,
    v_w_ref,
    back_ref,
    x_ref,
    *rest,
):
    cross = len(rest) > 5
    if cross:
        text_ref, text_grad_ref, in_ref, mine_a, mine_b, other_a, other_b = rest
    else:
        in_ref, mine_a, mine_b, other_a, other_b = rest
        text_ref = x_ref
    query = q_ref[...] * bf16(HD**-0.5)
    keys, values, bias = k_ref[...], v_ref[...], bias_ref[0]
    back = back_ref[...]
    grad = outer_cols(back, out_w_ref[...]).astype(bf16)
    gq, gk, gv = [], [], []
    for head in range(QUAD // HD):
        own = own_lanes(head)
        scores = outer_cols(keys, jnp.where(own, query, bf16(0))) + bias
        raised = jnp.exp(scores - jnp.max(scores, axis=0, keepdims=True))
        weights = raised * (1.0 / jnp.sum(raised, axis=0, keepdims=True))
        grad_weights = outer_cols(jnp.where(own, values, bf16(0)), grad)
        mean = jnp.sum(weights * grad_weights, axis=0, keepdims=True)
        grad_scores = (weights * (grad_weights - mean)).astype(bf16)
        gv.append(matmul(weights.astype(bf16), grad))
        gk.append(matmul(grad_scores, query))
        gq.append(inner_rows(grad_scores, keys))
    gq = (merged(gq) * HD**-0.5).astype(bf16)
    gk, gv = merged(gk).astype(bf16), merged(gv).astype(bf16)

    @pl.when(pl.program_id(1) == 0)
    def _():
        in_ref[...] = jnp.zeros_like(in_ref)
        if cross:
            text_grad_ref[...] = jnp.zeros_like(text_grad_ref)

    if cross:
        in_ref[...] += matmul(gq, q_w_ref[...])
        text_grad_ref[...] += matmul(gk, k_w_ref[...]) + matmul(gv, v_w_ref[...])
    else:
        in_ref[...] += (
            matmul(gq, q_w_ref[...]) + matmul(gk, k_w_ref[...]) + matmul(gv, v_w_ref[...])
        )
    half = mine_a.shape[-1]
    first = core_ref[0] == 0
    mine, other = (mine_a, mine_b), (other_a, other_b)
    pairs = [(mix_ref[...], back), (gq, x_ref[...]), (gk, text_ref[...]), (gv, text_ref[...])]
    for which, (left, right) in enumerate(pairs):
        whole = inner_rows(left, right).astype(bf16)
        low, high = whole[:, :half], whole[:, half:]
        mine[which // 2][which % 2] = jnp.where(first, low, high)
        other[which // 2][which % 2] = jnp.where(first, high, low)


def attend(query, keys, values, bias):
    rows, frames, tokens = bias.shape
    pairs = query.shape[1] // QUAD
    blocks = [pl.BlockSpec((n, QUAD), lambda r, h: (r, h)) for n in (frames, tokens, tokens)]
    return pl.pallas_call(
        forward_kernel,
        grid=(rows, pairs),
        in_specs=blocks + [pl.BlockSpec((1, frames, tokens), lambda r, h: (r, 0, 0))],
        out_specs=blocks[0],
        out_shape=jax.ShapeDtypeStruct(query.shape, bf16),
        compiler_params=pltpu.CompilerParams(vmem_limit_bytes=VMEM),
        cost_estimate=pl.CostEstimate(flops=0, transcendentals=0, bytes_accessed=0),
    )(query, keys, values, bias)


def attend_back(core, query, keys, values, mix, bias, weights, back, x, text=None):
    rows, tokens, frames = bias.shape
    width = query.shape[1]
    pairs, half = width // QUAD, width // 2
    wide = pl.BlockSpec((frames, QUAD), lambda r, h, c: (r, h))
    held = pl.BlockSpec((tokens, QUAD), lambda r, h, c: (r, h))
    matrix = pl.BlockSpec((QUAD, width), lambda r, h, c: (h, 0))
    frames_all = pl.BlockSpec((frames, width), lambda r, h, c: (r, 0))
    tokens_all = pl.BlockSpec((tokens, width), lambda r, h, c: (r, 0))
    grads = pl.BlockSpec((2, QUAD, half), lambda r, h, c: (0, h, 0))
    grads_shape = jax.ShapeDtypeStruct((2, width, half), bf16)
    cross = text is not None
    return pl.pallas_call(
        backward_kernel,
        grid_spec=pltpu.PrefetchScalarGridSpec(
            num_scalar_prefetch=1,
            grid=(rows, pairs),
            in_specs=[wide, held, held, wide]
            + [pl.BlockSpec((1, tokens, frames), lambda r, h, c: (r, 0, 0))]
            + [matrix] * 4
            + [frames_all] * 2
            + [tokens_all] * cross,
            out_specs=[tokens_all] * cross + [frames_all] + [grads] * 4,
        ),
        out_shape=[jax.ShapeDtypeStruct((rows * tokens, width), f32)] * cross
        + [jax.ShapeDtypeStruct(x.shape, f32)]
        + [grads_shape] * 4,
        compiler_params=pltpu.CompilerParams(vmem_limit_bytes=VMEM),
        cost_estimate=pl.CostEstimate(flops=0, transcendentals=0, bytes_accessed=0),
    )(core, query, keys, values, mix, bias, *weights, back, x, *([text] if cross else []))


def feed_kernel(paired, me_ref, x_ref, x_far, g_ref, g_far, *refs):
    inputs, outs = refs[: 4 if paired else 2], refs[4 if paired else 2 :]
    out_ref, back_ref, out_far, back_far, *grad_refs = outs[:-6]
    out_sum, back_sum, third_both, grad_both, active_both, pre_both = outs[-6:]
    tokens = x_ref.shape[0]
    slope = (2.0 / jnp.pi) ** 0.5
    step = pl.program_id(0)

    @pl.when(step == 0)
    def _():
        for ref in (out_ref, back_ref, out_sum, back_sum):
            ref[...] = jnp.zeros_like(ref)
        third_both[:tokens], third_both[tokens:] = x_ref[...], x_far[...]
        grad_both[:tokens], grad_both[tokens:] = g_ref[...], g_far[...]

    my_y, my_x = me_ref[0], me_ref[1]
    if paired:
        up_near, up_far, down_near, down_far = inputs
        (nx, zb, _, rows, _), ny = up_near.shape, 2
        up_at = lambda b, x, y: jnp.where(my_y == y, up_near[x, b, 0], up_far[x, b, 0])
        down_at = lambda b, x, y: jnp.where(my_x == x, down_near[y, b, 0], down_far[y, b, 0])
    else:
        up_ref, down_ref = inputs
        ny, nx, zb, _, rows, _ = up_ref.shape
        up_at = lambda b, x, y: up_ref[y, x, b, 0]
        down_at = lambda b, x, y: down_ref[y, x, b, 0]
    places = [(b, x, y) for b in range(zb) for x in range(nx) for y in range(ny)]
    up = jnp.concatenate([up_at(*p) for p in places], axis=0)
    down = jnp.concatenate([down_at(*p) for p in places], axis=0)
    for which, (out, back) in enumerate(((out_ref, back_ref), (out_sum, back_sum))):
        here = slice(which * tokens, (which + 1) * tokens)
        pre = outer_cols(third_both[here], up)
        square = pre * pre
        rise = 0.5 + 0.5 * jnp.tanh(pre * (slope + (0.044715 * slope) * square))
        active = pre * rise
        steep = rise + active * (1.0 - rise) * (2.0 * slope + (0.26829 * slope) * square)
        active = active.astype(bf16)
        grad_pre = (outer_cols(grad_both[here], down) * steep).astype(bf16)
        out[...] += matmul(active, down)
        back[...] += matmul(grad_pre, up)
        active_both[here] = active
        pre_both[here] = grad_pre
    up_total = inner_rows(pre_both[...], third_both[...]).astype(bf16)
    down_total = inner_rows(active_both[...], grad_both[...]).astype(bf16)
    at = {p: slice(n * rows, (n + 1) * rows) for n, p in enumerate(places)}
    if paired:
        up_kept, up_sent, down_kept, down_sent = grad_refs
        for b in range(zb):
            for k in range(2):
                zero, one = up_total[at[b, 0, k]], up_total[at[b, 1, k]]
                up_kept[k, 0, b] = jnp.where(my_x == 0, zero, one)
                up_sent[k, 0, b] = jnp.where(my_x == 0, one, zero)
                zero, one = down_total[at[b, k, 0]], down_total[at[b, k, 1]]
                down_kept[k, 0, b] = jnp.where(my_y == 0, zero, one)
                down_sent[k, 0, b] = jnp.where(my_y == 0, one, zero)
    else:
        for ref, total in zip(grad_refs, (up_total, down_total)):
            for b, x, y in places:
                ref[0, b, x, y] = total[at[b, x, y]]

    @pl.when(step == pl.num_programs(0) - 1)
    def _():
        out_far[...] = out_sum[...].astype(bf16)
        back_far[...] = back_sum[...].astype(bf16)


def feed(third_in, grad_mlp, up, down):
    tokens, width = third_in.shape
    nx, zb, za, rows, _ = up.shape
    ny = lax.axis_size("y")
    paired = nx == 2 and ny == 2
    if paired:
        weights = [up, shifted(up, "y", 1), down, shifted(down, "x", 1)]
    else:
        weights = [gather_axis(up, "y"), gather_axis(down, "x").swapaxes(0, 1)]
    whole = pl.BlockSpec((tokens, width), lambda j, c: (0, 0))
    half_shape, whole_shape = (2, za, zb, rows, width), (za, zb, nx, ny, rows, width)
    grads_shape = half_shape if paired else whole_shape
    matrix_shape = (2, zb, 1, rows, width) if paired else (ny, nx, zb, 1, rows, width)
    zeros = len(matrix_shape) - 3
    matrix = pl.BlockSpec(matrix_shape, lambda j, c: (0,) * zeros + (j, 0, 0))
    if paired:
        grads = pl.BlockSpec((2, 1, zb, rows, width), lambda j, c: (0, j, 0, 0, 0))
    else:
        grads = pl.BlockSpec((1, *whole_shape[1:]), lambda j, c: (j, 0, 0, 0, 0, 0))
    count = 4 if paired else 2
    me = jnp.stack([lax.axis_index("y"), lax.axis_index("x")])
    out, back, out_far, back_far, *parts = pl.pallas_call(
        partial(feed_kernel, paired),
        grid_spec=pltpu.PrefetchScalarGridSpec(
            num_scalar_prefetch=1,
            grid=(za,),
            in_specs=[whole] * 4 + [matrix] * count,
            out_specs=[whole] * 4 + [grads] * count,
            scratch_shapes=[pltpu.VMEM((tokens, width), f32)] * 2
            + [pltpu.VMEM((2 * tokens, width), bf16)] * 2
            + [pltpu.VMEM((2 * tokens, zb * nx * ny * rows), bf16)] * 2,
        ),
        out_shape=[jax.ShapeDtypeStruct((tokens, width), f32)] * 2
        + [jax.ShapeDtypeStruct((tokens, width), bf16)] * 2
        + [jax.ShapeDtypeStruct(grads_shape, bf16)] * count,
        compiler_params=pltpu.CompilerParams(vmem_limit_bytes=56 << 20),
        cost_estimate=pl.CostEstimate(flops=0, transcendentals=0, bytes_accessed=0),
    )(me, third_in, shifted(third_in, "core", 1), grad_mlp, shifted(grad_mlp, "core", 1), *weights)
    if paired:
        up_kept, up_sent, down_kept, down_sent = parts

        def as_grid(part):
            return part.transpose(1, 2, 0, 3, 4)[None]

        sums = (
            ([as_grid(up_kept)], [], [as_grid(shifted(up_sent, "x", 1))]),
            ([as_grid(down_kept)], [], [as_grid(shifted(down_sent, "y", 1))]),
        )
    else:
        sums = launch([parts[0][None]], "x", 3), launch([parts[1][None]], "y", 4)
    out = out + shifted(out_far, "core", 1).astype(f32)
    back = back + shifted(back_far, "core", 1).astype(f32)
    return out, back, sums


def clips_kernel(clip_ref, digits_ref, first, one, resid, mixed, third, three, up, mlp, out_ref):
    clips, width = out_ref.shape[0], first.shape[1]
    row = lax.broadcasted_iota(jnp.int32, (16, 1), 0)
    chooser = (clip_ref[...] == row).astype(f32).astype(bf16)
    parts = [
        first[...],
        first[...] * one[...],
        resid[...] * mixed[...],
        third[...],
        third[...] * three[...],
        up[...].astype(f32) * mlp[...],
    ]
    for place, part in enumerate(parts):
        total = matmul(chooser, part.astype(bf16))[:clips]
        out_ref[:, place * width : (place + 1) * width] = total.astype(bf16)
    out_ref[:, len(parts) * width :] = digits_ref[...]


def clip_sums(clips, clip, digits, *values):
    width = values[0].shape[1]
    return pl.pallas_call(
        clips_kernel,
        out_shape=jax.ShapeDtypeStruct((clips, 6 * width + digits.shape[1]), bf16),
        compiler_params=pltpu.CompilerParams(vmem_limit_bytes=VMEM),
    )(clip[None, :], digits, *values)


def shards(
    frames,
    seg_ids,
    text,
    text_lens,
    step_ids,
    step_table,
    ada_weight,
    ada_bias,
    query_w,
    key_w,
    value_w,
    out_w,
    cross_query_w,
    cross_key_w,
    cross_value_w,
    cross_out_w,
    up_weight,
    down_weight,
    out_grad,
):
    width = frames.shape[1]
    za, zb, nx = (lax.axis_size(axis) for axis in MP_AXES)
    mp = za * zb * nx
    position = (lax.axis_index("za") * zb + lax.axis_index("zb")) * nx + lax.axis_index("x")
    rows_dev = seg_ids.shape[0] // mp
    frames_row = seg_ids.shape[1]
    segs_dev = rows_dev * SEGS
    my_ids = lax.dynamic_slice_in_dim(seg_ids, position * rows_dev, rows_dev, 0)
    my_lens = lax.dynamic_slice_in_dim(text_lens, position * segs_dev, segs_dev, 0)

    half = width // 2
    first, more = weight_parts(
        [
            query_w.T,
            key_w.T,
            value_w.T,
            out_w,
            cross_query_w.T,
            cross_key_w.T,
            cross_value_w.T,
            cross_out_w,
        ]
    )
    first_column = gather_axis(first, "za")
    feed_part = feed_parts(up_weight, down_weight, first_column)
    column = gather_axis(first_column, "zb")
    more = after(more, column)
    first_left = gather_axis(column[..., :half], "x")
    first_right = gather_axis(column[..., half:], "y")
    crossed = (first_left, first_right)
    more = gather_axis(more, "za", *crossed)
    feed_part = after(feed_part, more)
    my_steps = lax.dynamic_slice_in_dim(after(step_ids, column), position * segs_dev, segs_dev, 0)
    digits = jnp.stack([my_steps // 256, my_steps % 256], axis=1).astype(bf16)
    digits = jnp.pad(digits, ((0, 0), (0, 126)))

    same_seg = my_ids[:, :, None] == my_ids[:, None, :]
    self_bias = jnp.where(same_seg, 0.0, masked_score).astype(f32)
    key_segment = jnp.arange(SEGS * CAPTION) % SEGS
    valid_key = (
        jnp.arange(CAPTION)[None, :, None] < my_lens.reshape(rows_dev, SEGS)[:, None, :]
    ).reshape(rows_dev, SEGS * CAPTION)
    allowed = (my_ids[:, :, None] == key_segment[None, None, :]) & valid_key[:, None, :]
    cross_bias = jnp.where(allowed, 0.0, masked_score).astype(f32)
    allowed_t = (my_ids[:, None, :] == key_segment[None, :, None]) & valid_key[:, :, None]
    cross_bias_t = jnp.where(allowed_t, 0.0, masked_score).astype(f32)

    text = after(text, column)
    text_flat = text.reshape(rows_dev, SEGS, CAPTION, width).swapaxes(1, 2).reshape(-1, width)
    prepared = (digits, text_flat)
    first_left = gather_axis(first_left, "y", more)
    first_right = gather_axis(first_right, "x", more)
    more = gather_axis(more, "zb", first_left, first_right, *prepared)
    feed_part = gather_axis(feed_part, "za", first_left, first_right)
    more_left = gather_axis(more[..., :half], "x", first_left, first_right)
    more_right = gather_axis(more[..., half:], "y", first_left, first_right)
    qkv = assemble(gather_axis(first_left, "core"), gather_axis(first_right, "core"))
    qkv = qkv.reshape(-1, width)
    table_low = step_table
    step_ids = after(step_ids, first_column)
    choose_step = (step_ids[:, None] == jnp.arange(step_table.shape[0])[None, :]).astype(bf16)
    silu_mine = jax.nn.silu(matmul(choose_step, table_low)).astype(bf16)
    partial_mod = matmul(silu_mine, ada_weight)
    partial_mod = partial_mod.reshape(za, zb, nx, segs_dev, partial_mod.shape[1])
    modulation = summed(landed(launch_wide(partial_mod, "x", 2), column)).astype(bf16)
    modulation = summed(landed(launch([modulation], "zb", 1), *crossed)).astype(bf16)
    modulation = summed(landed(launch([modulation], "za", 0), first_left, first_right))
    modulation = modulation + ada_bias.astype(f32)
    flat_ids = my_ids.reshape(-1)
    row_of = jnp.arange(flat_ids.shape[0]) // frames_row
    clip = flat_ids + row_of * SEGS
    chosen = clip[:, None] == jnp.arange(segs_dev)[None, :]

    def per_frame(index):
        table = modulation[:, index * width : (index + 1) * width]
        value = jnp.broadcast_to(table[0:1], (clip.shape[0], width))
        for segment in range(1, segs_dev):
            value = jnp.where(chosen[:, segment : segment + 1], table[segment : segment + 1], value)
        return value

    shift_one, scale_one, gate_one, shift_two, scale_two, gate_two = map(per_frame, range(6))

    base = frames.astype(f32)
    normed_one, inverse_one = normalize(base)
    first_in = (normed_one * (1.0 + scale_one) + shift_one).astype(bf16)
    query, keys, values = (
        outer_cols(first_in, qkv[i * width : (i + 1) * width]).astype(bf16) for i in range(3)
    )
    self_mix = attend(query, keys, values, self_bias)
    more_left = gather_axis(more_left, "y", self_mix)
    more_right = gather_axis(more_right, "x", self_mix)
    feed_part = gather_axis(feed_part, "zb", self_mix)
    feed_up = gather_axis(feed_part[:, :, 0], "x", more_left, more_right)
    feed_down = gather_axis(feed_part[:, :, 1], "y", more_left, more_right)
    whole = assemble(gather_axis(more_left, "core"), gather_axis(more_right, "core"))
    out_full, cquery_t, cout_full = whole[0], whole[1], whole[4]
    ckv_t = whole[2:4].reshape(-1, width)
    self_out = matmul(self_mix, out_full)
    resid_one = base + gate_one * self_out
    normed_two, inverse_two = normalize(resid_one)
    second_in = normed_two.astype(bf16)
    cross_query = outer_cols(second_in, cquery_t).astype(bf16)
    cross_keys = outer_cols(text_flat, ckv_t[:width]).astype(bf16)
    cross_values = outer_cols(text_flat, ckv_t[width:]).astype(bf16)
    cross_mix = attend(cross_query, cross_keys, cross_values, cross_bias)
    resid_two = resid_one + matmul(cross_mix, cout_full)
    normed_three, inverse_three = normalize(resid_two)
    third_in = (normed_three * (1.0 + scale_two) + shift_two).astype(bf16)
    upstream = out_grad.astype(f32)
    grad_mlp = (gate_two * upstream).astype(bf16)
    core = lax.axis_index("core").reshape(1)
    mlp_out, grad_third, feed_sums = feed(third_in, grad_mlp, feed_up, feed_down)
    layer_out = (resid_two + gate_two * mlp_out).astype(bf16)

    grad_resid_two = upstream + norm_back(
        normed_three, inverse_three, grad_third * (1.0 + scale_two)
    )
    grad_cross = after(grad_resid_two.astype(bf16), *sends(feed_sums))
    grad_text, grad_second, *cross_parts = attend_back(
        core,
        cross_query,
        cross_keys,
        cross_values,
        cross_mix,
        cross_bias_t,
        [cout_full, cquery_t, ckv_t[:width], ckv_t[width:]],
        grad_cross,
        second_in,
        text_flat,
    )
    with jax.named_scope("cross_sums_first_stage"):
        cross_sums = first_stage(*cross_parts)
    with jax.named_scope("feed_sums_second_stage"):
        feed_sums = second_stage(feed_sums, grad_second)
    grad_resid_one = grad_resid_two + norm_back(normed_two, inverse_two, grad_second)
    grad_self = after(
        (gate_one * grad_resid_one).astype(bf16), *sends(cross_sums), *sends(feed_sums)
    )
    grad_first, *self_parts = attend_back(
        core,
        query,
        keys,
        values,
        self_mix,
        self_bias,
        [out_full, qkv[:width], qkv[width : 2 * width], qkv[2 * width :]],
        grad_self,
        first_in,
    )
    with jax.named_scope("feed_sums_third_stage"):
        feed_sums = third_stage(feed_sums, grad_first)
    with jax.named_scope("cross_sums_second_stage"):
        cross_sums = second_stage(cross_sums, grad_first)
    with jax.named_scope("self_sums_first_stage"):
        self_sums = first_stage(*self_parts, *sends(cross_sums), *feed_sums[1])

    grad_first = after(grad_first, *sends(self_sums))
    grad_mod = clip_sums(
        segs_dev,
        clip,
        digits,
        grad_first,
        normed_one,
        grad_resid_one,
        self_out,
        grad_third,
        normed_three,
        out_grad,
        mlp_out,
    )
    with jax.named_scope("feed_sums_fourth_stage"):
        feed_sums = fourth_stage(feed_sums, grad_mod)
    with jax.named_scope("cross_sums_third_stage"):
        cross_sums = third_stage(cross_sums, *feed_sums[1])
    with jax.named_scope("self_sums_second_stage"):
        self_sums = second_stage(self_sums, *cross_sums[1])
    with jax.named_scope("gather_mod"):
        gathered = joined_rows(grad_mod, "za", *sends(self_sums))
    with jax.named_scope("cross_sums_fourth_stage"):
        cross_sums = fourth_stage(cross_sums, gathered)
    feed_done = summed(landed(feed_sums, *cross_sums[1])).astype(bf16)
    with jax.named_scope("feed_spread"):
        feed_quarters = spread(feed_done)
    with jax.named_scope("self_sums_third_stage"):
        self_sums = third_stage(self_sums, feed_done)
    with jax.named_scope("gather_mod"):
        gathered = joined_rows(gathered, "zb", *self_sums[1])
    cross_done = summed(landed(cross_sums, gathered)).astype(bf16)
    with jax.named_scope("cross_spread"):
        cross_quarters = spread(cross_done)
    with jax.named_scope("self_sums_fourth_stage"):
        self_sums = fourth_stage(self_sums, feed_quarters[1])
    with jax.named_scope("gather_mod"):
        gathered = joined_rows(gathered, "x", *self_sums[1])
    grad_frames = grad_resid_one + norm_back(
        normed_one, inverse_one, after(grad_first, gathered) * (1.0 + scale_one)
    )
    self_done = summed(landed(self_sums, grad_frames)).astype(bf16)
    with jax.named_scope("gather_mod"):
        gathered = joined_rows(gathered, "y", self_done, cross_done)
    with jax.named_scope("gather_mod"):
        gathered = joined_rows(gathered, "core", self_done)
    grad_mod_all = gathered[:, : 6 * width]
    digits = gathered[:, 6 * width : 6 * width + 2].astype(f32)
    steps_all = digits[:, 0] * 256.0 + digits[:, 1]
    choose_all = (
        steps_all[:, None] == jnp.arange(step_table.shape[0]).astype(f32)[None, :]
    ).astype(bf16)
    cond_all = matmul(choose_all, table_low)
    silu_all = jax.nn.silu(cond_all).astype(bf16)
    grad_ada_w = inner_rows(silu_all, grad_mod_all)
    grad_ada_b = jnp.sum(grad_mod_all.astype(f32), axis=0)
    grad_cond = silu_back(cond_all, outer_cols(grad_mod_all, ada_weight))
    grad_table = lax.dot_general(
        choose_all.astype(f32), grad_cond, (((0,), (0,)), ((), ())), precision=highest
    )

    hidden, low = down_weight.shape[0], out_w.shape[0]
    made = (grad_ada_w, grad_table)
    with jax.named_scope("self_spread"):
        self_quarters = spread(self_done, *made)
    shard_up, shard_down = finish(feed_quarters, hidden, [up_weight.shape, down_weight.shape])
    shard_cout, shard_cquery, shard_ckey, shard_cvalue = finish(
        cross_quarters, low, [out_w.shape] * 4
    )
    shard_out, shard_query, shard_key, shard_value = finish(
        self_quarters, low, [out_w.shape] * 4, shard_up, shard_cout
    )

    return (
        layer_out,
        grad_frames,
        grad_text.reshape(rows_dev, CAPTION, SEGS, width).swapaxes(1, 2).reshape(text.shape),
        grad_table,
        grad_ada_w,
        grad_ada_b,
        shard_query.T,
        shard_key.T,
        shard_value.T,
        shard_out,
        shard_cquery.T,
        shard_ckey.T,
        shard_cvalue.T,
        shard_cout,
        shard_up,
        shard_down,
    )


def solution(mesh):
    dp, mp = mesh.shape["dp"], mesh.shape["mp"]
    fine = Mesh(mesh.devices.reshape(dp // 2, 2, mp // 4, 2, 2), FINE)
    dp_axes, mp_axes = ("y", "core"), MP_AXES
    return jax.shard_map(
        shards,
        mesh=fine,
        in_specs=(
            P(FINE, None),
            P(dp_axes, None),
            P(FINE, None, None),
            P(dp_axes),
            P(dp_axes),
            P(None, mp_axes),
            P(mp_axes, None),
            P(),
            P(None, mp_axes),
            P(None, mp_axes),
            P(None, mp_axes),
            P(mp_axes, None),
            P(None, mp_axes),
            P(None, mp_axes),
            P(None, mp_axes),
            P(mp_axes, None),
            P(None, mp_axes),
            P(mp_axes, None),
            P(FINE, None),
        ),
        out_specs=(
            P(FINE, None),
            P(FINE, None),
            P(FINE, None, None),
            P(None, mp_axes),
            P(mp_axes, None),
            P(),
            P(None, mp_axes),
            P(None, mp_axes),
            P(None, mp_axes),
            P(mp_axes, None),
            P(None, mp_axes),
            P(None, mp_axes),
            P(None, mp_axes),
            P(mp_axes, None),
            P(None, mp_axes),
            P(mp_axes, None),
        ),
        check_vma=False,
    )
```

```python
from functools import partial
from typing import Any, NamedTuple

import jax
import jax.numpy as jnp
from jax import lax
from jax.experimental import pallas as pl
from jax.experimental.pallas import tpu as pltpu
from jax.sharding import Mesh, PartitionSpec as P

HEADS = 12
HD = 64
CAPTION = 77
SEGS = 4

QUAD = 4 * HD
highest = lax.Precision.HIGHEST
epsilon = 1e-06
masked_score = -1e30
bf16 = jnp.bfloat16
f32 = jnp.float32
FINE = ("y", "core", "za", "zb", "x")
MP_AXES = ("za", "zb", "x")
VMEM = 48 << 20


def shifted(value, axis, steps):
    count = lax.axis_size(axis)
    with jax.named_scope(f"to_{axis}_{steps}"):
        return lax.ppermute(value, axis, [(k, (k + steps) % count) for k in range(count)])


def gather_axis(value, axis, *hold):
    count = lax.axis_size(axis)
    me = lax.axis_index(axis)
    pieces = [shifted(value, axis, s) for s in range(1, count)]
    if hold:
        pieces = [after(piece, *hold) for piece in pieces]
    pieces = [value] + pieces

    def at(place):
        turn = (me - place) % count
        chosen = pieces[0]
        for s in range(1, count):
            chosen = jnp.where(turn == s, pieces[s], chosen)
        return chosen

    return jnp.stack([at(place) for place in range(count)])


def joined_rows(value, axis, *hold):
    return gather_axis(value, axis, *hold).reshape(-1, value.shape[-1])


def after(value, *done):
    return lax.optimization_barrier((value, *done))[0]


class Term(NamedTuple):
    value: Any
    picks: tuple = ()
    done: tuple = ()

    def piece(self):
        value = after(self.value, *self.done) if self.done else self.value
        for dim, which in self.picks:
            value = lax.dynamic_index_in_dim(value, which, dim, keepdims=False)
        return value


def picked(terms, dim, which):
    terms = [t if isinstance(t, Term) else Term(t) for t in terms]
    return [t._replace(picks=(*t.picks, (dim, which))) for t in terms]


def summed(terms):
    pieces = [t.piece() for t in terms]
    total = pieces[0].astype(f32)
    for piece in pieces[1:]:
        total = total + piece.astype(f32)
    return total


def launch(terms, axis, dim):
    count = lax.axis_size(axis)
    me = lax.axis_index(axis)
    sent = [
        summed(picked(terms, dim, (me + s) % count)).astype(bf16) for s in range(1, count)
    ]
    arrived = [shifted(part, axis, s) for s, part in enumerate(sent, 1)]
    return picked(terms, dim, me), sent, arrived


def launch_wide(value, axis, dim):
    count = lax.axis_size(axis)
    me = lax.axis_index(axis)
    sent = [picked([value], dim, (me + s) % count)[0].piece() for s in range(1, count)]
    arrived = [shifted(part, axis, s) for s, part in enumerate(sent, 1)]
    return picked([value], dim, me), sent, arrived


def landed(started, *done):
    kept, _, arrived = started
    kept = [t if isinstance(t, Term) else Term(t) for t in kept]
    if done:
        kept = [t._replace(done=done) for t in kept]
        arrived = [after(part, *done) for part in arrived]
    return kept + [Term(part) for part in arrived]


def split_rows(part):
    grid = [lax.axis_size(a) for a in (*MP_AXES, "y")]
    return part.reshape(part.shape[0], *grid, -1, part.shape[-1])


def first_stage(mine_a, mine_b, other_a, other_b, *done):
    other_a, other_b = shifted(other_a, "core", 1), shifted(other_b, "core", 1)
    if done:
        other_a, other_b = after(other_a, *done), after(other_b, *done)
    left = [split_rows(mine_a), split_rows(other_a)]
    right = [split_rows(mine_b), split_rows(other_b)]
    return launch(left, "x", 3), launch(right, "y", 4)


def second_stage(stage, *done):
    left = launch(landed(stage[0], *done), "y", 3)
    right = launch(landed(stage[1], *done), "x", 3)
    return left, right


def third_stage(stage, *done):
    left, right = (summed(landed(part, *done)).astype(bf16) for part in stage)
    return launch([jnp.stack([left, right])], "zb", 3)


def fourth_stage(stage, *done):
    return launch(landed(stage, *done), "za", 2)


def sends(stage):
    return stage[0][1] + stage[1][1]


def assemble(left, right):
    left = left.transpose(5, 4, 3, 2, 1, 0, 6, 7)
    right = right.transpose(5, 4, 3, 1, 2, 0, 6, 7)
    whole = jnp.concatenate([left, right], axis=-1)
    return whole.reshape(whole.shape[0], -1, whole.shape[-1])


def rows_kernel(mine_ref, *refs):
    *sources, first_ref, more_ref, sems = refs
    rows = first_ref.shape[1]
    own = pl.ds(pl.multiple_of(mine_ref[0] * rows, 8), rows)
    copies = []
    for which, source in enumerate(sources):
        target = first_ref.at[which] if which < 3 else more_ref.at[which - 3]
        copies.append(pltpu.make_async_copy(source.at[own, :], target, sems.at[which]))
    for copy in copies:
        copy.start()
    for copy in copies:
        copy.wait()


def feed_rows_kernel(mine_ref, up_ref, down_ref, feed_ref, wide_ref, tall_ref, sems):
    rows = feed_ref.shape[1]
    own = pl.ds(pl.multiple_of(mine_ref[0] * rows, 8), rows)
    down = pltpu.make_async_copy(down_ref.at[own, :], feed_ref.at[1], sems.at[0])
    up = pltpu.make_async_copy(up_ref, wide_ref, sems.at[1])
    down.start()
    up.start()
    up.wait()
    tall_ref[...] = wide_ref[...].astype(f32).T
    down.wait()
    feed_ref[0] = tall_ref[own, :].astype(bf16)


def own_rows(value, mine):
    part = value.shape[0] // (lax.axis_size("y") * lax.axis_size("core"))
    return lax.dynamic_slice_in_dim(value, mine * part, part, 0)


def weight_parts(weights):
    copies = lax.axis_size("y") * lax.axis_size("core")
    mine = lax.axis_index("y") * lax.axis_size("core") + lax.axis_index("core")
    width, rows = weights[0].shape[1], weights[0].shape[0] // copies
    if rows % 8:
        kept = [own_rows(w, mine) for w in weights]
        return jnp.stack(kept[:3]), jnp.stack(kept[3:])
    smem, hbm = pl.BlockSpec(memory_space=pltpu.SMEM), pl.BlockSpec(memory_space=pltpu.HBM)
    vmem = pl.BlockSpec(memory_space=pltpu.VMEM)
    return pl.pallas_call(
        rows_kernel,
        in_specs=[smem] + [hbm] * len(weights),
        out_specs=[vmem] * 2,
        out_shape=[
            jax.ShapeDtypeStruct((3, rows, width), bf16),
            jax.ShapeDtypeStruct((len(weights) - 3, rows, width), bf16),
        ],
        scratch_shapes=[pltpu.SemaphoreType.DMA((len(weights),))],
    )(mine.reshape(1), *weights)


def feed_parts(up_weight, down_weight, *done):
    copies = lax.axis_size("y") * lax.axis_size("core")
    mine = lax.axis_index("y") * lax.axis_size("core") + lax.axis_index("core")
    mine = after(mine, *done)
    hidden, width = down_weight.shape
    if hidden // copies % 8:
        return jnp.stack([own_rows(up_weight.T, mine), own_rows(down_weight, mine)])
    smem, hbm = pl.BlockSpec(memory_space=pltpu.SMEM), pl.BlockSpec(memory_space=pltpu.HBM)
    vmem = pl.BlockSpec(memory_space=pltpu.VMEM)
    return pl.pallas_call(
        feed_rows_kernel,
        in_specs=[smem, hbm, hbm],
        out_specs=vmem,
        out_shape=jax.ShapeDtypeStruct((2, hidden // copies, width), bf16),
        scratch_shapes=[
            pltpu.VMEM((width, hidden), bf16),
            pltpu.VMEM((hidden, width), f32),
            pltpu.SemaphoreType.DMA((2,)),
        ],
    )(mine.reshape(1), up_weight, down_weight)


def finish_kernel(me_ref, near, far_y, far_core, far_both, *refs):
    *outs, whole_ref = refs
    y, core = me_ref[0], me_ref[1]
    matrices, rows, lanes = near.shape
    by_rows = lanes == whole_ref.shape[1]

    def place(which, part, turn_y, turn_core):
        here_y, here_core = y ^ turn_y, core ^ turn_core
        row = (2 * here_y + here_core) * rows if by_rows else here_y * rows
        row = pl.ds(pl.multiple_of(row, 8), rows)
        if by_rows:
            whole_ref[row, :] = part[which].astype(f32)
        else:
            lane = pl.ds(pl.multiple_of(here_core * lanes, 128), lanes)
            whole_ref[row, lane] = part[which].astype(f32)

    for which, out in enumerate(outs):
        for part, turns in ((near, (0, 0)), (far_y, (1, 0)), (far_core, (0, 1)), (far_both, (1, 1))):
            place(which, part, *turns)
        out[...] = whole_ref[...] if out.shape == whole_ref.shape else whole_ref[...].T


def spread(done, *hold):
    done = done.reshape(-1, *done.shape[2:])
    far_y = shifted(done, "y", 1)
    if hold:
        far_y = after(far_y, *hold)
    return done, far_y, shifted(done, "core", 1), shifted(far_y, "core", 1)


def finish(quarters, rows, shapes, *hold):
    done, far_y, far_core, far_both = quarters
    by_rows = lax.axis_size("y") * lax.axis_size("core") * done.shape[1] == rows
    width = done.shape[2] if by_rows else 2 * done.shape[2]
    if lax.axis_size("y") != 2 or done.shape[1] % 8 or done.shape[2] % 128:
        done = gather_axis(gather_axis(done, "core"), "y")
        axes = (2, 0, 1, 3, 4) if by_rows else (2, 0, 3, 1, 4)
        done = done.transpose(axes).reshape(done.shape[2], rows, width)
        return [
            (d if s == (rows, width) else d.T).astype(f32) for d, s in zip(done, shapes)
        ]
    if hold:
        far_core, far_both = after(far_core, *hold), after(far_both, *hold)
    me = jnp.stack([lax.axis_index("y"), lax.axis_index("core")])

    def whole(shape):
        return pl.BlockSpec(shape, lambda i: (0,) * len(shape))

    return pl.pallas_call(
        finish_kernel,
        grid=(1,),
        in_specs=[pl.BlockSpec(memory_space=pltpu.SMEM)] + [whole(done.shape)] * 4,
        out_specs=[whole(shape) for shape in shapes],
        out_shape=[jax.ShapeDtypeStruct(shape, f32) for shape in shapes],
        scratch_shapes=[pltpu.VMEM((rows, width), f32)],
        compiler_params=pltpu.CompilerParams(vmem_limit_bytes=VMEM),
    )(me, done, far_y, far_core, far_both)


def normalize(values):
    centre = values - jnp.mean(values, axis=-1, keepdims=True)
    inverse = lax.rsqrt(jnp.mean(centre * centre, axis=-1, keepdims=True) + epsilon)
    return (centre * inverse, inverse)


def norm_back(normed, inverse, upstream):
    mean_grad = jnp.mean(upstream, axis=-1, keepdims=True)
    mean_both = jnp.mean(upstream * normed, axis=-1, keepdims=True)
    return inverse * (upstream - mean_grad - normed * mean_both)


def matmul(left, right):
    return jnp.dot(left, right, preferred_element_type=f32)


def inner_rows(left, right):
    return lax.dot_general(left, right, (((0,), (0,)), ((), ())), preferred_element_type=f32)


def outer_cols(left, right):
    return lax.dot_general(left, right, (((1,), (1,)), ((), ())), preferred_element_type=f32)


def gelu_back(pre_act, upstream):
    return jax.vjp(partial(jax.nn.gelu, approximate=True), pre_act)[1](upstream)[0]


def silu_back(inputs, upstream):
    return jax.vjp(jax.nn.silu, inputs)[1](upstream)[0]


def own_lanes(head):
    lane = lax.broadcasted_iota(jnp.int32, (1, QUAD), 1)
    return (lane >= head * HD) & (lane < (head + 1) * HD)


def merged(parts):
    whole = parts[0]
    for head in range(1, len(parts)):
        whole = jnp.where(own_lanes(head), parts[head], whole)
    return whole


def forward_kernel(q_ref, k_ref, v_ref, bias_ref, mix_ref):
    query = q_ref[...] * bf16(HD**-0.5)
    keys, values, bias = k_ref[...], v_ref[...], bias_ref[0]
    parts = []
    for head in range(QUAD // HD):
        own = jnp.where(own_lanes(head), query, bf16(0))
        scores = outer_cols(own, keys) + bias
        raised = jnp.exp(scores - jnp.max(scores, axis=1, keepdims=True))
        total = jnp.sum(raised, axis=1, keepdims=True)
        parts.append(matmul(raised.astype(bf16), values) / total)
    mix_ref[...] = merged(parts).astype(bf16)


def backward_kernel(
    core_ref,
    q_ref,
    k_ref,
    v_ref,
    mix_ref,
    bias_ref,
    out_w_ref,
    q_w_ref,
    k_w_ref,
    v_w_ref,
    back_ref,
    x_ref,
    *rest,
):
    cross = len(rest) > 5
    if cross:
        text_ref, text_grad_ref, in_ref, mine_a, mine_b, other_a, other_b = rest
    else:
        in_ref, mine_a, mine_b, other_a, other_b = rest
        text_ref = x_ref
    query = q_ref[...] * bf16(HD**-0.5)
    keys, values, bias = k_ref[...], v_ref[...], bias_ref[0]
    back = back_ref[...]
    grad = outer_cols(back, out_w_ref[...]).astype(bf16)
    gq, gk, gv = [], [], []
    for head in range(QUAD // HD):
        own = own_lanes(head)
        scores = outer_cols(keys, jnp.where(own, query, bf16(0))) + bias
        raised = jnp.exp(scores - jnp.max(scores, axis=0, keepdims=True))
        weights = raised * (1.0 / jnp.sum(raised, axis=0, keepdims=True))
        grad_weights = outer_cols(jnp.where(own, values, bf16(0)), grad)
        mean = jnp.sum(weights * grad_weights, axis=0, keepdims=True)
        grad_scores = (weights * (grad_weights - mean)).astype(bf16)
        gv.append(matmul(weights.astype(bf16), grad))
        gk.append(matmul(grad_scores, query))
        gq.append(inner_rows(grad_scores, keys))
    gq = (merged(gq) * HD**-0.5).astype(bf16)
    gk, gv = merged(gk).astype(bf16), merged(gv).astype(bf16)

    @pl.when(pl.program_id(1) == 0)
    def _():
        in_ref[...] = jnp.zeros_like(in_ref)
        if cross:
            text_grad_ref[...] = jnp.zeros_like(text_grad_ref)

    if cross:
        in_ref[...] += matmul(gq, q_w_ref[...])
        text_grad_ref[...] += matmul(gk, k_w_ref[...]) + matmul(gv, v_w_ref[...])
    else:
        in_ref[...] += (
            matmul(gq, q_w_ref[...]) + matmul(gk, k_w_ref[...]) + matmul(gv, v_w_ref[...])
        )
    half = mine_a.shape[-1]
    first = core_ref[0] == 0
    mine, other = (mine_a, mine_b), (other_a, other_b)
    pairs = [(mix_ref[...], back), (gq, x_ref[...]), (gk, text_ref[...]), (gv, text_ref[...])]
    for which, (left, right) in enumerate(pairs):
        whole = inner_rows(left, right).astype(bf16)
        low, high = whole[:, :half], whole[:, half:]
        mine[which // 2][which % 2] = jnp.where(first, low, high)
        other[which // 2][which % 2] = jnp.where(first, high, low)


def attend(query, keys, values, bias):
    rows, frames, tokens = bias.shape
    pairs = query.shape[1] // QUAD
    blocks = [pl.BlockSpec((n, QUAD), lambda r, h: (r, h)) for n in (frames, tokens, tokens)]
    return pl.pallas_call(
        forward_kernel,
        grid=(rows, pairs),
        in_specs=blocks + [pl.BlockSpec((1, frames, tokens), lambda r, h: (r, 0, 0))],
        out_specs=blocks[0],
        out_shape=jax.ShapeDtypeStruct(query.shape, bf16),
        compiler_params=pltpu.CompilerParams(vmem_limit_bytes=VMEM),
        cost_estimate=pl.CostEstimate(flops=0, transcendentals=0, bytes_accessed=0),
    )(query, keys, values, bias)


def attend_back(core, query, keys, values, mix, bias, weights, back, x, text=None):
    rows, tokens, frames = bias.shape
    width = query.shape[1]
    pairs, half = width // QUAD, width // 2
    wide = pl.BlockSpec((frames, QUAD), lambda r, h, c: (r, h))
    held = pl.BlockSpec((tokens, QUAD), lambda r, h, c: (r, h))
    matrix = pl.BlockSpec((QUAD, width), lambda r, h, c: (h, 0))
    frames_all = pl.BlockSpec((frames, width), lambda r, h, c: (r, 0))
    tokens_all = pl.BlockSpec((tokens, width), lambda r, h, c: (r, 0))
    grads = pl.BlockSpec((2, QUAD, half), lambda r, h, c: (0, h, 0))
    grads_shape = jax.ShapeDtypeStruct((2, width, half), bf16)
    cross = text is not None
    return pl.pallas_call(
        backward_kernel,
        grid_spec=pltpu.PrefetchScalarGridSpec(
            num_scalar_prefetch=1,
            grid=(rows, pairs),
            in_specs=[wide, held, held, wide]
            + [pl.BlockSpec((1, tokens, frames), lambda r, h, c: (r, 0, 0))]
            + [matrix] * 4
            + [frames_all] * 2
            + [tokens_all] * cross,
            out_specs=[tokens_all] * cross + [frames_all] + [grads] * 4,
        ),
        out_shape=[jax.ShapeDtypeStruct((rows * tokens, width), f32)] * cross
        + [jax.ShapeDtypeStruct(x.shape, f32)]
        + [grads_shape] * 4,
        compiler_params=pltpu.CompilerParams(vmem_limit_bytes=VMEM),
        cost_estimate=pl.CostEstimate(flops=0, transcendentals=0, bytes_accessed=0),
    )(core, query, keys, values, mix, bias, *weights, back, x, *([text] if cross else []))


def feed_kernel(paired, me_ref, x_ref, x_far, g_ref, g_far, *refs):
    inputs, outs = refs[: 4 if paired else 2], refs[4 if paired else 2 :]
    out_ref, back_ref, out_far, back_far, *grad_refs = outs[:-6]
    out_sum, back_sum, third_both, grad_both, active_both, pre_both = outs[-6:]
    tokens = x_ref.shape[0]
    slope = (2.0 / jnp.pi) ** 0.5
    step = pl.program_id(0)

    @pl.when(step == 0)
    def _():
        for ref in (out_ref, back_ref, out_sum, back_sum):
            ref[...] = jnp.zeros_like(ref)
        third_both[:tokens], third_both[tokens:] = x_ref[...], x_far[...]
        grad_both[:tokens], grad_both[tokens:] = g_ref[...], g_far[...]

    my_y, my_x = me_ref[0], me_ref[1]
    if paired:
        up_near, up_far, down_near, down_far = inputs
        (nx, zb, _, rows, _), ny = up_near.shape, 2
        up_at = lambda b, x, y: jnp.where(my_y == y, up_near[x, b, 0], up_far[x, b, 0])
        down_at = lambda b, x, y: jnp.where(my_x == x, down_near[y, b, 0], down_far[y, b, 0])
    else:
        up_ref, down_ref = inputs
        ny, nx, zb, _, rows, _ = up_ref.shape
        up_at = lambda b, x, y: up_ref[y, x, b, 0]
        down_at = lambda b, x, y: down_ref[y, x, b, 0]
    places = [(b, x, y) for b in range(zb) for x in range(nx) for y in range(ny)]
    up = jnp.concatenate([up_at(*p) for p in places], axis=0)
    down = jnp.concatenate([down_at(*p) for p in places], axis=0)
    for which, (out, back) in enumerate(((out_ref, back_ref), (out_sum, back_sum))):
        here = slice(which * tokens, (which + 1) * tokens)
        pre = outer_cols(third_both[here], up)
        square = pre * pre
        rise = 0.5 + 0.5 * jnp.tanh(pre * (slope + (0.044715 * slope) * square))
        active = pre * rise
        steep = rise + active * (1.0 - rise) * (2.0 * slope + (0.26829 * slope) * square)
        active = active.astype(bf16)
        grad_pre = (outer_cols(grad_both[here], down) * steep).astype(bf16)
        out[...] += matmul(active, down)
        back[...] += matmul(grad_pre, up)
        active_both[here] = active
        pre_both[here] = grad_pre
    up_total = inner_rows(pre_both[...], third_both[...]).astype(bf16)
    down_total = inner_rows(active_both[...], grad_both[...]).astype(bf16)
    at = {p: slice(n * rows, (n + 1) * rows) for n, p in enumerate(places)}
    if paired:
        up_kept, up_sent, down_kept, down_sent = grad_refs
        for b in range(zb):
            for k in range(2):
                zero, one = up_total[at[b, 0, k]], up_total[at[b, 1, k]]
                up_kept[k, 0, b] = jnp.where(my_x == 0, zero, one)
                up_sent[k, 0, b] = jnp.where(my_x == 0, one, zero)
                zero, one = down_total[at[b, k, 0]], down_total[at[b, k, 1]]
                down_kept[k, 0, b] = jnp.where(my_y == 0, zero, one)
                down_sent[k, 0, b] = jnp.where(my_y == 0, one, zero)
    else:
        for ref, total in zip(grad_refs, (up_total, down_total)):
            for b, x, y in places:
                ref[0, b, x, y] = total[at[b, x, y]]

    @pl.when(step == pl.num_programs(0) - 1)
    def _():
        out_far[...] = out_sum[...].astype(bf16)
        back_far[...] = back_sum[...].astype(bf16)


def feed(third_in, grad_mlp, up, down):
    tokens, width = third_in.shape
    nx, zb, za, rows, _ = up.shape
    ny = lax.axis_size("y")
    paired = nx == 2 and ny == 2
    if paired:
        weights = [up, shifted(up, "y", 1), down, shifted(down, "x", 1)]
    else:
        weights = [gather_axis(up, "y"), gather_axis(down, "x").swapaxes(0, 1)]
    whole = pl.BlockSpec((tokens, width), lambda j, c: (0, 0))
    half_shape, whole_shape = (2, za, zb, rows, width), (za, zb, nx, ny, rows, width)
    grads_shape = half_shape if paired else whole_shape
    matrix_shape = (2, zb, 1, rows, width) if paired else (ny, nx, zb, 1, rows, width)
    zeros = len(matrix_shape) - 3
    matrix = pl.BlockSpec(matrix_shape, lambda j, c: (0,) * zeros + (j, 0, 0))
    if paired:
        grads = pl.BlockSpec((2, 1, zb, rows, width), lambda j, c: (0, j, 0, 0, 0))
    else:
        grads = pl.BlockSpec((1, *whole_shape[1:]), lambda j, c: (j, 0, 0, 0, 0, 0))
    count = 4 if paired else 2
    me = jnp.stack([lax.axis_index("y"), lax.axis_index("x")])
    out, back, out_far, back_far, *parts = pl.pallas_call(
        partial(feed_kernel, paired),
        grid_spec=pltpu.PrefetchScalarGridSpec(
            num_scalar_prefetch=1,
            grid=(za,),
            in_specs=[whole] * 4 + [matrix] * count,
            out_specs=[whole] * 4 + [grads] * count,
            scratch_shapes=[pltpu.VMEM((tokens, width), f32)] * 2
            + [pltpu.VMEM((2 * tokens, width), bf16)] * 2
            + [pltpu.VMEM((2 * tokens, zb * nx * ny * rows), bf16)] * 2,
        ),
        out_shape=[jax.ShapeDtypeStruct((tokens, width), f32)] * 2
        + [jax.ShapeDtypeStruct((tokens, width), bf16)] * 2
        + [jax.ShapeDtypeStruct(grads_shape, bf16)] * count,
        compiler_params=pltpu.CompilerParams(vmem_limit_bytes=56 << 20),
        cost_estimate=pl.CostEstimate(flops=0, transcendentals=0, bytes_accessed=0),
    )(me, third_in, shifted(third_in, "core", 1), grad_mlp, shifted(grad_mlp, "core", 1), *weights)
    if paired:
        up_kept, up_sent, down_kept, down_sent = parts

        def as_grid(part):
            return part.transpose(1, 2, 0, 3, 4)[None]

        sums = (
            ([as_grid(up_kept)], [], [as_grid(shifted(up_sent, "x", 1))]),
            ([as_grid(down_kept)], [], [as_grid(shifted(down_sent, "y", 1))]),
        )
    else:
        sums = launch([parts[0][None]], "x", 3), launch([parts[1][None]], "y", 4)
    back = back + shifted(back_far, "core", 1).astype(f32)
    return out, shifted(out_far, "core", 1), back, sums


def clips_kernel(clip_ref, digits_ref, first, one, resid, mixed, third, three, up, mlp, mlp_far, out_ref):
    clips, width = out_ref.shape[0], first.shape[1]
    row = lax.broadcasted_iota(jnp.int32, (16, 1), 0)
    chooser = (clip_ref[...] == row).astype(f32).astype(bf16)
    parts = [
        first[...],
        first[...] * one[...],
        resid[...] * mixed[...],
        third[...],
        third[...] * three[...],
        up[...].astype(f32) * (mlp[...] + mlp_far[...].astype(f32)),
    ]
    for place, part in enumerate(parts):
        total = matmul(chooser, part.astype(bf16))[:clips]
        out_ref[:, place * width : (place + 1) * width] = total.astype(bf16)
    out_ref[:, len(parts) * width :] = digits_ref[...]


def clip_sums(clips, clip, digits, *values):
    width = values[0].shape[1]
    return pl.pallas_call(
        clips_kernel,
        out_shape=jax.ShapeDtypeStruct((clips, 6 * width + digits.shape[1]), bf16),
        compiler_params=pltpu.CompilerParams(vmem_limit_bytes=VMEM),
    )(clip[None, :], digits, *values)


def shards(
    frames,
    seg_ids,
    text,
    text_lens,
    step_ids,
    step_table,
    ada_weight,
    ada_bias,
    query_w,
    key_w,
    value_w,
    out_w,
    cross_query_w,
    cross_key_w,
    cross_value_w,
    cross_out_w,
    up_weight,
    down_weight,
    out_grad,
):
    width = frames.shape[1]
    za, zb, nx = (lax.axis_size(axis) for axis in MP_AXES)
    mp = za * zb * nx
    position = (lax.axis_index("za") * zb + lax.axis_index("zb")) * nx + lax.axis_index("x")
    rows_dev = seg_ids.shape[0] // mp
    frames_row = seg_ids.shape[1]
    segs_dev = rows_dev * SEGS
    my_ids = lax.dynamic_slice_in_dim(seg_ids, position * rows_dev, rows_dev, 0)
    my_lens = lax.dynamic_slice_in_dim(text_lens, position * segs_dev, segs_dev, 0)

    half = width // 2
    first, more = weight_parts(
        [
            query_w.T,
            key_w.T,
            value_w.T,
            out_w,
            cross_query_w.T,
            cross_key_w.T,
            cross_value_w.T,
            cross_out_w,
        ]
    )
    first_column = gather_axis(first, "za")
    feed_part = feed_parts(up_weight, down_weight, first_column)
    column = gather_axis(first_column, "zb")
    more = after(more, column)
    first_left = gather_axis(column[..., :half], "x")
    first_right = gather_axis(column[..., half:], "y")
    crossed = (first_left, first_right)
    more = gather_axis(more, "za", *crossed)
    feed_part = after(feed_part, more)
    my_steps = lax.dynamic_slice_in_dim(after(step_ids, column), position * segs_dev, segs_dev, 0)
    digits = jnp.stack([my_steps // 256, my_steps % 256], axis=1).astype(bf16)
    digits = jnp.pad(digits, ((0, 0), (0, 126)))

    same_seg = my_ids[:, :, None] == my_ids[:, None, :]
    self_bias = jnp.where(same_seg, 0.0, masked_score).astype(f32)
    key_segment = jnp.arange(SEGS * CAPTION) % SEGS
    valid_key = (
        jnp.arange(CAPTION)[None, :, None] < my_lens.reshape(rows_dev, SEGS)[:, None, :]
    ).reshape(rows_dev, SEGS * CAPTION)
    allowed = (my_ids[:, :, None] == key_segment[None, None, :]) & valid_key[:, None, :]
    cross_bias = jnp.where(allowed, 0.0, masked_score).astype(f32)
    allowed_t = (my_ids[:, None, :] == key_segment[None, :, None]) & valid_key[:, :, None]
    cross_bias_t = jnp.where(allowed_t, 0.0, masked_score).astype(f32)

    text = after(text, column)
    text_flat = text.reshape(rows_dev, SEGS, CAPTION, width).swapaxes(1, 2).reshape(-1, width)
    prepared = (digits, text_flat)
    first_left = gather_axis(first_left, "y", more)
    first_right = gather_axis(first_right, "x", more)
    more = gather_axis(more, "zb", first_left, first_right, *prepared)
    feed_part = gather_axis(feed_part, "za", first_left, first_right)
    more_left = gather_axis(more[..., :half], "x", first_left, first_right)
    more_right = gather_axis(more[..., half:], "y", first_left, first_right)
    qkv = assemble(gather_axis(first_left, "core"), gather_axis(first_right, "core"))
    qkv = qkv.reshape(-1, width)
    table_low = step_table
    step_ids = after(step_ids, first_column)
    choose_step = (step_ids[:, None] == jnp.arange(step_table.shape[0])[None, :]).astype(bf16)
    silu_mine = jax.nn.silu(matmul(choose_step, table_low)).astype(bf16)
    partial_mod = matmul(silu_mine, ada_weight)
    partial_mod = partial_mod.reshape(za, zb, nx, segs_dev, partial_mod.shape[1])
    modulation = summed(landed(launch_wide(partial_mod, "x", 2), column)).astype(bf16)
    modulation = summed(landed(launch([modulation], "zb", 1), *crossed)).astype(bf16)
    modulation = summed(landed(launch([modulation], "za", 0), first_left, first_right))
    modulation = modulation + ada_bias.astype(f32)
    flat_ids = my_ids.reshape(-1)
    row_of = jnp.arange(flat_ids.shape[0]) // frames_row
    clip = flat_ids + row_of * SEGS
    chosen = clip[:, None] == jnp.arange(segs_dev)[None, :]

    def per_frame(index):
        table = modulation[:, index * width : (index + 1) * width]
        value = jnp.broadcast_to(table[0:1], (clip.shape[0], width))
        for segment in range(1, segs_dev):
            value = jnp.where(chosen[:, segment : segment + 1], table[segment : segment + 1], value)
        return value

    shift_one, scale_one, gate_one, shift_two, scale_two, gate_two = map(per_frame, range(6))

    base = frames.astype(f32)
    normed_one, inverse_one = normalize(base)
    first_in = (normed_one * (1.0 + scale_one) + shift_one).astype(bf16)
    query, keys, values = (
        outer_cols(first_in, qkv[i * width : (i + 1) * width]).astype(bf16) for i in range(3)
    )
    self_mix = attend(query, keys, values, self_bias)
    more_left = gather_axis(more_left, "y", self_mix)
    more_right = gather_axis(more_right, "x", self_mix)
    feed_part = gather_axis(feed_part, "zb", self_mix)
    feed_up = gather_axis(feed_part[:, :, 0], "x", more_left, more_right)
    feed_down = gather_axis(feed_part[:, :, 1], "y", more_left, more_right)
    whole = assemble(gather_axis(more_left, "core"), gather_axis(more_right, "core"))
    out_full, cquery_t, cout_full = whole[0], whole[1], whole[4]
    ckv_t = whole[2:4].reshape(-1, width)
    self_out = matmul(self_mix, out_full)
    resid_one = base + gate_one * self_out
    normed_two, inverse_two = normalize(resid_one)
    second_in = normed_two.astype(bf16)
    cross_query = outer_cols(second_in, cquery_t).astype(bf16)
    cross_keys = outer_cols(text_flat, ckv_t[:width]).astype(bf16)
    cross_values = outer_cols(text_flat, ckv_t[width:]).astype(bf16)
    cross_mix = attend(cross_query, cross_keys, cross_values, cross_bias)
    resid_two = resid_one + matmul(cross_mix, cout_full)
    normed_three, inverse_three = normalize(resid_two)
    third_in = (normed_three * (1.0 + scale_two) + shift_two).astype(bf16)
    upstream = out_grad.astype(f32)
    grad_mlp = (gate_two * upstream).astype(bf16)
    core = lax.axis_index("core").reshape(1)
    mlp_near, mlp_far, grad_third, feed_sums = feed(third_in, grad_mlp, feed_up, feed_down)

    grad_resid_two = upstream + norm_back(
        normed_three, inverse_three, grad_third * (1.0 + scale_two)
    )
    grad_cross = after(grad_resid_two.astype(bf16), *sends(feed_sums))
    grad_text, grad_second, *cross_parts = attend_back(
        core,
        cross_query,
        cross_keys,
        cross_values,
        cross_mix,
        cross_bias_t,
        [cout_full, cquery_t, ckv_t[:width], ckv_t[width:]],
        grad_cross,
        second_in,
        text_flat,
    )
    with jax.named_scope("feed_sums_second_stage"):
        feed_sums = second_stage(feed_sums, grad_second)
    with jax.named_scope("cross_sums_first_stage"):
        cross_sums = first_stage(*cross_parts, *sends(feed_sums))
    grad_resid_one = grad_resid_two + norm_back(normed_two, inverse_two, grad_second)
    grad_self = after(
        (gate_one * grad_resid_one).astype(bf16), *sends(cross_sums), *sends(feed_sums)
    )
    grad_first, *self_parts = attend_back(
        core,
        query,
        keys,
        values,
        self_mix,
        self_bias,
        [out_full, qkv[:width], qkv[width : 2 * width], qkv[2 * width :]],
        grad_self,
        first_in,
    )
    with jax.named_scope("cross_sums_second_stage"):
        cross_sums = second_stage(cross_sums, grad_first)
    with jax.named_scope("feed_sums_third_stage"):
        feed_sums = third_stage(feed_sums, grad_first, *sends(cross_sums))
    with jax.named_scope("self_sums_first_stage"):
        self_sums = first_stage(*self_parts, *sends(cross_sums), *feed_sums[1])

    grad_first = after(grad_first, *sends(self_sums))
    grad_mod = clip_sums(
        segs_dev,
        clip,
        digits,
        grad_first,
        normed_one,
        grad_resid_one,
        self_out,
        grad_third,
        normed_three,
        out_grad,
        mlp_near,
        mlp_far,
    )
    with jax.named_scope("feed_sums_fourth_stage"):
        feed_sums = fourth_stage(feed_sums, grad_mod)
    with jax.named_scope("self_sums_second_stage"):
        self_sums = second_stage(self_sums, *feed_sums[1])
    with jax.named_scope("cross_sums_third_stage"):
        cross_sums = third_stage(cross_sums, *sends(self_sums))
    with jax.named_scope("gather_mod"):
        gathered = joined_rows(grad_mod, "za", *cross_sums[1])
    feed_done = summed(landed(feed_sums, gathered)).astype(bf16)
    with jax.named_scope("feed_spread"):
        feed_quarters = spread(feed_done)
    with jax.named_scope("self_sums_third_stage"):
        self_sums = third_stage(self_sums, feed_done)
    with jax.named_scope("cross_sums_fourth_stage"):
        cross_sums = fourth_stage(cross_sums, *self_sums[1])
    layer_out = resid_two + gate_two * (after(mlp_near, *cross_sums[1]) + mlp_far.astype(f32))
    layer_out = layer_out.astype(bf16)
    with jax.named_scope("gather_mod"):
        gathered = joined_rows(gathered, "zb", *cross_sums[1])
    hidden, low = down_weight.shape[0], out_w.shape[0]
    shard_up, shard_down = finish(feed_quarters, hidden, [up_weight.shape, down_weight.shape])
    grad_text = grad_text.reshape(rows_dev, CAPTION, SEGS, width).swapaxes(1, 2)
    grad_text = after(grad_text.reshape(text.shape), *self_sums[1])
    with jax.named_scope("self_sums_fourth_stage"):
        self_sums = fourth_stage(self_sums, gathered, shard_up, grad_text)
    cross_done = summed(landed(cross_sums, *self_sums[1])).astype(bf16)
    with jax.named_scope("gather_mod"):
        gathered = joined_rows(gathered, "x", cross_done)
    grad_frames = grad_resid_one + norm_back(
        normed_one, inverse_one, after(grad_first, gathered) * (1.0 + scale_one)
    )
    self_done = summed(landed(self_sums, grad_frames)).astype(bf16)
    with jax.named_scope("gather_mod"):
        gathered = joined_rows(gathered, "y", self_done, cross_done)
    with jax.named_scope("gather_mod"):
        gathered = joined_rows(gathered, "core", self_done)
    grad_mod_all = gathered[:, : 6 * width]
    digits = gathered[:, 6 * width : 6 * width + 2].astype(f32)
    steps_all = digits[:, 0] * 256.0 + digits[:, 1]
    choose_all = (
        steps_all[:, None] == jnp.arange(step_table.shape[0]).astype(f32)[None, :]
    ).astype(bf16)
    cond_all = matmul(choose_all, table_low)
    silu_all = jax.nn.silu(cond_all).astype(bf16)
    grad_ada_w = inner_rows(silu_all, grad_mod_all)
    grad_ada_b = jnp.sum(grad_mod_all.astype(f32), axis=0)
    grad_cond = silu_back(cond_all, outer_cols(grad_mod_all, ada_weight))
    grad_table = lax.dot_general(
        choose_all.astype(f32), grad_cond, (((0,), (0,)), ((), ())), precision=highest
    )

    made = (grad_ada_w, grad_table)
    with jax.named_scope("cross_spread"):
        cross_quarters = spread(cross_done, *made)
    with jax.named_scope("self_spread"):
        self_quarters = spread(self_done, *made)
    shard_cout, shard_cquery, shard_ckey, shard_cvalue = finish(
        cross_quarters, low, [out_w.shape] * 4
    )
    shard_out, shard_query, shard_key, shard_value = finish(
        self_quarters, low, [out_w.shape] * 4, shard_up, shard_cout
    )

    return (
        layer_out,
        grad_frames,
        grad_text,
        grad_table,
        grad_ada_w,
        grad_ada_b,
        shard_query.T,
        shard_key.T,
        shard_value.T,
        shard_out,
        shard_cquery.T,
        shard_ckey.T,
        shard_cvalue.T,
        shard_cout,
        shard_up,
        shard_down,
    )


def solution(mesh):
    dp, mp = mesh.shape["dp"], mesh.shape["mp"]
    fine = Mesh(mesh.devices.reshape(dp // 2, 2, mp // 4, 2, 2), FINE)
    dp_axes, mp_axes = ("y", "core"), MP_AXES
    return jax.shard_map(
        shards,
        mesh=fine,
        in_specs=(
            P(FINE, None),
            P(dp_axes, None),
            P(FINE, None, None),
            P(dp_axes),
            P(dp_axes),
            P(None, mp_axes),
            P(mp_axes, None),
            P(),
            P(None, mp_axes),
            P(None, mp_axes),
            P(None, mp_axes),
            P(mp_axes, None),
            P(None, mp_axes),
            P(None, mp_axes),
            P(None, mp_axes),
            P(mp_axes, None),
            P(None, mp_axes),
            P(mp_axes, None),
            P(FINE, None),
        ),
        out_specs=(
            P(FINE, None),
            P(FINE, None),
            P(FINE, None, None),
            P(None, mp_axes),
            P(mp_axes, None),
            P(),
            P(None, mp_axes),
            P(None, mp_axes),
            P(None, mp_axes),
            P(mp_axes, None),
            P(None, mp_axes),
            P(None, mp_axes),
            P(None, mp_axes),
            P(mp_axes, None),
            P(None, mp_axes),
            P(mp_axes, None),
        ),
        check_vma=False,
    )
```

```python
from functools import partial
from typing import Any, NamedTuple

import jax
import jax.numpy as jnp
from jax import lax
from jax.experimental import pallas as pl
from jax.experimental.pallas import tpu as pltpu
from jax.sharding import Mesh, PartitionSpec as P

HEADS = 12
HD = 64
CAPTION = 77
SEGS = 4

QUAD = 4 * HD
highest = lax.Precision.HIGHEST
epsilon = 1e-06
masked_score = -1e30
bf16 = jnp.bfloat16
f32 = jnp.float32
FINE = ("y", "core", "za", "zb", "x")
MP_AXES = ("za", "zb", "x")
VMEM = 48 << 20


def shifted(value, axis, steps):
    count = lax.axis_size(axis)
    with jax.named_scope(f"to_{axis}_{steps}"):
        return lax.ppermute(value, axis, [(k, (k + steps) % count) for k in range(count)])


def gather_axis(value, axis, *hold):
    count = lax.axis_size(axis)
    me = lax.axis_index(axis)
    pieces = [shifted(value, axis, s) for s in range(1, count)]
    if hold:
        pieces = [after(piece, *hold) for piece in pieces]
    pieces = [value] + pieces

    def at(place):
        turn = (me - place) % count
        chosen = pieces[0]
        for s in range(1, count):
            chosen = jnp.where(turn == s, pieces[s], chosen)
        return chosen

    return jnp.stack([at(place) for place in range(count)])


def joined_rows(value, axis, *hold):
    return gather_axis(value, axis, *hold).reshape(-1, value.shape[-1])


def after(value, *done):
    return lax.optimization_barrier((value, *done))[0]


class Term(NamedTuple):
    value: Any
    picks: tuple = ()
    done: tuple = ()

    def piece(self):
        value = after(self.value, *self.done) if self.done else self.value
        for dim, which in self.picks:
            value = lax.dynamic_index_in_dim(value, which, dim, keepdims=False)
        return value


def picked(terms, dim, which):
    terms = [t if isinstance(t, Term) else Term(t) for t in terms]
    return [t._replace(picks=(*t.picks, (dim, which))) for t in terms]


def summed(terms):
    pieces = [t.piece() for t in terms]
    total = pieces[0].astype(f32)
    for piece in pieces[1:]:
        total = total + piece.astype(f32)
    return total


def launch(terms, axis, dim):
    count = lax.axis_size(axis)
    me = lax.axis_index(axis)
    sent = [
        summed(picked(terms, dim, (me + s) % count)).astype(bf16) for s in range(1, count)
    ]
    arrived = [shifted(part, axis, s) for s, part in enumerate(sent, 1)]
    return picked(terms, dim, me), sent, arrived


def launch_wide(value, axis, dim):
    count = lax.axis_size(axis)
    me = lax.axis_index(axis)
    sent = [picked([value], dim, (me + s) % count)[0].piece() for s in range(1, count)]
    arrived = [shifted(part, axis, s) for s, part in enumerate(sent, 1)]
    return picked([value], dim, me), sent, arrived


def landed(started, *done):
    kept, _, arrived = started
    kept = [t if isinstance(t, Term) else Term(t) for t in kept]
    if done:
        kept = [t._replace(done=done) for t in kept]
        arrived = [after(part, *done) for part in arrived]
    return kept + [Term(part) for part in arrived]


def split_rows(part):
    grid = [lax.axis_size(a) for a in (*MP_AXES, "y")]
    return part.reshape(part.shape[0], *grid, -1, part.shape[-1])


def first_stage(mine_a, mine_b, other_a, other_b, *done):
    other_a, other_b = shifted(other_a, "core", 1), shifted(other_b, "core", 1)
    if done:
        other_a, other_b = after(other_a, *done), after(other_b, *done)
    left = [split_rows(mine_a), split_rows(other_a)]
    right = [split_rows(mine_b), split_rows(other_b)]
    return launch(left, "x", 3), launch(right, "y", 4)


def second_stage(stage, *done):
    left = launch(landed(stage[0], *done), "y", 3)
    right = launch(landed(stage[1], *done), "x", 3)
    return left, right


def third_stage(stage, *done):
    left, right = (summed(landed(part, *done)).astype(bf16) for part in stage)
    return launch([jnp.stack([left, right])], "zb", 3)


def fourth_stage(stage, *done):
    return launch(landed(stage, *done), "za", 2)


def sends(stage):
    return stage[0][1] + stage[1][1]


def assemble(left, right):
    left = left.transpose(5, 4, 3, 2, 1, 0, 6, 7)
    right = right.transpose(5, 4, 3, 1, 2, 0, 6, 7)
    whole = jnp.concatenate([left, right], axis=-1)
    return whole.reshape(whole.shape[0], -1, whole.shape[-1])


def rows_kernel(mine_ref, *refs):
    *sources, first_ref, more_ref, sems = refs
    rows = first_ref.shape[1]
    own = pl.ds(pl.multiple_of(mine_ref[0] * rows, 8), rows)
    copies = []
    for which, source in enumerate(sources):
        target = first_ref.at[which] if which < 3 else more_ref.at[which - 3]
        copies.append(pltpu.make_async_copy(source.at[own, :], target, sems.at[which]))
    for copy in copies:
        copy.start()
    for copy in copies:
        copy.wait()


def feed_rows_kernel(mine_ref, up_ref, down_ref, feed_ref, wide_ref, tall_ref, sems):
    rows = feed_ref.shape[1]
    own = pl.ds(pl.multiple_of(mine_ref[0] * rows, 8), rows)
    down = pltpu.make_async_copy(down_ref.at[own, :], feed_ref.at[1], sems.at[0])
    up = pltpu.make_async_copy(up_ref, wide_ref, sems.at[1])
    down.start()
    up.start()
    up.wait()
    tall_ref[...] = wide_ref[...].astype(f32).T
    down.wait()
    feed_ref[0] = tall_ref[own, :].astype(bf16)


def own_rows(value, mine):
    part = value.shape[0] // (lax.axis_size("y") * lax.axis_size("core"))
    return lax.dynamic_slice_in_dim(value, mine * part, part, 0)


def weight_parts(weights):
    copies = lax.axis_size("y") * lax.axis_size("core")
    mine = lax.axis_index("y") * lax.axis_size("core") + lax.axis_index("core")
    width, rows = weights[0].shape[1], weights[0].shape[0] // copies
    if rows % 8:
        kept = [own_rows(w, mine) for w in weights]
        return jnp.stack(kept[:3]), jnp.stack(kept[3:])
    smem, hbm = pl.BlockSpec(memory_space=pltpu.SMEM), pl.BlockSpec(memory_space=pltpu.HBM)
    vmem = pl.BlockSpec(memory_space=pltpu.VMEM)
    return pl.pallas_call(
        rows_kernel,
        in_specs=[smem] + [hbm] * len(weights),
        out_specs=[vmem] * 2,
        out_shape=[
            jax.ShapeDtypeStruct((3, rows, width), bf16),
            jax.ShapeDtypeStruct((len(weights) - 3, rows, width), bf16),
        ],
        scratch_shapes=[pltpu.SemaphoreType.DMA((len(weights),))],
    )(mine.reshape(1), *weights)


def feed_parts(up_weight, down_weight, *done):
    copies = lax.axis_size("y") * lax.axis_size("core")
    mine = lax.axis_index("y") * lax.axis_size("core") + lax.axis_index("core")
    mine = after(mine, *done)
    hidden, width = down_weight.shape
    if hidden // copies % 8:
        return jnp.stack([own_rows(up_weight.T, mine), own_rows(down_weight, mine)])
    smem, hbm = pl.BlockSpec(memory_space=pltpu.SMEM), pl.BlockSpec(memory_space=pltpu.HBM)
    vmem = pl.BlockSpec(memory_space=pltpu.VMEM)
    return pl.pallas_call(
        feed_rows_kernel,
        in_specs=[smem, hbm, hbm],
        out_specs=vmem,
        out_shape=jax.ShapeDtypeStruct((2, hidden // copies, width), bf16),
        scratch_shapes=[
            pltpu.VMEM((width, hidden), bf16),
            pltpu.VMEM((hidden, width), f32),
            pltpu.SemaphoreType.DMA((2,)),
        ],
    )(mine.reshape(1), up_weight, down_weight)


def finish_kernel(me_ref, near, far_y, far_core, far_both, *refs):
    *outs, whole_ref = refs
    y, core = me_ref[0], me_ref[1]
    matrices, rows, lanes = near.shape
    by_rows = lanes == whole_ref.shape[1]

    def place(which, part, turn_y, turn_core):
        here_y, here_core = y ^ turn_y, core ^ turn_core
        row = (2 * here_y + here_core) * rows if by_rows else here_y * rows
        row = pl.ds(pl.multiple_of(row, 8), rows)
        if by_rows:
            whole_ref[row, :] = part[which].astype(f32)
        else:
            lane = pl.ds(pl.multiple_of(here_core * lanes, 128), lanes)
            whole_ref[row, lane] = part[which].astype(f32)

    for which, out in enumerate(outs):
        for part, turns in ((near, (0, 0)), (far_y, (1, 0)), (far_core, (0, 1)), (far_both, (1, 1))):
            place(which, part, *turns)
        out[...] = whole_ref[...] if out.shape == whole_ref.shape else whole_ref[...].T


def spread(done, *hold):
    done = done.reshape(-1, *done.shape[2:])
    far_y = shifted(done, "y", 1)
    if hold:
        far_y = after(far_y, *hold)
    return done, far_y, shifted(done, "core", 1), shifted(far_y, "core", 1)


def finish(quarters, rows, shapes, *hold):
    done, far_y, far_core, far_both = quarters
    by_rows = lax.axis_size("y") * lax.axis_size("core") * done.shape[1] == rows
    width = done.shape[2] if by_rows else 2 * done.shape[2]
    if lax.axis_size("y") != 2 or done.shape[1] % 8 or done.shape[2] % 128:
        done = gather_axis(gather_axis(done, "core"), "y")
        axes = (2, 0, 1, 3, 4) if by_rows else (2, 0, 3, 1, 4)
        done = done.transpose(axes).reshape(done.shape[2], rows, width)
        return [
            (d if s == (rows, width) else d.T).astype(f32) for d, s in zip(done, shapes)
        ]
    if hold:
        far_core, far_both = after(far_core, *hold), after(far_both, *hold)
    me = jnp.stack([lax.axis_index("y"), lax.axis_index("core")])

    def whole(shape):
        return pl.BlockSpec(shape, lambda i: (0,) * len(shape))

    return pl.pallas_call(
        finish_kernel,
        grid=(1,),
        in_specs=[pl.BlockSpec(memory_space=pltpu.SMEM)] + [whole(done.shape)] * 4,
        out_specs=[whole(shape) for shape in shapes],
        out_shape=[jax.ShapeDtypeStruct(shape, f32) for shape in shapes],
        scratch_shapes=[pltpu.VMEM((rows, width), f32)],
        compiler_params=pltpu.CompilerParams(vmem_limit_bytes=VMEM),
    )(me, done, far_y, far_core, far_both)


def normalize(values):
    centre = values - jnp.mean(values, axis=-1, keepdims=True)
    inverse = lax.rsqrt(jnp.mean(centre * centre, axis=-1, keepdims=True) + epsilon)
    return (centre * inverse, inverse)


def norm_back(normed, inverse, upstream):
    mean_grad = jnp.mean(upstream, axis=-1, keepdims=True)
    mean_both = jnp.mean(upstream * normed, axis=-1, keepdims=True)
    return inverse * (upstream - mean_grad - normed * mean_both)


def matmul(left, right):
    return jnp.dot(left, right, preferred_element_type=f32)


def inner_rows(left, right):
    return lax.dot_general(left, right, (((0,), (0,)), ((), ())), preferred_element_type=f32)


def outer_cols(left, right):
    return lax.dot_general(left, right, (((1,), (1,)), ((), ())), preferred_element_type=f32)


def gelu_back(pre_act, upstream):
    return jax.vjp(partial(jax.nn.gelu, approximate=True), pre_act)[1](upstream)[0]


def silu_back(inputs, upstream):
    return jax.vjp(jax.nn.silu, inputs)[1](upstream)[0]


def own_lanes(head):
    lane = lax.broadcasted_iota(jnp.int32, (1, QUAD), 1)
    return (lane >= head * HD) & (lane < (head + 1) * HD)


def merged(parts):
    whole = parts[0]
    for head in range(1, len(parts)):
        whole = jnp.where(own_lanes(head), parts[head], whole)
    return whole


def forward_kernel(q_ref, k_ref, v_ref, bias_ref, mix_ref):
    query = q_ref[...] * bf16(HD**-0.5)
    keys, values, bias = k_ref[...], v_ref[...], bias_ref[0]
    parts = []
    for head in range(QUAD // HD):
        own = jnp.where(own_lanes(head), query, bf16(0))
        scores = outer_cols(own, keys) + bias
        raised = jnp.exp(scores - jnp.max(scores, axis=1, keepdims=True))
        total = jnp.sum(raised, axis=1, keepdims=True)
        parts.append(matmul(raised.astype(bf16), values) / total)
    mix_ref[...] = merged(parts).astype(bf16)


def backward_kernel(
    core_ref,
    q_ref,
    k_ref,
    v_ref,
    mix_ref,
    bias_ref,
    out_w_ref,
    q_w_ref,
    k_w_ref,
    v_w_ref,
    back_ref,
    x_ref,
    *rest,
):
    cross = len(rest) > 5
    if cross:
        text_ref, text_grad_ref, in_ref, mine_a, mine_b, other_a, other_b = rest
    else:
        in_ref, mine_a, mine_b, other_a, other_b = rest
        text_ref = x_ref
    query = q_ref[...] * bf16(HD**-0.5)
    keys, values, bias = k_ref[...], v_ref[...], bias_ref[0]
    back = back_ref[...]
    grad = outer_cols(back, out_w_ref[...]).astype(bf16)
    gq, gk, gv = [], [], []
    for head in range(QUAD // HD):
        own = own_lanes(head)
        scores = outer_cols(keys, jnp.where(own, query, bf16(0))) + bias
        raised = jnp.exp(scores - jnp.max(scores, axis=0, keepdims=True))
        weights = raised * (1.0 / jnp.sum(raised, axis=0, keepdims=True))
        grad_weights = outer_cols(jnp.where(own, values, bf16(0)), grad)
        mean = jnp.sum(weights * grad_weights, axis=0, keepdims=True)
        grad_scores = (weights * (grad_weights - mean)).astype(bf16)
        gv.append(matmul(weights.astype(bf16), grad))
        gk.append(matmul(grad_scores, query))
        gq.append(inner_rows(grad_scores, keys))
    gq = (merged(gq) * HD**-0.5).astype(bf16)
    gk, gv = merged(gk).astype(bf16), merged(gv).astype(bf16)

    @pl.when(pl.program_id(1) == 0)
    def _():
        in_ref[...] = jnp.zeros_like(in_ref)
        if cross:
            text_grad_ref[...] = jnp.zeros_like(text_grad_ref)

    if cross:
        in_ref[...] += matmul(gq, q_w_ref[...])
        text_grad_ref[...] += matmul(gk, k_w_ref[...]) + matmul(gv, v_w_ref[...])
    else:
        in_ref[...] += (
            matmul(gq, q_w_ref[...]) + matmul(gk, k_w_ref[...]) + matmul(gv, v_w_ref[...])
        )
    half = mine_a.shape[-1]
    first = core_ref[0] == 0
    mine, other = (mine_a, mine_b), (other_a, other_b)
    pairs = [(mix_ref[...], back), (gq, x_ref[...]), (gk, text_ref[...]), (gv, text_ref[...])]
    for which, (left, right) in enumerate(pairs):
        whole = inner_rows(left, right).astype(bf16)
        low, high = whole[:, :half], whole[:, half:]
        mine[which // 2][which % 2] = jnp.where(first, low, high)
        other[which // 2][which % 2] = jnp.where(first, high, low)


def attend(query, keys, values, bias):
    rows, frames, tokens = bias.shape
    pairs = query.shape[1] // QUAD
    blocks = [pl.BlockSpec((n, QUAD), lambda r, h: (r, h)) for n in (frames, tokens, tokens)]
    return pl.pallas_call(
        forward_kernel,
        grid=(rows, pairs),
        in_specs=blocks + [pl.BlockSpec((1, frames, tokens), lambda r, h: (r, 0, 0))],
        out_specs=blocks[0],
        out_shape=jax.ShapeDtypeStruct(query.shape, bf16),
        compiler_params=pltpu.CompilerParams(vmem_limit_bytes=VMEM),
        cost_estimate=pl.CostEstimate(flops=0, transcendentals=0, bytes_accessed=0),
    )(query, keys, values, bias)


def attend_back(core, query, keys, values, mix, bias, weights, back, x, text=None):
    rows, tokens, frames = bias.shape
    width = query.shape[1]
    pairs, half = width // QUAD, width // 2
    wide = pl.BlockSpec((frames, QUAD), lambda r, h, c: (r, h))
    held = pl.BlockSpec((tokens, QUAD), lambda r, h, c: (r, h))
    matrix = pl.BlockSpec((QUAD, width), lambda r, h, c: (h, 0))
    frames_all = pl.BlockSpec((frames, width), lambda r, h, c: (r, 0))
    tokens_all = pl.BlockSpec((tokens, width), lambda r, h, c: (r, 0))
    grads = pl.BlockSpec((2, QUAD, half), lambda r, h, c: (0, h, 0))
    grads_shape = jax.ShapeDtypeStruct((2, width, half), bf16)
    cross = text is not None
    return pl.pallas_call(
        backward_kernel,
        grid_spec=pltpu.PrefetchScalarGridSpec(
            num_scalar_prefetch=1,
            grid=(rows, pairs),
            in_specs=[wide, held, held, wide]
            + [pl.BlockSpec((1, tokens, frames), lambda r, h, c: (r, 0, 0))]
            + [matrix] * 4
            + [frames_all] * 2
            + [tokens_all] * cross,
            out_specs=[tokens_all] * cross + [frames_all] + [grads] * 4,
        ),
        out_shape=[jax.ShapeDtypeStruct((rows * tokens, width), f32)] * cross
        + [jax.ShapeDtypeStruct(x.shape, f32)]
        + [grads_shape] * 4,
        compiler_params=pltpu.CompilerParams(vmem_limit_bytes=VMEM),
        cost_estimate=pl.CostEstimate(flops=0, transcendentals=0, bytes_accessed=0),
    )(core, query, keys, values, mix, bias, *weights, back, x, *([text] if cross else []))


def feed_kernel(paired, me_ref, x_ref, x_far, g_ref, g_far, *refs):
    inputs, outs = refs[: 4 if paired else 2], refs[4 if paired else 2 :]
    out_ref, back_ref, out_far, back_far, *grad_refs = outs[:-6]
    out_sum, back_sum, third_both, grad_both, active_both, pre_both = outs[-6:]
    tokens = x_ref.shape[0]
    slope = (2.0 / jnp.pi) ** 0.5
    step = pl.program_id(0)

    @pl.when(step == 0)
    def _():
        for ref in (out_ref, back_ref, out_sum, back_sum):
            ref[...] = jnp.zeros_like(ref)
        third_both[:tokens], third_both[tokens:] = x_ref[...], x_far[...]
        grad_both[:tokens], grad_both[tokens:] = g_ref[...], g_far[...]

    my_y, my_x = me_ref[0], me_ref[1]
    if paired:
        up_near, up_far, down_near, down_far = inputs
        (nx, zb, _, rows, _), ny = up_near.shape, 2
        up_at = lambda b, x, y: jnp.where(my_y == y, up_near[x, b, 0], up_far[x, b, 0])
        down_at = lambda b, x, y: jnp.where(my_x == x, down_near[y, b, 0], down_far[y, b, 0])
    else:
        up_ref, down_ref = inputs
        ny, nx, zb, _, rows, _ = up_ref.shape
        up_at = lambda b, x, y: up_ref[y, x, b, 0]
        down_at = lambda b, x, y: down_ref[y, x, b, 0]
    places = [(b, x, y) for b in range(zb) for x in range(nx) for y in range(ny)]
    up = jnp.concatenate([up_at(*p) for p in places], axis=0)
    down = jnp.concatenate([down_at(*p) for p in places], axis=0)
    for which, (out, back) in enumerate(((out_ref, back_ref), (out_sum, back_sum))):
        here = slice(which * tokens, (which + 1) * tokens)
        pre = outer_cols(third_both[here], up)
        square = pre * pre
        rise = 0.5 + 0.5 * jnp.tanh(pre * (slope + (0.044715 * slope) * square))
        active = pre * rise
        steep = rise + active * (1.0 - rise) * (2.0 * slope + (0.26829 * slope) * square)
        active = active.astype(bf16)
        grad_pre = (outer_cols(grad_both[here], down) * steep).astype(bf16)
        out[...] += matmul(active, down)
        back[...] += matmul(grad_pre, up)
        active_both[here] = active
        pre_both[here] = grad_pre
    up_total = inner_rows(pre_both[...], third_both[...]).astype(bf16)
    down_total = inner_rows(active_both[...], grad_both[...]).astype(bf16)
    at = {p: slice(n * rows, (n + 1) * rows) for n, p in enumerate(places)}
    if paired:
        up_kept, up_sent, down_kept, down_sent = grad_refs
        for b in range(zb):
            for k in range(2):
                zero, one = up_total[at[b, 0, k]], up_total[at[b, 1, k]]
                up_kept[k, 0, b] = jnp.where(my_x == 0, zero, one)
                up_sent[k, 0, b] = jnp.where(my_x == 0, one, zero)
                zero, one = down_total[at[b, k, 0]], down_total[at[b, k, 1]]
                down_kept[k, 0, b] = jnp.where(my_y == 0, zero, one)
                down_sent[k, 0, b] = jnp.where(my_y == 0, one, zero)
    else:
        for ref, total in zip(grad_refs, (up_total, down_total)):
            for b, x, y in places:
                ref[0, b, x, y] = total[at[b, x, y]]

    @pl.when(step == pl.num_programs(0) - 1)
    def _():
        out_far[...] = out_sum[...].astype(bf16)
        back_far[...] = back_sum[...].astype(bf16)


def feed(third_in, grad_mlp, up, down):
    tokens, width = third_in.shape
    nx, zb, za, rows, _ = up.shape
    ny = lax.axis_size("y")
    paired = nx == 2 and ny == 2
    if paired:
        weights = [up, shifted(up, "y", 1), down, shifted(down, "x", 1)]
    else:
        weights = [gather_axis(up, "y"), gather_axis(down, "x").swapaxes(0, 1)]
    whole = pl.BlockSpec((tokens, width), lambda j, c: (0, 0))
    half_shape, whole_shape = (2, za, zb, rows, width), (za, zb, nx, ny, rows, width)
    grads_shape = half_shape if paired else whole_shape
    matrix_shape = (2, zb, 1, rows, width) if paired else (ny, nx, zb, 1, rows, width)
    zeros = len(matrix_shape) - 3
    matrix = pl.BlockSpec(matrix_shape, lambda j, c: (0,) * zeros + (j, 0, 0))
    if paired:
        grads = pl.BlockSpec((2, 1, zb, rows, width), lambda j, c: (0, j, 0, 0, 0))
    else:
        grads = pl.BlockSpec((1, *whole_shape[1:]), lambda j, c: (j, 0, 0, 0, 0, 0))
    count = 4 if paired else 2
    me = jnp.stack([lax.axis_index("y"), lax.axis_index("x")])
    out, back, out_far, back_far, *parts = pl.pallas_call(
        partial(feed_kernel, paired),
        grid_spec=pltpu.PrefetchScalarGridSpec(
            num_scalar_prefetch=1,
            grid=(za,),
            in_specs=[whole] * 4 + [matrix] * count,
            out_specs=[whole] * 4 + [grads] * count,
            scratch_shapes=[pltpu.VMEM((tokens, width), f32)] * 2
            + [pltpu.VMEM((2 * tokens, width), bf16)] * 2
            + [pltpu.VMEM((2 * tokens, zb * nx * ny * rows), bf16)] * 2,
        ),
        out_shape=[jax.ShapeDtypeStruct((tokens, width), f32)] * 2
        + [jax.ShapeDtypeStruct((tokens, width), bf16)] * 2
        + [jax.ShapeDtypeStruct(grads_shape, bf16)] * count,
        compiler_params=pltpu.CompilerParams(vmem_limit_bytes=50 << 20),
        cost_estimate=pl.CostEstimate(flops=0, transcendentals=0, bytes_accessed=0),
    )(me, third_in, shifted(third_in, "core", 1), grad_mlp, shifted(grad_mlp, "core", 1), *weights)
    if paired:
        up_kept, up_sent, down_kept, down_sent = parts

        def as_grid(part):
            return part.transpose(1, 2, 0, 3, 4)[None]

        sums = (
            ([as_grid(up_kept)], [], [as_grid(shifted(up_sent, "x", 1))]),
            ([as_grid(down_kept)], [], [as_grid(shifted(down_sent, "y", 1))]),
        )
    else:
        sums = launch([parts[0][None]], "x", 3), launch([parts[1][None]], "y", 4)
    back = back + shifted(back_far, "core", 1).astype(f32)
    return out, shifted(out_far, "core", 1), back, sums


def clips_kernel(clip_ref, digits_ref, first, one, resid, mixed, third, three, up, mlp, mlp_far, out_ref):
    clips, width = out_ref.shape[0], first.shape[1]
    row = lax.broadcasted_iota(jnp.int32, (16, 1), 0)
    chooser = (clip_ref[...] == row).astype(f32).astype(bf16)
    parts = [
        first[...],
        first[...] * one[...],
        resid[...] * mixed[...],
        third[...],
        third[...] * three[...],
        up[...].astype(f32) * (mlp[...] + mlp_far[...].astype(f32)),
    ]
    for place, part in enumerate(parts):
        total = matmul(chooser, part.astype(bf16))[:clips]
        out_ref[:, place * width : (place + 1) * width] = total.astype(bf16)
    out_ref[:, len(parts) * width :] = digits_ref[...]


def clip_sums(clips, clip, digits, *values):
    width = values[0].shape[1]
    return pl.pallas_call(
        clips_kernel,
        out_shape=jax.ShapeDtypeStruct((clips, 6 * width + digits.shape[1]), bf16),
        compiler_params=pltpu.CompilerParams(vmem_limit_bytes=VMEM),
    )(clip[None, :], digits, *values)


def shards(
    frames,
    seg_ids,
    text,
    text_lens,
    step_ids,
    step_table,
    ada_weight,
    ada_bias,
    query_w,
    key_w,
    value_w,
    out_w,
    cross_query_w,
    cross_key_w,
    cross_value_w,
    cross_out_w,
    up_weight,
    down_weight,
    out_grad,
):
    width = frames.shape[1]
    za, zb, nx = (lax.axis_size(axis) for axis in MP_AXES)
    mp = za * zb * nx
    position = (lax.axis_index("za") * zb + lax.axis_index("zb")) * nx + lax.axis_index("x")
    rows_dev = seg_ids.shape[0] // mp
    frames_row = seg_ids.shape[1]
    segs_dev = rows_dev * SEGS
    my_ids = lax.dynamic_slice_in_dim(seg_ids, position * rows_dev, rows_dev, 0)
    my_lens = lax.dynamic_slice_in_dim(text_lens, position * segs_dev, segs_dev, 0)

    half = width // 2
    first, more = weight_parts(
        [
            query_w.T,
            key_w.T,
            value_w.T,
            out_w,
            cross_query_w.T,
            cross_key_w.T,
            cross_value_w.T,
            cross_out_w,
        ]
    )
    first_column = gather_axis(first, "za")
    feed_part = feed_parts(up_weight, down_weight, first_column)
    column = gather_axis(first_column, "zb")
    more = after(more, column)
    first_left = gather_axis(column[..., :half], "x")
    first_right = gather_axis(column[..., half:], "y")
    crossed = (first_left, first_right)
    more = gather_axis(more, "za", *crossed)
    feed_part = after(feed_part, more)
    my_steps = lax.dynamic_slice_in_dim(after(step_ids, column), position * segs_dev, segs_dev, 0)
    digits = jnp.stack([my_steps // 256, my_steps % 256], axis=1).astype(bf16)
    digits = jnp.pad(digits, ((0, 0), (0, 126)))

    same_seg = my_ids[:, :, None] == my_ids[:, None, :]
    self_bias = jnp.where(same_seg, 0.0, masked_score).astype(f32)
    key_segment = jnp.arange(SEGS * CAPTION) % SEGS
    valid_key = (
        jnp.arange(CAPTION)[None, :, None] < my_lens.reshape(rows_dev, SEGS)[:, None, :]
    ).reshape(rows_dev, SEGS * CAPTION)
    allowed = (my_ids[:, :, None] == key_segment[None, None, :]) & valid_key[:, None, :]
    cross_bias = jnp.where(allowed, 0.0, masked_score).astype(f32)
    allowed_t = (my_ids[:, None, :] == key_segment[None, :, None]) & valid_key[:, :, None]
    cross_bias_t = jnp.where(allowed_t, 0.0, masked_score).astype(f32)

    text = after(text, column)
    text_flat = text.reshape(rows_dev, SEGS, CAPTION, width).swapaxes(1, 2).reshape(-1, width)
    prepared = (digits, text_flat)
    first_left = gather_axis(first_left, "y", more)
    first_right = gather_axis(first_right, "x", more)
    more = gather_axis(more, "zb", first_left, first_right, *prepared)
    feed_part = gather_axis(feed_part, "za", first_left, first_right)
    more_left = gather_axis(more[..., :half], "x", first_left, first_right)
    more_right = gather_axis(more[..., half:], "y", first_left, first_right)
    qkv = assemble(gather_axis(first_left, "core"), gather_axis(first_right, "core"))
    qkv = qkv.reshape(-1, width)
    table_low = step_table
    step_ids = after(step_ids, first_column)
    choose_step = (step_ids[:, None] == jnp.arange(step_table.shape[0])[None, :]).astype(bf16)
    silu_mine = jax.nn.silu(matmul(choose_step, table_low)).astype(bf16)
    partial_mod = matmul(silu_mine, ada_weight)
    partial_mod = partial_mod.reshape(za, zb, nx, segs_dev, partial_mod.shape[1])
    modulation = summed(landed(launch_wide(partial_mod, "x", 2), column)).astype(bf16)
    modulation = summed(landed(launch([modulation], "zb", 1), *crossed)).astype(bf16)
    modulation = summed(landed(launch([modulation], "za", 0), first_left, first_right))
    modulation = modulation + ada_bias.astype(f32)
    flat_ids = my_ids.reshape(-1)
    row_of = jnp.arange(flat_ids.shape[0]) // frames_row
    clip = flat_ids + row_of * SEGS
    chosen = clip[:, None] == jnp.arange(segs_dev)[None, :]

    def per_frame(index):
        table = modulation[:, index * width : (index + 1) * width]
        value = jnp.broadcast_to(table[0:1], (clip.shape[0], width))
        for segment in range(1, segs_dev):
            value = jnp.where(chosen[:, segment : segment + 1], table[segment : segment + 1], value)
        return value

    shift_one, scale_one, gate_one, shift_two, scale_two, gate_two = map(per_frame, range(6))

    base = frames.astype(f32)
    normed_one, inverse_one = normalize(base)
    first_in = (normed_one * (1.0 + scale_one) + shift_one).astype(bf16)
    query, keys, values = (
        outer_cols(first_in, qkv[i * width : (i + 1) * width]).astype(bf16) for i in range(3)
    )
    self_mix = attend(query, keys, values, self_bias)
    more_left = gather_axis(more_left, "y", self_mix)
    more_right = gather_axis(more_right, "x", self_mix)
    feed_part = gather_axis(feed_part, "zb", self_mix)
    feed_up = gather_axis(feed_part[:, :, 0], "x", more_left, more_right)
    feed_down = gather_axis(feed_part[:, :, 1], "y", more_left, more_right)
    whole = assemble(gather_axis(more_left, "core"), gather_axis(more_right, "core"))
    out_full, cquery_t, cout_full = whole[0], whole[1], whole[4]
    ckv_t = whole[2:4].reshape(-1, width)
    self_out = matmul(self_mix, out_full)
    resid_one = base + gate_one * self_out
    normed_two, inverse_two = normalize(resid_one)
    second_in = normed_two.astype(bf16)
    cross_query = outer_cols(second_in, cquery_t).astype(bf16)
    cross_keys = outer_cols(text_flat, ckv_t[:width]).astype(bf16)
    cross_values = outer_cols(text_flat, ckv_t[width:]).astype(bf16)
    cross_mix = attend(cross_query, cross_keys, cross_values, cross_bias)
    resid_two = resid_one + matmul(cross_mix, cout_full)
    normed_three, inverse_three = normalize(resid_two)
    third_in = (normed_three * (1.0 + scale_two) + shift_two).astype(bf16)
    upstream = out_grad.astype(f32)
    grad_mlp = (gate_two * upstream).astype(bf16)
    core = lax.axis_index("core").reshape(1)
    mlp_near, mlp_far, grad_third, feed_sums = feed(third_in, grad_mlp, feed_up, feed_down)

    grad_resid_two = upstream + norm_back(
        normed_three, inverse_three, grad_third * (1.0 + scale_two)
    )
    grad_cross = after(grad_resid_two.astype(bf16), *sends(feed_sums))
    grad_text, grad_second, *cross_parts = attend_back(
        core,
        cross_query,
        cross_keys,
        cross_values,
        cross_mix,
        cross_bias_t,
        [cout_full, cquery_t, ckv_t[:width], ckv_t[width:]],
        grad_cross,
        second_in,
        text_flat,
    )
    with jax.named_scope("feed_sums_second_stage"):
        feed_sums = second_stage(feed_sums, grad_second)
    with jax.named_scope("cross_sums_first_stage"):
        cross_sums = first_stage(*cross_parts, *sends(feed_sums))
    grad_resid_one = grad_resid_two + norm_back(normed_two, inverse_two, grad_second)
    grad_self = after(
        (gate_one * grad_resid_one).astype(bf16), *sends(cross_sums), *sends(feed_sums)
    )
    grad_first, *self_parts = attend_back(
        core,
        query,
        keys,
        values,
        self_mix,
        self_bias,
        [out_full, qkv[:width], qkv[width : 2 * width], qkv[2 * width :]],
        grad_self,
        first_in,
    )
    with jax.named_scope("cross_sums_second_stage"):
        cross_sums = second_stage(cross_sums, grad_first)
    with jax.named_scope("feed_sums_third_stage"):
        feed_sums = third_stage(feed_sums, grad_first, *sends(cross_sums))
    with jax.named_scope("self_sums_first_stage"):
        self_sums = first_stage(*self_parts, *sends(cross_sums), *feed_sums[1])

    grad_first = after(grad_first, *sends(self_sums))
    grad_mod = clip_sums(
        segs_dev,
        clip,
        digits,
        grad_first,
        normed_one,
        grad_resid_one,
        self_out,
        grad_third,
        normed_three,
        out_grad,
        mlp_near,
        mlp_far,
    )
    with jax.named_scope("feed_sums_fourth_stage"):
        feed_sums = fourth_stage(feed_sums, grad_mod)
    with jax.named_scope("self_sums_second_stage"):
        self_sums = second_stage(self_sums, *feed_sums[1])
    with jax.named_scope("cross_sums_third_stage"):
        cross_sums = third_stage(cross_sums, *sends(self_sums))
    with jax.named_scope("gather_mod"):
        gathered = joined_rows(grad_mod, "za", *cross_sums[1])
    feed_done = summed(landed(feed_sums, gathered)).astype(bf16)
    with jax.named_scope("feed_spread"):
        feed_quarters = spread(feed_done)
    with jax.named_scope("self_sums_third_stage"):
        self_sums = third_stage(self_sums, feed_done)
    with jax.named_scope("cross_sums_fourth_stage"):
        cross_sums = fourth_stage(cross_sums, *self_sums[1])
    layer_out = resid_two + gate_two * (after(mlp_near, *cross_sums[1]) + mlp_far.astype(f32))
    layer_out = layer_out.astype(bf16)
    with jax.named_scope("gather_mod"):
        gathered = joined_rows(gathered, "zb", *cross_sums[1])
    hidden, low = down_weight.shape[0], out_w.shape[0]
    shard_up, shard_down = finish(feed_quarters, hidden, [up_weight.shape, down_weight.shape])
    grad_text = grad_text.reshape(rows_dev, CAPTION, SEGS, width).swapaxes(1, 2)
    grad_text = after(grad_text.reshape(text.shape), *self_sums[1])
    with jax.named_scope("self_sums_fourth_stage"):
        self_sums = fourth_stage(self_sums, gathered, shard_up, grad_text)
    cross_done = summed(landed(cross_sums, *self_sums[1])).astype(bf16)
    with jax.named_scope("gather_mod"):
        gathered = joined_rows(gathered, "x", cross_done)
    grad_frames = grad_resid_one + norm_back(
        normed_one, inverse_one, after(grad_first, gathered) * (1.0 + scale_one)
    )
    self_done = summed(landed(self_sums, grad_frames)).astype(bf16)
    with jax.named_scope("gather_mod"):
        gathered = joined_rows(gathered, "y", self_done, cross_done)
    with jax.named_scope("gather_mod"):
        gathered = joined_rows(gathered, "core", self_done)
    grad_mod_all = gathered[:, : 6 * width]
    digits = gathered[:, 6 * width : 6 * width + 2].astype(f32)
    steps_all = digits[:, 0] * 256.0 + digits[:, 1]
    choose_all = (
        steps_all[:, None] == jnp.arange(step_table.shape[0]).astype(f32)[None, :]
    ).astype(bf16)
    cond_all = matmul(choose_all, table_low)
    silu_all = jax.nn.silu(cond_all).astype(bf16)
    grad_ada_w = inner_rows(silu_all, grad_mod_all)
    grad_ada_b = jnp.sum(grad_mod_all.astype(f32), axis=0)
    grad_cond = silu_back(cond_all, outer_cols(grad_mod_all, ada_weight))
    grad_table = lax.dot_general(
        choose_all.astype(f32), grad_cond, (((0,), (0,)), ((), ())), precision=highest
    )

    made = (grad_ada_w, grad_table)
    with jax.named_scope("cross_spread"):
        cross_quarters = spread(cross_done, *made)
    with jax.named_scope("self_spread"):
        self_quarters = spread(self_done, *made)
    shard_cout, shard_cquery, shard_ckey, shard_cvalue = finish(
        cross_quarters, low, [out_w.shape] * 4
    )
    shard_out, shard_query, shard_key, shard_value = finish(
        self_quarters, low, [out_w.shape] * 4, shard_up, shard_cout
    )

    return (
        layer_out,
        grad_frames,
        grad_text,
        grad_table,
        grad_ada_w,
        grad_ada_b,
        shard_query.T,
        shard_key.T,
        shard_value.T,
        shard_out,
        shard_cquery.T,
        shard_ckey.T,
        shard_cvalue.T,
        shard_cout,
        shard_up,
        shard_down,
    )


def solution(mesh):
    dp, mp = mesh.shape["dp"], mesh.shape["mp"]
    fine = Mesh(mesh.devices.reshape(dp // 2, 2, mp // 4, 2, 2), FINE)
    dp_axes, mp_axes = ("y", "core"), MP_AXES
    return jax.shard_map(
        shards,
        mesh=fine,
        in_specs=(
            P(FINE, None),
            P(dp_axes, None),
            P(FINE, None, None),
            P(dp_axes),
            P(dp_axes),
            P(None, mp_axes),
            P(mp_axes, None),
            P(),
            P(None, mp_axes),
            P(None, mp_axes),
            P(None, mp_axes),
            P(mp_axes, None),
            P(None, mp_axes),
            P(None, mp_axes),
            P(None, mp_axes),
            P(mp_axes, None),
            P(None, mp_axes),
            P(mp_axes, None),
            P(FINE, None),
        ),
        out_specs=(
            P(FINE, None),
            P(FINE, None),
            P(FINE, None, None),
            P(None, mp_axes),
            P(mp_axes, None),
            P(),
            P(None, mp_axes),
            P(None, mp_axes),
            P(None, mp_axes),
            P(mp_axes, None),
            P(None, mp_axes),
            P(None, mp_axes),
            P(None, mp_axes),
            P(mp_axes, None),
            P(None, mp_axes),
            P(mp_axes, None),
        ),
        check_vma=False,
    )
```
